32 devices in a mesh: rep: 2 (over x), key: 16 (over z, y, core).
Axes of the slice: x: 2, y: 2, z: 4, core: 2. Of those that a mesh axis runs over, the one named last changes fastest.
Arguments:
- query_tokens: bfloat16 [48, 256, 768], P('rep', 'key'), parts along dimension 0, may hold values from -110 to 110
- key_tokens: bfloat16 [48, 1024, 768], P('rep', 'key'), parts along dimension 0, may hold values from -6 to 6
- pair: bfloat16 [512, 1024, 128], P('rep', 'key'), parts along dimension 0, may hold values from -6 to 6
- key_mask: int32 [2048], P(('rep', 'key')), parts along dimension 0, may hold values 0 or 1
- span_owner: int32 [32], P('rep'), parts along dimension 0, may hold values from 0 to 15, each once
- pair_gain: float32 [128], replicated, may hold values from 0.1 to 1.9
- pair_proj: bfloat16 [128, 16], replicated, may hold values from -1 to 1
- w_query: bfloat16 [768, 768], replicated, may hold values from -0.21875 to 0.21875
- w_key: bfloat16 [768, 768], replicated, may hold values from -0.21875 to 0.21875
- w_value: bfloat16 [768, 768], replicated, may hold values from -0.21875 to 0.21875
- w_gate: bfloat16 [768, 768], replicated, may hold values from -0.21875 to 0.21875
- w_out: bfloat16 [768, 768], replicated, may hold values from -0.21875 to 0.21875
Outputs:
- attended: bfloat16 [48, 256, 768], P('rep', 'key'), parts along dimension 0
The draws below stay inside these ranges and needn't reach their ends.
There are 2 independent parts, one for each index of `rep`. The reference program is written for one: setup_inputs(seed, part) draws one part's arguments, and reference() takes and returns one part's arrays. A program takes and returns all parts, laid end to end along the dimension named above; an argument that names none is the same for every part. Nothing has to cross between parts.
All inputs are finite; a program needn't handle non-finite values. No bound on the sum of `key_mask` on one device may be relied on, other than what follows from the above.
Results may differ from the reference program's by a relative error of at most 0.012.
The reference program's roundings to bfloat16 on the way count: a program that leaves them out, or rounds other values in their place, can miss the bound.
Values may be sent and summed in bfloat16 or wider, within the bound.
No kernel may reach another device: no remote copies, remote signals or barrier semaphores. Data moves between devices by JAX's collectives and lax.ppermute only.
A program may use at most 192 MiB of HBM per device.

```python
import jax
import jax.numpy as jnp
from jax import lax

D = 768
H = 16
C = 128
DH = 48
KEY_DEV = 64
Q = 256
SMP = 24
TOKENS = 1024
SPANS = 16


def draw_query_tokens(key, part):
    return jnp.clip(jax.random.normal(key, (SMP, Q, D), jnp.float32), -4.0, 4.0).astype(jnp.bfloat16)


def with_ends(values, rng, least, high):
    longest = values.shape.index(max(values.shape))
    spots = []
    for shift in (0, 1):
        where = [jax.random.randint(jax.random.fold_in(rng, axis), (), 0, length) for axis, length in enumerate(values.shape)]
        where[longest] = (where[longest] + shift) % values.shape[longest]
        spots.append(tuple(where))
    return values.at[spots[0]].set(least).at[spots[1]].set(high)


def steps_of(own_key, extent, pieces, low, top_value):
    gain, own = 1.0, jax.random.fold_in(own_key, 6)
    for position, shards_of in pieces:
        draws = jnp.exp(jax.random.uniform(jax.random.fold_in(own, position), (shards_of,), jnp.float32, low / len(pieces), top_value / len(pieces)))
        gain = gain * jnp.repeat(draws, extent[position] // shards_of).reshape([-1 if axis == position else 1 for axis in range(len(extent))])
    return gain


def gaussian(rng, shape, width, limit, split=(), kind=jnp.bfloat16):
    values = jax.random.normal(rng, shape, jnp.float32) * width
    if len(split) > 0:
        values = steps_of(rng, shape, split, -0.22, 0.18) * values
    return jnp.clip(values, min=-limit, max=limit).astype(kind)


def setup_inputs(seed: int = 0, part: int = 0) -> dict:
    key_list = jax.random.split(jax.random.key(seed), 13)
    part_splits = jax.random.split(jax.random.fold_in(key_list[12], part), 13)
    return {
        "query_tokens": draw_query_tokens(jax.random.fold_in(jax.random.fold_in(key_list[12], part), 71), part),
        "key_tokens": gaussian(part_splits[1], (SMP, TOKENS, D), 1.0, 6.0, ((1, 16),)),
        "pair": gaussian(part_splits[2], (Q, TOKENS, C), 1.0, 6.0, ((1, 16),)),
        "key_mask": with_ends((jax.random.randint(part_splits[3], (TOKENS,), 0, 8) < 7).astype(jnp.int32), jax.random.fold_in(part_splits[3], 1), 0, 1),
        "span_owner": jax.random.permutation(part_splits[4], SPANS).astype(jnp.int32),
        "pair_gain": jnp.clip(1.0 + 0.18 * jax.random.normal(key_list[5], (C,), jnp.float32), 0.1, 1.9),
        "pair_proj": gaussian(key_list[6], (C, H), 0.18, 1.0),
        "w_query": gaussian(key_list[7], (D, D), D ** -0.5, 0.21875),
        "w_key": gaussian(key_list[8], (D, D), D ** -0.5, 0.21875),
        "w_value": gaussian(key_list[9], (D, D), D ** -0.5, 0.21875),
        "w_gate": gaussian(key_list[10], (D, D), D ** -0.5, 0.21875),
        "w_out": gaussian(key_list[11], (D, D), D ** -0.5, 0.21875),
    }


def layer_normed(pair, pair_gain):
    values = pair.astype(jnp.float32)
    center = values - lax.optimization_barrier(jnp.mean(values, axis=-1, keepdims=True))
    spread = lax.optimization_barrier(jnp.mean(center * center, axis=-1, keepdims=True))
    return (center * lax.rsqrt(spread + 1e-05) * pair_gain).astype(jnp.bfloat16)

def reference(query_tokens, key_tokens, pair, key_mask, span_owner, pair_gain, pair_proj, w_query, w_key, w_value, w_gate, w_out):
    normed = layer_normed(pair, pair_gain)
    stored = jnp.einsum('qkc,ch->hqk', normed.astype(jnp.float32), pair_proj.astype(jnp.float32)).astype(jnp.bfloat16)
    inverse = jnp.argsort(span_owner).astype(jnp.int32)
    blocks = stored.reshape(H, Q, SPANS, KEY_DEV)
    pair_bias = jnp.take(blocks, inverse, axis=2).reshape(H, Q, TOKENS)
    queries = jnp.dot(query_tokens, w_query, preferred_element_type=jnp.float32).astype(jnp.bfloat16)
    keys = jnp.dot(key_tokens, w_key, preferred_element_type=jnp.float32).astype(jnp.bfloat16)
    values = jnp.dot(key_tokens, w_value, preferred_element_type=jnp.float32).astype(jnp.bfloat16)
    present = (key_mask > 0)[None, None, :]
    scale = 1.0 / DH ** 0.5

    def one_head(index):
        start = index * DH
        q_head = lax.dynamic_slice_in_dim(queries, start, DH, 2).astype(jnp.float32)
        k_head = lax.dynamic_slice_in_dim(keys, start, DH, 2).astype(jnp.float32)
        v_head = lax.dynamic_slice_in_dim(values, start, DH, 2).astype(jnp.float32)
        bias_head = lax.dynamic_index_in_dim(pair_bias, index, 0, keepdims=False).astype(jnp.float32)
        scores = jnp.einsum('sqd,snd->sqn', q_head, k_head) * scale + bias_head[None]
        scores = jnp.where(present, scores, -1000000000.0)
        probs = jax.nn.softmax(scores, axis=-1).astype(jnp.bfloat16)
        return jnp.einsum('sqn,snd->sqd', probs.astype(jnp.float32), v_head).astype(jnp.bfloat16)
    per_head = lax.map(one_head, jnp.arange(H, dtype=jnp.int32))
    heads_out = jnp.transpose(per_head, (1, 2, 0, 3)).reshape(SMP, Q, D)
    gate = jax.nn.sigmoid(jnp.dot(query_tokens, w_gate, preferred_element_type=jnp.float32))
    gated = (gate * heads_out.astype(jnp.float32)).astype(jnp.bfloat16)
    return jnp.dot(gated, w_out, preferred_element_type=jnp.float32).astype(jnp.bfloat16)
```

```python
import functools
import math

import jax
import jax.numpy as jnp
from jax import lax
from jax.experimental import pallas as pl
from jax.experimental.pallas import tpu as pltpu
from jax.sharding import PartitionSpec as P

H = 16
CHUNKS = 3
LOG2E = 1.4426950408889634
NEG = -1e9
VMEM_LIMIT = 60 * 1024 * 1024
F32 = jnp.float32
BF16 = jnp.bfloat16


def nt_dot(a, b):
    return lax.dot_general(a, b, (((1,), (1,)), ((), ())), preferred_element_type=F32)


def nn_dot(a, b):
    return jnp.dot(a, b, preferred_element_type=F32)


def bias_kernel(hpg, mask_ref, pair_ref, gain_ref, proj_ref, out_ref):
    fold, rows, keys, c = pair_ref.shape
    heads = proj_ref.shape[0]
    groups = heads // hpg
    step = pl.program_id(0)
    total_rows = (out_ref.shape[1] - 16) // hpg
    x = jnp.swapaxes(pair_ref[...], 0, 1).reshape(rows * fold * keys, c).astype(F32)
    center = x - jnp.mean(x, axis=-1, keepdims=True)
    spread = jnp.mean(center * center, axis=-1, keepdims=True)
    normed = (center * lax.rsqrt(spread + 1e-5) * gain_ref[...]).astype(BF16)
    bias = nt_dot(proj_ref[...], normed)
    bias = bias.reshape(heads, rows, fold * keys).astype(BF16)
    for h in range(heads):
        start = pl.multiple_of((h % hpg) * total_rows + step * rows, 16)
        out_ref[h // hpg, pl.ds(start, rows), :] = bias[h]

    @pl.when(step == 0)
    def _():
        row = jnp.broadcast_to(mask_ref[...], (16, fold * keys)).astype(BF16)
        for g in range(groups):
            out_ref[g, hpg * total_rows :, :] = row


def local_bias(pair, key_mask, pair_gain, pair_proj, hpg):
    window, keys, c = pair.shape
    heads = pair_proj.shape[1]
    fold = 128 // keys
    rows = window // fold
    tile = 16
    mask = jnp.tile(key_mask.astype(F32), fold)[None]
    out_rows = hpg * rows + 16
    return pl.pallas_call(
        functools.partial(bias_kernel, hpg),
        grid=(rows // tile,),
        in_specs=[
            pl.BlockSpec((1, 128), lambda i: (0, 0)),
            pl.BlockSpec((fold, tile, keys, c), lambda i: (0, i, 0, 0)),
            pl.BlockSpec((1, c), lambda i: (0, 0)),
            pl.BlockSpec((heads, c), lambda i: (0, 0)),
        ],
        out_specs=pl.BlockSpec((heads // hpg, out_rows, 128), lambda i: (0, 0, 0)),
        out_shape=jax.ShapeDtypeStruct((heads // hpg, out_rows, 128), BF16),
        cost_estimate=pl.CostEstimate(
            flops=2 * window * keys * c * 256, bytes_accessed=window * keys * c * 2, transcendentals=0
        ),
        compiler_params=pltpu.CompilerParams(vmem_limit_bytes=VMEM_LIMIT),
        name="bias_local",
    )(mask, pair.reshape(fold, rows, keys, c), pair_gain[None], pair_proj.T)


def order_kernel(hpg, keys, codes, me_ref, owner_ref, qsel_ref, x_ref, bias_ref, mask_ref, inv_ref):
    n = len(codes)
    fold = 128 // keys
    me = me_ref[0]
    rows = (x_ref.shape[1] - 16) // hpg
    slots = bias_ref.shape[1] // 16
    for d in range(n):
        inv_ref[owner_ref[d]] = d
    lane = lax.broadcasted_iota(jnp.int32, (16, 128), 1) // keys

    def of_tile(t):
        stored = [inv_ref[me ^ codes[t * fold + f]] ^ me for f in range(fold)]
        masks = x_ref[codes[t * fold], hpg * rows : hpg * rows + 16, :].astype(F32)
        for f in range(1, fold):
            part = x_ref[codes[t * fold + f], hpg * rows : hpg * rows + 16, :].astype(F32)
            masks = jnp.where(lane == f, part, masks)
        mask_ref[:, t * 128 : (t + 1) * 128] = masks[:8]
        return stored, masks > 0

    tiles = [of_tile(t) for t in range(n // fold)]

    def query_slot(p, carry):
        a = qsel_ref[p]
        part = a // (rows // 16)
        row = a % (rows // 16) * 16
        out = pl.multiple_of(p * 16, 16)
        for h in range(hpg):
            start = pl.multiple_of(h * rows + row, 16)
            for t, (stored, present) in enumerate(tiles):
                value = None
                for f in range(fold):
                    block = x_ref[stored[f], pl.ds(start, 16), :].astype(F32)
                    if fold == 2:
                        block = jnp.where(part == f, block, pltpu.roll(block, keys, 1))
                    value = block if value is None else jnp.where(lane == f, block, value)
                value = jnp.where(present, value * LOG2E, NEG * LOG2E)
                bias_ref[h, pl.ds(out, 16), t * 128 : (t + 1) * 128] = value
        return carry

    lax.fori_loop(0, slots, query_slot, 0)


def ordered_bias(x, me, span_owner, qsel, hpg, keys, codes, window):
    n = len(codes)
    smem = pl.BlockSpec(memory_space=pltpu.SMEM)
    vmem = pl.BlockSpec(memory_space=pltpu.VMEM)
    return pl.pallas_call(
        functools.partial(order_kernel, hpg, keys, codes),
        in_specs=[smem, smem, smem, vmem],
        out_specs=[vmem, vmem],
        out_shape=[
            jax.ShapeDtypeStruct((hpg, window, n * keys), F32),
            jax.ShapeDtypeStruct((8, n * keys), F32),
        ],
        scratch_shapes=[pltpu.SMEM((n,), jnp.int32)],
        cost_estimate=pl.CostEstimate(
            flops=hpg * window * n * keys * 8, bytes_accessed=hpg * window * n * keys * 6, transcendentals=0
        ),
        compiler_params=pltpu.CompilerParams(vmem_limit_bytes=VMEM_LIMIT),
        name="bias_order",
    )(me.reshape(1), span_owner, qsel, x)


def attention_kernel(pieces, hpg, direct, *refs):
    key_refs, refs = refs[:pieces], refs[pieces:]
    count = pieces if direct else 1
    query_refs, refs = refs[:count], refs[count:]
    bias_ref, mask_ref, wq_ref, wk_ref, wv_ref = refs[:5]
    out_refs = refs[5 : 5 + count]
    q_ref, k_ref, v_ref = refs[5 + count :]
    feats = wq_ref.shape[1]
    head_size = feats // hpg
    scale = LOG2E / math.sqrt(head_size)
    for m in range(pieces):
        block = key_refs[m][...]
        block = block.reshape(block.shape[0] * block.shape[1], block.shape[2])
        span = slice(m * block.shape[0], (m + 1) * block.shape[0])
        k_t = nt_dot(wk_ref[...], block)
        k_ref[:, span] = jnp.where(mask_ref[:1, span] > 0, k_t, 0.0).astype(BF16)
        v_ref[span, :] = nn_dot(block, wv_ref[...]).astype(BF16)
    for m in range(count):
        block = query_refs[m][...]
        block = block.reshape(block.shape[0] * block.shape[1], block.shape[2])
        span = slice(m * block.shape[0], (m + 1) * block.shape[0])
        q_ref[span, :] = nn_dot(block, wq_ref[...]).astype(BF16)
    q = q_ref[...]
    owner = lax.broadcasted_iota(jnp.int32, q.shape, 1) // head_size
    total = None
    for h in range(hpg):
        mine = owner == h
        scores = nn_dot(jnp.where(mine, q, jnp.zeros_like(q)), k_ref[...])
        scores = scores * scale + bias_ref[h]
        weights = jnp.exp2(scores - jnp.max(scores, axis=-1, keepdims=True))
        norm = 1.0 / jnp.sum(weights, axis=-1, keepdims=True)
        result = nn_dot((weights * norm).astype(BF16), v_ref[...])
        total = result if total is None else jnp.where(mine, result, total)
    rows = total.shape[0] // count
    for m in range(count):
        out_refs[m][0] = total[m * rows : (m + 1) * rows].astype(BF16)


def attention(arrays, queries, bias, mask, wq, wk_t, wv, hpg, keys, chunk_samples, query_rows):
    pieces = len(arrays)
    sg = arrays[0].shape[0]
    width = arrays[0].shape[2]
    window = bias.shape[1]
    tokens = bias.shape[2]
    feats = wq.shape[1]
    direct = queries is None
    whole = lambda shape: pl.BlockSpec(shape, lambda s: (0,) * len(shape))
    key_specs = [pl.BlockSpec((sg, keys, width), lambda s: (0, s, 0))] * pieces
    if direct:
        first = chunk_samples * keys // query_rows
        query_specs = [pl.BlockSpec((sg, query_rows, width), lambda s: (0, first + s, 0))] * pieces
        query_args = arrays
        out_rows = [sg * query_rows] * pieces
    else:
        query_specs = [pl.BlockSpec((1, window, width), lambda s: (s, 0, 0))]
        query_args = [queries]
        out_rows = [window]
    flops = 2 * chunk_samples * (tokens * width * feats * 2 + hpg * window * tokens * 512)
    return pl.pallas_call(
        functools.partial(attention_kernel, pieces, hpg, direct),
        grid=(chunk_samples,),
        in_specs=key_specs
        + query_specs
        + [whole(bias.shape), whole(mask.shape), whole(wq.shape), whole(wk_t.shape), whole(wv.shape)],
        out_specs=[pl.BlockSpec((1, r, feats), lambda s: (s, 0, 0)) for r in out_rows],
        out_shape=[jax.ShapeDtypeStruct((chunk_samples, r, feats), BF16) for r in out_rows],
        scratch_shapes=[
            pltpu.VMEM((window, feats), BF16),
            pltpu.VMEM((feats, tokens), BF16),
            pltpu.VMEM((tokens, feats), BF16),
        ],
        cost_estimate=pl.CostEstimate(
            flops=flops,
            bytes_accessed=chunk_samples * tokens * width * 2 + hpg * window * tokens * 4,
            transcendentals=chunk_samples * hpg * window * tokens,
        ),
        compiler_params=pltpu.CompilerParams(vmem_limit_bytes=VMEM_LIMIT),
        name="attend",
    )(*arrays, *query_args, bias, mask, wq, wk_t, wv)


def head_groups(n, samples):
    hg = 1
    while hg * hg < n or H % hg or samples % (n // hg):
        hg *= 2
    return hg


def local(
    query_tokens,
    key_tokens,
    pair,
    key_mask,
    span_owner,
    pair_gain,
    pair_proj,
    w_query,
    w_key,
    w_value,
    w_gate,
    w_out,
):
    n = lax.axis_size("key")
    samples, query_rows, width = query_tokens.shape
    keys = key_tokens.shape[1]
    window = pair.shape[0]
    hg = head_groups(n, samples)
    sg = n // hg
    hpg = H // hg
    feats = width // hg
    group_samples = samples // sg
    chunks = CHUNKS if group_samples % CHUNKS == 0 else 1
    cs = group_samples // chunks
    direct = query_rows % 16 == 0
    me = lax.axis_index("key")
    group, lane = me // hg, me % hg

    def across(x, code):
        if code == 0:
            return x
        return lax.ppermute(x, "key", [(i, i ^ code) for i in range(n)])

    labels = [0]
    bit = hg // 2
    while bit:
        labels = labels + [m ^ bit for m in labels]
        bit //= 2
    codes = [k * hg + m for m in labels for k in range(sg)]

    def own(w):
        return lax.dynamic_slice_in_dim(w, lane * feats, feats, 1)

    wq, wk_t, wv = own(w_query), own(w_key).T, own(w_value)
    relative = jnp.array(labels, jnp.int32) ^ lane
    gate_w = jnp.take(w_gate.reshape(width, hg, feats), relative, axis=1).reshape(width, width)
    out_w = jnp.take(w_out.reshape(hg, feats, width), relative, axis=0).reshape(width, width)

    key_groups = key_tokens.reshape(sg, chunks, cs * keys, width)
    query_groups = query_tokens.reshape(sg, chunks, cs * query_rows, width)

    def piece(c, k):
        at = (group ^ k, c, 0, 0)
        ks = lax.dynamic_slice(key_groups, at, (1, 1, cs * keys, width))
        qs = lax.dynamic_slice(query_groups, at, (1, 1, cs * query_rows, width))
        return jnp.concatenate([ks[0, 0], qs[0, 0]], axis=0)

    bias_groups = local_bias(pair, key_mask, pair_gain, pair_proj, hpg)

    def bias_piece(m):
        return lax.dynamic_index_in_dim(bias_groups, lane ^ m, 0, keepdims=False)

    spread = jnp.stack([across(bias_piece(m), m) for m in range(hg)])
    parts = {0: spread}
    bit = sg // 2
    while bit:
        parts.update({k ^ bit: across(x, bit * hg) for k, x in parts.items()})
        bit //= 2
    x = jnp.concatenate([parts[k] for k in range(sg)], axis=0)
    slots = window // 16
    if direct:
        qsel = jnp.array(codes, jnp.int32) ^ me
        qsel = (qsel[:, None] * (query_rows // 16) + jnp.arange(query_rows // 16)).reshape(slots)
    else:
        qsel = jnp.arange(slots, dtype=jnp.int32)
    bias, mask = ordered_bias(x, me, span_owner, qsel, hpg, keys, codes, window)
    slot_of = [0] * n
    for p, code in enumerate(codes):
        slot_of[code] = p

    outs = []
    previous = None
    for c in range(chunks):
        sent = [piece(c, k) for k in range(sg)]
        if previous is not None:
            sent, previous = lax.optimization_barrier((sent, previous))
        got = [across(x, k * hg) for k, x in enumerate(sent)]
        previous = got
        arrays = [jnp.stack(got)]
        bit = hg // 2
        while bit:
            arrays = arrays + [across(x, bit) for x in arrays]
            bit //= 2
        queries = None
        if not direct:
            parts = [x[:, cs * keys :].reshape(sg, cs, query_rows, width) for x in arrays]
            order = jnp.array(slot_of, jnp.int32)[me ^ jnp.arange(n)]
            queries = jnp.take(jnp.concatenate(parts, axis=0), order, axis=0)
            queries = jnp.swapaxes(queries, 0, 1).reshape(cs, window, width)
        results = attention(arrays, queries, bias, mask, wq, wk_t, wv, hpg, keys, cs, query_rows)
        if not direct:
            blocks = results[0].reshape(cs, n, query_rows, feats)
            blocks = jnp.take(blocks, jnp.array(codes, jnp.int32) ^ me, axis=1)
            results = [
                blocks[:, i * sg : (i + 1) * sg].reshape(cs, sg * query_rows, feats) for i in range(hg)
            ]
        heads = [across(r, m) for r, m in zip(results, labels)]
        joined = jnp.concatenate(heads, axis=-1).reshape(cs, sg, query_rows, width)
        back = [across(joined[:, k], k * hg) for k in range(sg)]
        heads_out = jnp.stack(back).reshape(sg * cs * query_rows, width)
        tokens = jnp.concatenate([x[cs * keys :] for x in sent], axis=0)
        gate = jax.nn.sigmoid(nn_dot(tokens, gate_w))
        gated = (gate * heads_out.astype(F32)).astype(BF16)
        outs.append(nn_dot(gated, out_w).astype(BF16).reshape(sg, 1, cs, query_rows, width))
    out = jnp.concatenate(outs, axis=1)
    out = jnp.take(out, group ^ jnp.arange(sg), axis=0)
    return out.reshape(samples, query_rows, width)


def solution(mesh):
    return jax.shard_map(
        local,
        mesh=mesh,
        in_specs=(
            P("rep", "key", None),
            P("rep", "key", None),
            P("rep", "key", None),
            P(("rep", "key")),
            P("rep"),
            P(),
            P(),
            P(),
            P(),
            P(),
            P(),
            P(),
        ),
        out_specs=P("rep", "key", None),
        check_vma=False,
    )
```

```python
import functools
import math

import jax
import jax.numpy as jnp
from jax import lax
from jax.experimental import pallas as pl
from jax.experimental.pallas import tpu as pltpu
from jax.sharding import PartitionSpec as P

H = 16
LOG2E = 1.4426950408889634
NEG = -1e9
VMEM_LIMIT = 60 * 1024 * 1024
F32 = jnp.float32
BF16 = jnp.bfloat16


def nt_dot(a, b):
    return lax.dot_general(a, b, (((1,), (1,)), ((), ())), preferred_element_type=F32)


def nn_dot(a, b):
    return jnp.dot(a, b, preferred_element_type=F32)


def bias_kernel(hpg, mask_ref, pair_ref, gain_ref, proj_ref, *out_refs):
    fold, rows, keys, c = pair_ref.shape
    heads = proj_ref.shape[0]
    step = pl.program_id(0)
    total_rows = (out_refs[0].shape[0] - 16) // hpg
    x = jnp.swapaxes(pair_ref[...], 0, 1).reshape(rows * fold * keys, c).astype(F32)
    center = x - jnp.mean(x, axis=-1, keepdims=True)
    spread = jnp.mean(center * center, axis=-1, keepdims=True)
    normed = (center * lax.rsqrt(spread + 1e-5) * gain_ref[...]).astype(BF16)
    bias = nt_dot(proj_ref[...], normed)
    bias = bias.reshape(heads, rows, fold * keys).astype(BF16)
    for h in range(heads):
        start = pl.multiple_of((h % hpg) * total_rows + step * rows, 16)
        out_refs[h // hpg][pl.ds(start, rows), :] = bias[h]

    @pl.when(step == 0)
    def _():
        row = jnp.broadcast_to(mask_ref[...], (16, fold * keys)).astype(BF16)
        for out_ref in out_refs:
            out_ref[hpg * total_rows :, :] = row


def local_bias(pair, key_mask, pair_gain, proj_t, hpg):
    window, keys, c = pair.shape
    heads = proj_t.shape[0]
    fold = 128 // keys
    rows = window // fold
    tile = 16
    mask = jnp.tile(key_mask.astype(F32), fold)[None]
    shape = (hpg * rows + 16, 128)
    return pl.pallas_call(
        functools.partial(bias_kernel, hpg),
        grid=(rows // tile,),
        in_specs=[
            pl.BlockSpec((1, 128), lambda i: (0, 0)),
            pl.BlockSpec((fold, tile, keys, c), lambda i: (0, i, 0, 0)),
            pl.BlockSpec((1, c), lambda i: (0, 0)),
            pl.BlockSpec((heads, c), lambda i: (0, 0)),
        ],
        out_specs=[pl.BlockSpec(shape, lambda i: (0, 0))] * (heads // hpg),
        out_shape=[jax.ShapeDtypeStruct(shape, BF16)] * (heads // hpg),
        cost_estimate=pl.CostEstimate(
            flops=2 * window * keys * c * 256, bytes_accessed=window * keys * c * 2, transcendentals=0
        ),
        compiler_params=pltpu.CompilerParams(vmem_limit_bytes=VMEM_LIMIT),
        name="bias_local",
    )(mask, pair.reshape(fold, rows, keys, c), pair_gain[None], proj_t)


def pack_kernel(group_ref, *refs):
    count = len(refs) // 3
    for k in range(count):
        keys = refs[k].shape[2]
        refs[2 * count + k][0, :keys] = refs[k][0, 0]
        refs[2 * count + k][0, keys:] = refs[count + k][0, 0]


def pack(group, key_groups, query_groups, first, size):
    sg, _, keys, width = key_groups.shape
    rows = query_groups.shape[2]

    def spec(length, k):
        return pl.BlockSpec((1, 1, length, width), lambda s, g: (g[0] ^ k, first + s, 0, 0))

    out = jax.ShapeDtypeStruct((size, keys + rows, width), BF16)
    return pl.pallas_call(
        pack_kernel,
        grid_spec=pltpu.PrefetchScalarGridSpec(
            num_scalar_prefetch=1,
            grid=(size,),
            in_specs=[spec(keys, k) for k in range(sg)] + [spec(rows, k) for k in range(sg)],
            out_specs=[pl.BlockSpec((1, keys + rows, width), lambda s, g: (s, 0, 0))] * sg,
        ),
        out_shape=[out] * sg,
        cost_estimate=pl.CostEstimate(
            flops=0, bytes_accessed=4 * sg * size * (keys + rows) * width, transcendentals=0
        ),
        compiler_params=pltpu.CompilerParams(vmem_limit_bytes=VMEM_LIMIT),
        name="pack",
    )(group.reshape(1), *([key_groups] * sg), *([query_groups] * sg))


def stack_kernel(*refs):
    for i, ref in enumerate(refs[:-1]):
        refs[-1][i] = ref[...]


def stacked(parts):
    count, shape = len(parts), parts[0].shape
    rest = (0,) * (len(shape) - 1)
    block = (1,) + shape[1:] if len(shape) == 3 else shape
    steps = shape[0] if len(shape) == 3 else 1
    return pl.pallas_call(
        stack_kernel,
        grid=(steps,),
        in_specs=[pl.BlockSpec(block, lambda s: (s,) + rest)] * count,
        out_specs=pl.BlockSpec((count,) + block, lambda s: (0, s) + rest),
        out_shape=jax.ShapeDtypeStruct((count,) + shape, BF16),
        cost_estimate=pl.CostEstimate(
            flops=0, bytes_accessed=4 * count * math.prod(shape), transcendentals=0
        ),
        compiler_params=pltpu.CompilerParams(vmem_limit_bytes=VMEM_LIMIT),
        name="stack",
    )(*parts)


def order_kernel(hpg, keys, codes, me_ref, owner_ref, qsel_ref, *refs):
    parts, (bias_ref, mask_ref, inv_ref, x_ref) = refs[:-4], refs[-4:]
    n = len(codes)
    each = n // len(parts)
    for k, part_ref in enumerate(parts):
        x_ref[k * each : (k + 1) * each] = part_ref[...]
    fold = 128 // keys
    me = me_ref[0]
    rows = (x_ref.shape[1] - 16) // hpg
    slots = bias_ref.shape[1] // 16
    for d in range(n):
        inv_ref[owner_ref[d]] = d
    lane = lax.broadcasted_iota(jnp.int32, (16, 128), 1) // keys

    def of_tile(t):
        stored = [inv_ref[me ^ codes[t * fold + f]] ^ me for f in range(fold)]
        masks = x_ref[codes[t * fold], hpg * rows : hpg * rows + 16, :].astype(F32)
        for f in range(1, fold):
            part = x_ref[codes[t * fold + f], hpg * rows : hpg * rows + 16, :].astype(F32)
            masks = jnp.where(lane == f, part, masks)
        mask_ref[:, t * 128 : (t + 1) * 128] = masks[:8]
        return stored, masks > 0

    tiles = [of_tile(t) for t in range(n // fold)]

    def query_slot(p, carry):
        a = qsel_ref[p]
        part = a // (rows // 16)
        row = a % (rows // 16) * 16
        out = pl.multiple_of(p * 16, 16)
        for h in range(hpg):
            start = pl.multiple_of(h * rows + row, 16)
            for t, (stored, present) in enumerate(tiles):
                value = None
                for f in range(fold):
                    block = x_ref[stored[f], pl.ds(start, 16), :].astype(F32)
                    if fold == 2:
                        block = jnp.where(part == f, block, pltpu.roll(block, keys, 1))
                    value = block if value is None else jnp.where(lane == f, block, value)
                value = jnp.where(present, value * LOG2E, NEG * LOG2E)
                bias_ref[h, pl.ds(out, 16), t * 128 : (t + 1) * 128] = value
        return carry

    lax.fori_loop(0, slots, query_slot, 0)


def ordered_bias(parts, me, span_owner, qsel, hpg, keys, codes, window):
    n = len(codes)
    smem = pl.BlockSpec(memory_space=pltpu.SMEM)
    vmem = pl.BlockSpec(memory_space=pltpu.VMEM)
    return pl.pallas_call(
        functools.partial(order_kernel, hpg, keys, codes),
        in_specs=[smem, smem, smem] + [vmem] * len(parts),
        out_specs=[vmem, vmem],
        out_shape=[
            jax.ShapeDtypeStruct((hpg, window, n * keys), F32),
            jax.ShapeDtypeStruct((8, n * keys), F32),
        ],
        scratch_shapes=[
            pltpu.SMEM((n,), jnp.int32),
            pltpu.VMEM((n,) + parts[0].shape[1:], BF16),
        ],
        cost_estimate=pl.CostEstimate(
            flops=hpg * window * n * keys * 8, bytes_accessed=hpg * window * n * keys * 6, transcendentals=0
        ),
        compiler_params=pltpu.CompilerParams(vmem_limit_bytes=VMEM_LIMIT),
        name="bias_order",
    )(me.reshape(1), span_owner, qsel, *parts)


def attention_kernel(pieces, hpg, direct, keys, *refs):
    token_refs, refs = refs[:pieces], refs[pieces:]
    if not direct:
        query_ref, refs = refs[0], refs[1:]
    count = pieces if direct else 1
    bias_ref, mask_ref, wq_ref, wk_ref, wv_ref, wg_ref = refs[:6]
    out_refs, gate_ref = refs[6 : 6 + count], refs[6 + count]
    q_ref, k_ref, v_ref = refs[7 + count :]
    sg, _, _, width = token_refs[0].shape
    feats = wq_ref.shape[1]
    head_size = feats // hpg
    scale = LOG2E / math.sqrt(head_size)

    def rows_of(ref, start, stop):
        block = ref[:, 0, start:stop]
        return block.reshape(block.shape[0] * block.shape[1], width)

    for m in range(pieces):
        block = rows_of(token_refs[m], 0, keys)
        span = slice(m * sg * keys, (m + 1) * sg * keys)
        k_t = nt_dot(wk_ref[...], block)
        k_ref[:, span] = jnp.where(mask_ref[:1, span] > 0, k_t, 0.0).astype(BF16)
        v_ref[span, :] = nn_dot(block, wv_ref[...]).astype(BF16)
    if direct:
        for m in range(pieces):
            block = rows_of(token_refs[m], keys, token_refs[m].shape[2])
            span = slice(m * block.shape[0], (m + 1) * block.shape[0])
            q_ref[span, :] = nn_dot(block, wq_ref[...]).astype(BF16)
            if m == 0:
                gate_ref[0] = jax.nn.sigmoid(nn_dot(block, wg_ref[...]))
    else:
        q_ref[...] = nn_dot(query_ref[0], wq_ref[...]).astype(BF16)
        gate_ref[...] = jnp.zeros_like(gate_ref)
    q = q_ref[...]
    owner = lax.broadcasted_iota(jnp.int32, q.shape, 1) // head_size
    total = None
    for h in range(hpg):
        mine = owner == h
        scores = nn_dot(jnp.where(mine, q, jnp.zeros_like(q)), k_ref[...])
        scores = scores * scale + bias_ref[h]
        weights = jnp.exp2(scores - jnp.max(scores, axis=-1, keepdims=True))
        norm = 1.0 / jnp.sum(weights, axis=-1, keepdims=True)
        result = nn_dot((weights * norm).astype(BF16), v_ref[...])
        total = result if total is None else jnp.where(mine, result, total)
    rows = total.shape[0] // count
    for m in range(count):
        out_refs[m][0] = total[m * rows : (m + 1) * rows].astype(BF16)


def attention(arrays, queries, bias, mask, wq, wk_t, wv, w_gate, hpg, keys, query_rows):
    pieces = len(arrays)
    sg, size, rows, width = arrays[0].shape
    window = bias.shape[1]
    tokens = bias.shape[2]
    feats = wq.shape[1]
    direct = queries is None
    whole = lambda x: pl.BlockSpec(x.shape, lambda s: (0,) * x.ndim)
    specs = [pl.BlockSpec((sg, 1, rows, width), lambda s: (0, s, 0, 0))] * pieces
    args = list(arrays)
    out_rows = [sg * query_rows] * pieces
    if not direct:
        specs.append(pl.BlockSpec((1, window, width), lambda s: (s, 0, 0)))
        args.append(queries)
        out_rows = [window]
    consts = [bias, mask, wq, wk_t, wv, w_gate]
    gate_rows = sg * query_rows
    flops = 2 * size * (tokens * width * feats * 2 + hpg * window * tokens * 512)
    return pl.pallas_call(
        functools.partial(attention_kernel, pieces, hpg, direct, keys),
        grid=(size,),
        in_specs=specs + [whole(x) for x in consts],
        out_specs=[pl.BlockSpec((1, r, feats), lambda s: (s, 0, 0)) for r in out_rows]
        + [pl.BlockSpec((1, gate_rows, width), lambda s: (s, 0, 0))],
        out_shape=[jax.ShapeDtypeStruct((size, r, feats), BF16) for r in out_rows]
        + [jax.ShapeDtypeStruct((size, gate_rows, width), F32)],
        scratch_shapes=[
            pltpu.VMEM((window, feats), BF16),
            pltpu.VMEM((feats, tokens), BF16),
            pltpu.VMEM((tokens, feats), BF16),
        ],
        cost_estimate=pl.CostEstimate(
            flops=flops,
            bytes_accessed=size * tokens * width * 2 + hpg * window * tokens * 4,
            transcendentals=size * hpg * window * tokens,
        ),
        compiler_params=pltpu.CompilerParams(vmem_limit_bytes=VMEM_LIMIT),
        name="attend",
    )(*args, *consts)


def project_kernel(labels, lane_ref, *refs):
    count = len(labels)
    head_refs, (gate_ref, w_ref), out_refs, joined_ref = (
        refs[:count],
        refs[count : count + 2],
        refs[count + 2 : -1],
        refs[-1],
    )
    lane = lane_ref[0]
    size, rows, feats = head_refs[0].shape
    width = w_ref.shape[1]
    values = [ref[...].astype(F32).reshape(size * rows, feats) for ref in head_refs]
    for g in range(count):
        value = values[0]
        for label, other in zip(labels[1:], values[1:]):
            value = jnp.where(lane == g ^ label, other, value)
        joined_ref[:, g * feats : (g + 1) * feats] = value
    gate = gate_ref[...].reshape(size * rows, width)
    gated = (gate * joined_ref[...]).astype(BF16)
    result = nn_dot(gated, w_ref[...]).astype(BF16).reshape(size, len(out_refs), rows // len(out_refs), width)
    for k, out_ref in enumerate(out_refs):
        out_ref[...] = result[:, k]


def projected(lane, heads, gate, w_out, labels, sg, query_rows):
    size, rows, feats = heads[0].shape
    width = w_out.shape[1]
    vmem = pl.BlockSpec(memory_space=pltpu.VMEM)
    return pl.pallas_call(
        functools.partial(project_kernel, labels),
        in_specs=[pl.BlockSpec(memory_space=pltpu.SMEM)] + [vmem] * (len(heads) + 2),
        out_specs=[vmem] * sg,
        out_shape=[jax.ShapeDtypeStruct((size, query_rows, width), BF16)] * sg,
        scratch_shapes=[pltpu.VMEM((size * rows, width), F32)],
        cost_estimate=pl.CostEstimate(
            flops=2 * size * rows * width * width, bytes_accessed=2 * width * width, transcendentals=0
        ),
        compiler_params=pltpu.CompilerParams(vmem_limit_bytes=VMEM_LIMIT),
        name="project",
    )(lane.reshape(1), *heads, gate, w_out)


def assemble_kernel(sg, firsts, group_ref, *refs):
    out_ref = refs[-1]
    group = group_ref[0]
    for i, ref in enumerate(refs[:-1]):
        first, k = firsts[i // sg], i % sg
        out_ref[group ^ k, first : first + ref.shape[0]] = ref[...]


def assembled(group, parts, firsts, shape):
    vmem = pl.BlockSpec(memory_space=pltpu.VMEM)
    return pl.pallas_call(
        functools.partial(assemble_kernel, shape[0], firsts),
        in_specs=[pl.BlockSpec(memory_space=pltpu.SMEM)] + [vmem] * len(parts),
        out_specs=vmem,
        out_shape=jax.ShapeDtypeStruct(shape, BF16),
        compiler_params=pltpu.CompilerParams(vmem_limit_bytes=VMEM_LIMIT),
        name="assemble",
    )(group.reshape(1), *parts)


def head_groups(n, samples):
    hg = 1
    while hg * hg < n or H % hg or samples % (n // hg):
        hg *= 2
    return hg


def local(
    query_tokens,
    key_tokens,
    pair,
    key_mask,
    span_owner,
    pair_gain,
    pair_proj,
    w_query,
    w_key,
    w_value,
    w_gate,
    w_out,
):
    n = lax.axis_size("key")
    samples, query_rows, width = query_tokens.shape
    keys = key_tokens.shape[1]
    window = pair.shape[0]
    hg = head_groups(n, samples)
    sg = n // hg
    hpg = H // hg
    feats = width // hg
    group_samples = samples // sg
    sizes = [2] * ((group_samples - 2) // 2) + [1] * (group_samples - (group_samples - 2) // 2 * 2)
    firsts = [sum(sizes[:c]) for c in range(len(sizes))]
    direct = query_rows % 16 == 0
    me = lax.axis_index("key")
    group, lane = me // hg, me % hg

    def across(x, code):
        if code == 0:
            return x
        return lax.ppermute(x, "key", [(i, i ^ code) for i in range(n)])

    labels = [0]
    bit = hg // 2
    while bit:
        labels = labels + [m ^ bit for m in labels]
        bit //= 2
    codes = [k * hg + m for m in labels for k in range(sg)]
    code_list = jnp.array(codes, jnp.int32)
    slot_of = [0] * n
    for p, code in enumerate(codes):
        slot_of[code] = p

    key_groups = key_tokens.reshape(sg, group_samples, keys, width)
    query_groups = query_tokens.reshape(sg, group_samples, query_rows, width)

    def send(c, after):
        sent = pack(group, key_groups, query_groups, firsts[c], sizes[c])
        if after is not None:
            sent, after = lax.optimization_barrier((sent, after))
        with jax.named_scope(f"z{c}"):
            return [across(x, k * hg) for k, x in enumerate(sent)]

    got = [send(0, None), send(1, None)]

    with jax.named_scope("bias"):
        relative = jnp.arange(hg) ^ lane
        proj_t = jnp.take(pair_proj.T.reshape(hg, hpg, -1), relative, axis=0).reshape(H, -1)
        pieces = local_bias(pair, key_mask, pair_gain, proj_t, hpg)
        spread = stacked([across(x, m) for m, x in enumerate(pieces)])
        parts = {0: spread}
        bit = sg // 2
        while bit:
            parts.update({k ^ bit: across(x, bit * hg) for k, x in parts.items()})
            bit //= 2
        if direct:
            each = query_rows // 16
            qsel = ((code_list ^ me)[:, None] * each + jnp.arange(each)).reshape(window // 16)
        else:
            qsel = jnp.arange(window // 16, dtype=jnp.int32)
        bias, mask = ordered_bias(
            [parts[k] for k in range(sg)], me, span_owner, qsel, hpg, keys, codes, window
        )

    def own(w):
        return lax.dynamic_slice_in_dim(w, lane * feats, feats, 1)

    wq, wk_t, wv = own(w_query), own(w_key).T, own(w_value)

    outs = []
    for c, size in enumerate(sizes):
        if c >= 2:
            got.append(send(c, (got[c - 2], spread) if c == 2 else got[c - 2]))
        arrays = [stacked(got[c])]
        bit = hg // 2
        while bit:
            with jax.named_scope(f"y{c}"):
                arrays = arrays + [across(x, bit) for x in arrays]
            bit //= 2
        queries = None
        if not direct:
            order = jnp.array(slot_of, jnp.int32)[me ^ jnp.arange(n)]
            queries = jnp.concatenate([x[:, :, keys:] for x in arrays], axis=0)
            queries = jnp.swapaxes(jnp.take(queries, order, axis=0), 0, 1).reshape(size, window, width)
        results = attention(arrays, queries, bias, mask, wq, wk_t, wv, w_gate, hpg, keys, query_rows)
        results, gate = results[:-1], results[-1]
        if not direct:
            blocks = jnp.take(results[0].reshape(size, n, query_rows, feats), code_list ^ me, axis=1)
            results = [
                blocks[:, i * sg : (i + 1) * sg].reshape(size, sg * query_rows, feats) for i in range(hg)
            ]
            tokens = jnp.swapaxes(arrays[0][:, :, keys:], 0, 1).reshape(size, sg * query_rows, width)
            gate = jax.nn.sigmoid(nn_dot(tokens, w_gate))
        heads = [across(r, m) for r, m in zip(results, labels)]
        back = projected(lane, heads, gate, w_out, labels, sg, query_rows)
        outs.extend(across(x, k * hg) for k, x in enumerate(back))
    out = assembled(group, outs, firsts, (sg, group_samples, query_rows, width))
    return out.reshape(samples, query_rows, width)


def solution(mesh):
    return jax.shard_map(
        local,
        mesh=mesh,
        in_specs=(
            P("rep", "key", None),
            P("rep", "key", None),
            P("rep", "key", None),
            P(("rep", "key")),
            P("rep"),
            P(),
            P(),
            P(),
            P(),
            P(),
            P(),
            P(),
        ),
        out_specs=P("rep", "key", None),
        check_vma=False,
    )
```

```python
import functools
import math

import jax
import jax.numpy as jnp
from jax import lax
from jax.experimental import pallas as pl
from jax.experimental.pallas import tpu as pltpu
from jax.sharding import PartitionSpec as P


H = 16
LOG2E = 1.4426950408889634
NEG = -1e9
VMEM_LIMIT = 60 * 1024 * 1024
F32 = jnp.float32
BF16 = jnp.bfloat16


def nt_dot(a, b):
    return lax.dot_general(a, b, (((1,), (1,)), ((), ())), preferred_element_type=F32)


def nn_dot(a, b):
    return jnp.dot(a, b, preferred_element_type=F32)


def bias_kernel(hpg, mask_ref, pair_ref, gain_ref, proj_ref, *out_refs):
    fold, rows, keys, c = pair_ref.shape
    heads = proj_ref.shape[0]
    step = pl.program_id(0)
    total_rows = (out_refs[0].shape[0] - 16) // hpg
    x = jnp.swapaxes(pair_ref[...], 0, 1).reshape(rows * fold * keys, c).astype(F32)
    center = x - jnp.mean(x, axis=-1, keepdims=True)
    spread = jnp.mean(center * center, axis=-1, keepdims=True)
    normed = (center * lax.rsqrt(spread + 1e-5) * gain_ref[...]).astype(BF16)
    bias = nt_dot(proj_ref[...], normed)
    bias = bias.reshape(heads, rows, fold * keys).astype(BF16)
    for h in range(heads):
        start = pl.multiple_of((h % hpg) * total_rows + step * rows, 16)
        out_refs[h // hpg][pl.ds(start, rows), :] = bias[h]

    @pl.when(step == 0)
    def _():
        row = jnp.broadcast_to(mask_ref[...], (16, fold * keys)).astype(BF16)
        for out_ref in out_refs:
            out_ref[hpg * total_rows :, :] = row


def local_bias(pair, key_mask, pair_gain, proj_t, hpg):
    window, keys, c = pair.shape
    heads = proj_t.shape[0]
    fold = 128 // keys
    rows = window // fold
    tile = 16
    mask = jnp.tile(key_mask.astype(F32), fold)[None]
    shape = (hpg * rows + 16, 128)
    return pl.pallas_call(
        functools.partial(bias_kernel, hpg),
        grid=(rows // tile,),
        in_specs=[
            pl.BlockSpec((1, 128), lambda i: (0, 0)),
            pl.BlockSpec((fold, tile, keys, c), lambda i: (0, i, 0, 0)),
            pl.BlockSpec((1, c), lambda i: (0, 0)),
            pl.BlockSpec((heads, c), lambda i: (0, 0)),
        ],
        out_specs=[pl.BlockSpec(shape, lambda i: (0, 0))] * (heads // hpg),
        out_shape=[jax.ShapeDtypeStruct(shape, BF16)] * (heads // hpg),
        cost_estimate=pl.CostEstimate(
            flops=2 * window * keys * c * 256, bytes_accessed=window * keys * c * 2, transcendentals=0
        ),
        compiler_params=pltpu.CompilerParams(vmem_limit_bytes=VMEM_LIMIT),
        name="bias_local",
    )(mask, pair.reshape(fold, rows, keys, c), pair_gain[None], proj_t)


def pack_kernel(sizes, sg, group_ref, *refs):
    step = pl.program_id(0)
    start = 0
    for i, size in enumerate(sizes):

        @pl.when((step >= start) & (step < start + size))
        def _(i=i):
            for k in range(sg):
                out_ref = refs[(2 + i) * sg + k]
                keys = refs[k].shape[2]
                out_ref[0, :keys] = refs[k][0, 0]
                out_ref[0, keys:] = refs[sg + k][0, 0]

        start += size


def pack(group, key_groups, query_groups, first, sizes):
    sg, _, keys, width = key_groups.shape
    rows = query_groups.shape[2]
    total = sum(sizes)

    def spec(length, k):
        return pl.BlockSpec((1, 1, length, width), lambda s, g: (g[0] ^ k, first + s, 0, 0))

    def out_spec(i):
        start = sum(sizes[:i])
        return pl.BlockSpec(
            (1, keys + rows, width), lambda s, g: (jnp.clip(s - start, 0, sizes[i] - 1), 0, 0)
        )

    outs = pl.pallas_call(
        functools.partial(pack_kernel, sizes, sg),
        grid_spec=pltpu.PrefetchScalarGridSpec(
            num_scalar_prefetch=1,
            grid=(total,),
            in_specs=[spec(keys, k) for k in range(sg)] + [spec(rows, k) for k in range(sg)],
            out_specs=[out_spec(i) for i in range(len(sizes)) for _ in range(sg)],
        ),
        out_shape=[jax.ShapeDtypeStruct((size, keys + rows, width), BF16) for size in sizes for _ in range(sg)],
        cost_estimate=pl.CostEstimate(
            flops=0, bytes_accessed=4 * sg * total * (keys + rows) * width, transcendentals=0
        ),
        name="pack",
    )(group.reshape(1), *([key_groups] * sg), *([query_groups] * sg))
    return [outs[i * sg : (i + 1) * sg] for i in range(len(sizes))]


def stack_kernel(*refs):
    for i, ref in enumerate(refs[:-1]):
        refs[-1][i] = ref[...]


def stacked(parts):
    count, shape = len(parts), parts[0].shape
    rest = (0,) * (len(shape) - 1)
    block = (1,) + shape[1:] if len(shape) == 3 else shape
    steps = shape[0] if len(shape) == 3 else 1
    return pl.pallas_call(
        stack_kernel,
        grid=(steps,),
        in_specs=[pl.BlockSpec(block, lambda s: (s,) + rest)] * count,
        out_specs=pl.BlockSpec((count,) + block, lambda s: (0, s) + rest),
        out_shape=jax.ShapeDtypeStruct((count,) + shape, BF16),
        cost_estimate=pl.CostEstimate(
            flops=0, bytes_accessed=4 * count * math.prod(shape), transcendentals=0
        ),
        name="stack",
    )(*parts)


def order_kernel(hpg, keys, codes, me_ref, owner_ref, qsel_ref, *refs):
    parts, (bias_ref, mask_ref, inv_ref, x_ref) = refs[:-4], refs[-4:]
    n = len(codes)
    each = n // len(parts)
    for k, part_ref in enumerate(parts):
        x_ref[k * each : (k + 1) * each] = part_ref[...]
    fold = 128 // keys
    me = me_ref[0]
    rows = (x_ref.shape[1] - 16) // hpg
    slots = bias_ref.shape[1] // 16
    for d in range(n):
        inv_ref[owner_ref[d]] = d
    lane = lax.broadcasted_iota(jnp.int32, (16, 128), 1) // keys

    def of_tile(t):
        stored = [inv_ref[me ^ codes[t * fold + f]] ^ me for f in range(fold)]
        masks = x_ref[codes[t * fold], hpg * rows : hpg * rows + 16, :].astype(F32)
        for f in range(1, fold):
            part = x_ref[codes[t * fold + f], hpg * rows : hpg * rows + 16, :].astype(F32)
            masks = jnp.where(lane == f, part, masks)
        mask_ref[:, t * 128 : (t + 1) * 128] = masks[:8]
        return stored, masks > 0

    tiles = [of_tile(t) for t in range(n // fold)]

    def query_slot(p, carry):
        a = qsel_ref[p]
        part = a // (rows // 16)
        row = a % (rows // 16) * 16
        out = pl.multiple_of(p * 16, 16)
        for h in range(hpg):
            start = pl.multiple_of(h * rows + row, 16)
            for t, (stored, present) in enumerate(tiles):
                value = None
                for f in range(fold):
                    block = x_ref[stored[f], pl.ds(start, 16), :].astype(F32)
                    if fold == 2:
                        block = jnp.where(part == f, block, pltpu.roll(block, keys, 1))
                    value = block if value is None else jnp.where(lane == f, block, value)
                value = jnp.where(present, value * LOG2E, NEG * LOG2E)
                bias_ref[h, pl.ds(out, 16), t * 128 : (t + 1) * 128] = value
        return carry

    lax.fori_loop(0, slots, query_slot, 0)


def ordered_bias(parts, me, span_owner, qsel, hpg, keys, codes, window):
    n = len(codes)
    smem = pl.BlockSpec(memory_space=pltpu.SMEM)
    vmem = pl.BlockSpec(memory_space=pltpu.VMEM)
    return pl.pallas_call(
        functools.partial(order_kernel, hpg, keys, codes),
        in_specs=[smem, smem, smem] + [vmem] * len(parts),
        out_specs=[vmem, vmem],
        out_shape=[
            jax.ShapeDtypeStruct((hpg, window, n * keys), F32),
            jax.ShapeDtypeStruct((8, n * keys), F32),
        ],
        scratch_shapes=[
            pltpu.SMEM((n,), jnp.int32),
            pltpu.VMEM((n,) + parts[0].shape[1:], BF16),
        ],
        cost_estimate=pl.CostEstimate(
            flops=hpg * window * n * keys * 8, bytes_accessed=hpg * window * n * keys * 6, transcendentals=0
        ),
        compiler_params=pltpu.CompilerParams(vmem_limit_bytes=VMEM_LIMIT),
        name="bias_order",
    )(me.reshape(1), span_owner, qsel, *parts)


def attention_kernel(pieces, hpg, direct, keys, *refs):
    token_refs, refs = refs[:pieces], refs[pieces:]
    if not direct:
        query_ref, refs = refs[0], refs[1:]
    count = pieces if direct else 1
    bias_ref, mask_ref, wq_ref, wk_ref, wv_ref, wg_ref = refs[:6]
    out_refs, gate_ref = refs[6 : 6 + count], refs[6 + count]
    q_ref, k_ref, v_ref = refs[7 + count :]
    sg, _, _, width = token_refs[0].shape
    feats = wq_ref.shape[1]
    head_size = feats // hpg
    scale = LOG2E / math.sqrt(head_size)

    def rows_of(ref, start, stop):
        block = ref[:, 0, start:stop]
        return block.reshape(block.shape[0] * block.shape[1], width)

    for m in range(pieces):
        block = rows_of(token_refs[m], 0, keys)
        span = slice(m * sg * keys, (m + 1) * sg * keys)
        k_t = nt_dot(wk_ref[...], block)
        k_ref[:, span] = jnp.where(mask_ref[:1, span] > 0, k_t, 0.0).astype(BF16)
        v_ref[span, :] = nn_dot(block, wv_ref[...]).astype(BF16)
    if direct:
        for m in range(pieces):
            block = rows_of(token_refs[m], keys, token_refs[m].shape[2])
            span = slice(m * block.shape[0], (m + 1) * block.shape[0])
            q_ref[span, :] = nn_dot(block, wq_ref[...]).astype(BF16)
            if m == 0:
                gate_ref[0] = jax.nn.sigmoid(nn_dot(block, wg_ref[...]))
    else:
        q_ref[...] = nn_dot(query_ref[0], wq_ref[...]).astype(BF16)
        gate_ref[...] = jnp.zeros_like(gate_ref)
    q = q_ref[...]
    owner = lax.broadcasted_iota(jnp.int32, q.shape, 1) // head_size
    total = None
    for h in range(hpg):
        mine = owner == h
        scores = nn_dot(jnp.where(mine, q, jnp.zeros_like(q)), k_ref[...])
        scores = scores * scale + bias_ref[h]
        weights = jnp.exp2(scores - jnp.max(scores, axis=-1, keepdims=True))
        norm = 1.0 / jnp.sum(weights, axis=-1, keepdims=True)
        result = nn_dot((weights * norm).astype(BF16), v_ref[...])
        total = result if total is None else jnp.where(mine, result, total)
    rows = total.shape[0] // count
    for m in range(count):
        out_refs[m][0] = total[m * rows : (m + 1) * rows].astype(BF16)


def attention(arrays, queries, bias, mask, wq, wk_t, wv, w_gate, hpg, keys, query_rows):
    pieces = len(arrays)
    sg, size, rows, width = arrays[0].shape
    window = bias.shape[1]
    tokens = bias.shape[2]
    feats = wq.shape[1]
    direct = queries is None
    whole = pl.BlockSpec(memory_space=pltpu.VMEM)
    specs = [pl.BlockSpec((sg, 1, rows, width), lambda s: (0, s, 0, 0))] * pieces
    args = list(arrays)
    out_rows = [sg * query_rows] * pieces
    if not direct:
        specs.append(pl.BlockSpec((1, window, width), lambda s: (s, 0, 0)))
        args.append(queries)
        out_rows = [window]
    consts = [bias, mask, wq, wk_t, wv, w_gate]
    gate_rows = sg * query_rows
    limit = VMEM_LIMIT if tokens > 2048 else 36 * 1024 * 1024
    flops = 2 * size * (tokens * width * feats * 2 + hpg * window * tokens * 512)
    return pl.pallas_call(
        functools.partial(attention_kernel, pieces, hpg, direct, keys),
        grid=(size,),
        in_specs=specs + [whole] * len(consts),
        out_specs=[pl.BlockSpec((1, r, feats), lambda s: (s, 0, 0)) for r in out_rows]
        + [pl.BlockSpec((1, gate_rows, width), lambda s: (s, 0, 0))],
        out_shape=[jax.ShapeDtypeStruct((size, r, feats), BF16) for r in out_rows]
        + [jax.ShapeDtypeStruct((size, gate_rows, width), F32)],
        scratch_shapes=[
            pltpu.VMEM((window, feats), BF16),
            pltpu.VMEM((feats, tokens), BF16),
            pltpu.VMEM((tokens, feats), BF16),
        ],
        cost_estimate=pl.CostEstimate(
            flops=flops,
            bytes_accessed=size * tokens * width * 2 + hpg * window * tokens * 4,
            transcendentals=size * hpg * window * tokens,
        ),
        compiler_params=pltpu.CompilerParams(vmem_limit_bytes=limit),
        name="attend",
    )(*args, *consts)


def project_kernel(labels, sizes, lane_ref, *refs):
    count = len(labels)
    chunks = len(sizes)
    head_refs, refs = refs[: count * chunks], refs[count * chunks :]
    gate_refs, w_ref, refs = refs[:chunks], refs[chunks], refs[chunks + 1 :]
    out_refs, joined_ref = refs[:-1], refs[-1]
    lane = lane_ref[0]
    width = w_ref.shape[1]
    first = 0
    for c, size in enumerate(sizes):
        parts = head_refs[c * count : (c + 1) * count]
        _, rows, feats = parts[0].shape
        values = [ref[...].astype(F32).reshape(size * rows, feats) for ref in parts]
        for g in range(count):
            value = values[0]
            for label, other in zip(labels[1:], values[1:]):
                value = jnp.where(lane == g ^ label, other, value)
            joined_ref[: size * rows, g * feats : (g + 1) * feats] = value
        gate = gate_refs[c][...].reshape(size * rows, width)
        gated = (gate * joined_ref[: size * rows]).astype(BF16)
        result = nn_dot(gated, w_ref[...]).astype(BF16)
        result = result.reshape(size, len(out_refs), rows // len(out_refs), width)
        for k, out_ref in enumerate(out_refs):
            out_ref[first : first + size] = result[:, k]
        first += size


def projected(lane, heads, gates, w_out, labels, sg, query_rows):
    sizes = [x[0].shape[0] for x in heads]
    _, rows, _ = heads[0][0].shape
    width = w_out.shape[1]
    vmem = pl.BlockSpec(memory_space=pltpu.VMEM)
    flat = [x for chunk in heads for x in chunk]
    return pl.pallas_call(
        functools.partial(project_kernel, labels, sizes),
        in_specs=[pl.BlockSpec(memory_space=pltpu.SMEM)] + [vmem] * (len(flat) + len(gates) + 1),
        out_specs=[vmem] * sg,
        out_shape=[jax.ShapeDtypeStruct((sum(sizes), query_rows, width), BF16)] * sg,
        scratch_shapes=[pltpu.VMEM((max(sizes) * rows, width), F32)],
        cost_estimate=pl.CostEstimate(
            flops=2 * sum(sizes) * rows * width * width, bytes_accessed=2 * width * width, transcendentals=0
        ),
        name="project",
    )(lane.reshape(1), *flat, *gates, w_out)


def assemble_kernel(sg, firsts, group_ref, *refs):
    out_ref = refs[-1]
    group = group_ref[0]
    for i, ref in enumerate(refs[:-1]):
        first, k = firsts[i // sg], i % sg
        out_ref[group ^ k, first : first + ref.shape[0]] = ref[...]


def assembled(group, parts, firsts, shape):
    vmem = pl.BlockSpec(memory_space=pltpu.VMEM)
    return pl.pallas_call(
        functools.partial(assemble_kernel, shape[0], firsts),
        in_specs=[pl.BlockSpec(memory_space=pltpu.SMEM)] + [vmem] * len(parts),
        out_specs=vmem,
        out_shape=jax.ShapeDtypeStruct(shape, BF16),
        name="assemble",
    )(group.reshape(1), *parts)


def head_groups(n, samples):
    hg = 1
    while hg * hg < n or H % hg or samples % (n // hg):
        hg *= 2
    return hg


def local(
    query_tokens,
    key_tokens,
    pair,
    key_mask,
    span_owner,
    pair_gain,
    pair_proj,
    w_query,
    w_key,
    w_value,
    w_gate,
    w_out,
):
    n = lax.axis_size("key")
    samples, query_rows, width = query_tokens.shape
    keys = key_tokens.shape[1]
    window = pair.shape[0]
    hg = head_groups(n, samples)
    sg = n // hg
    hpg = H // hg
    feats = width // hg
    group_samples = samples // sg
    last = max(group_samples // 6, 1)
    middle = max(group_samples // 3, 1)
    sizes = [group_samples - middle - last, middle, last]
    firsts = [sum(sizes[:c]) for c in range(len(sizes))]
    direct = query_rows % 16 == 0
    me = lax.axis_index("key")
    group, lane = me // hg, me % hg

    def across(x, code):
        if code == 0:
            return x
        return lax.ppermute(x, "key", [(i, i ^ code) for i in range(n)])

    labels = [0]
    bit = hg // 2
    while bit:
        labels = labels + [m ^ bit for m in labels]
        bit //= 2
    codes = [k * hg + m for m in labels for k in range(sg)]
    code_list = jnp.array(codes, jnp.int32)
    slot_of = [0] * n
    for p, code in enumerate(codes):
        slot_of[code] = p

    key_groups = key_tokens.reshape(sg, group_samples, keys, width)
    query_groups = query_tokens.reshape(sg, group_samples, query_rows, width)

    packed = pack(group, key_groups, query_groups, 0, sizes[:1])
    packed = packed + pack(group, key_groups, query_groups, firsts[1], sizes[1:])
    got = [[across(x, k * hg) for k, x in enumerate(sent)] for sent in packed]

    relative = jnp.arange(hg) ^ lane
    proj_t = jnp.take(pair_proj.T.reshape(hg, hpg, -1), relative, axis=0).reshape(H, -1)
    pieces = local_bias(pair, key_mask, pair_gain, proj_t, hpg)
    pieces = [across(x, m) for m, x in enumerate(pieces)]
    parts = {0: stacked(pieces)}
    bit = sg // 2
    while bit:
        parts.update({k ^ bit: across(x, bit * hg) for k, x in parts.items()})
        bit //= 2
    if direct:
        each = query_rows // 16
        qsel = ((code_list ^ me)[:, None] * each + jnp.arange(each)).reshape(window // 16)
    else:
        qsel = jnp.arange(window // 16, dtype=jnp.int32)
    bias, mask = ordered_bias(
        [parts[k] for k in range(sg)], me, span_owner, qsel, hpg, keys, codes, window
    )

    def own(w):
        return lax.dynamic_slice_in_dim(w, lane * feats, feats, 1)

    wq, wk_t, wv = own(w_query), own(w_key).T, own(w_value)

    heads, gates = [], []
    previous = None
    for c, size in enumerate(sizes):
        arrays = [stacked(got[c])]
        bit = hg // 2
        while bit:
            arrays = arrays + [across(x, bit) for x in arrays]
            bit //= 2
        queries = None
        if not direct:
            order = jnp.array(slot_of, jnp.int32)[me ^ jnp.arange(n)]
            queries = jnp.concatenate([x[:, :, keys:] for x in arrays], axis=0)
            queries = jnp.swapaxes(jnp.take(queries, order, axis=0), 0, 1).reshape(size, window, width)
        if previous is not None:
            arrays, previous = lax.optimization_barrier((arrays, previous))
        results = attention(arrays, queries, bias, mask, wq, wk_t, wv, w_gate, hpg, keys, query_rows)
        results, gate = results[:-1], results[-1]
        previous = gate
        if not direct:
            blocks = jnp.take(results[0].reshape(size, n, query_rows, feats), code_list ^ me, axis=1)
            results = [
                blocks[:, i * sg : (i + 1) * sg].reshape(size, sg * query_rows, feats) for i in range(hg)
            ]
            tokens = jnp.swapaxes(arrays[0][:, :, keys:], 0, 1).reshape(size, sg * query_rows, width)
            gate = jax.nn.sigmoid(nn_dot(tokens, w_gate))
        heads.append([across(r, m) for r, m in zip(results, labels)])
        gates.append(gate)
    outs = []
    cut = len(sizes) - 1
    for span in (slice(0, cut), slice(cut, cut + 1)):
        back = projected(lane, heads[span], gates[span], w_out, labels, sg, query_rows)
        outs.extend(across(x, k * hg) for k, x in enumerate(back))
    out = assembled(group, outs, [0, firsts[cut]], (sg, group_samples, query_rows, width))
    return out.reshape(samples, query_rows, width)


def solution(mesh):
    return jax.shard_map(
        local,
        mesh=mesh,
        in_specs=(
            P("rep", "key", None),
            P("rep", "key", None),
            P("rep", "key", None),
            P(("rep", "key")),
            P("rep"),
            P(),
            P(),
            P(),
            P(),
            P(),
            P(),
            P(),
        ),
        out_specs=P("rep", "key", None),
        check_vma=False,
    )
```

```python
import functools
import math

import jax
import jax.numpy as jnp
from jax import lax
from jax.experimental import pallas as pl
from jax.experimental.pallas import tpu as pltpu
from jax.sharding import PartitionSpec as P


H = 16
LOG2E = 1.4426950408889634
NEG = -1e9
MIB = 1024 * 1024
F32 = jnp.float32
BF16 = jnp.bfloat16


def nt_dot(a, b):
    return lax.dot_general(a, b, (((1,), (1,)), ((), ())), preferred_element_type=F32)


def nn_dot(a, b):
    return jnp.dot(a, b, preferred_element_type=F32)


def bias_kernel(hpg, mask_ref, pair_ref, gain_ref, proj_ref, *out_refs):
    fold, rows, keys, c = pair_ref.shape
    heads = proj_ref.shape[0]
    step = pl.program_id(0)
    total_rows = (out_refs[0].shape[0] - 16) // hpg
    x = jnp.swapaxes(pair_ref[...], 0, 1).reshape(rows * fold * keys, c).astype(F32)
    center = x - jnp.mean(x, axis=-1, keepdims=True)
    spread = jnp.mean(center * center, axis=-1, keepdims=True)
    normed = (center * lax.rsqrt(spread + 1e-5) * gain_ref[...]).astype(BF16)
    bias = nt_dot(proj_ref[...], normed)
    bias = bias.reshape(heads, rows, fold * keys).astype(BF16)
    for h in range(heads):
        start = pl.multiple_of((h % hpg) * total_rows + step * rows, 16)
        out_refs[h // hpg][pl.ds(start, rows), :] = bias[h]

    @pl.when(step == 0)
    def _():
        row = jnp.broadcast_to(mask_ref[...], (16, fold * keys)).astype(BF16)
        for out_ref in out_refs:
            out_ref[hpg * total_rows :, :] = row


def local_bias(pair, key_mask, pair_gain, proj_t, hpg):
    window, keys, c = pair.shape
    heads = proj_t.shape[0]
    fold = 128 // keys
    rows = window // fold
    tile = 16
    mask = jnp.tile(key_mask.astype(F32), fold)[None]
    shape = (hpg * rows + 16, 128)
    return pl.pallas_call(
        functools.partial(bias_kernel, hpg),
        grid=(rows // tile,),
        in_specs=[
            pl.BlockSpec((1, 128), lambda i: (0, 0)),
            pl.BlockSpec((fold, tile, keys, c), lambda i: (0, i, 0, 0)),
            pl.BlockSpec((1, c), lambda i: (0, 0)),
            pl.BlockSpec((heads, c), lambda i: (0, 0)),
        ],
        out_specs=[pl.BlockSpec(shape, lambda i: (0, 0))] * (heads // hpg),
        out_shape=[jax.ShapeDtypeStruct(shape, BF16)] * (heads // hpg),
        cost_estimate=pl.CostEstimate(
            flops=2 * window * keys * c * 256, bytes_accessed=window * keys * c * 2, transcendentals=0
        ),
        compiler_params=pltpu.CompilerParams(vmem_limit_bytes=16 * MIB),
        name="bias_local",
    )(mask, pair.reshape(fold, rows, keys, c), pair_gain[None], proj_t)


def pack_kernel(sizes, sg, group_ref, *refs):
    step = pl.program_id(0)
    start = 0
    for i, size in enumerate(sizes):

        @pl.when((step >= start) & (step < start + size))
        def _(i=i):
            for k in range(sg):
                out_ref = refs[(2 + i) * sg + k]
                keys = refs[k].shape[2]
                out_ref[0, :keys] = refs[k][0, 0]
                out_ref[0, keys:] = refs[sg + k][0, 0]

        start += size


def pack(group, key_groups, query_groups, first, sizes):
    sg, _, keys, width = key_groups.shape
    rows = query_groups.shape[2]
    total = sum(sizes)

    def spec(length, k):
        return pl.BlockSpec((1, 1, length, width), lambda s, g: (g[0] ^ k, first + s, 0, 0))

    def out_spec(i):
        start = sum(sizes[:i])
        return pl.BlockSpec(
            (1, keys + rows, width), lambda s, g: (jnp.clip(s - start, 0, sizes[i] - 1), 0, 0)
        )

    outs = pl.pallas_call(
        functools.partial(pack_kernel, sizes, sg),
        grid_spec=pltpu.PrefetchScalarGridSpec(
            num_scalar_prefetch=1,
            grid=(total,),
            in_specs=[spec(keys, k) for k in range(sg)] + [spec(rows, k) for k in range(sg)],
            out_specs=[out_spec(i) for i in range(len(sizes)) for _ in range(sg)],
        ),
        out_shape=[jax.ShapeDtypeStruct((size, keys + rows, width), BF16) for size in sizes for _ in range(sg)],
        cost_estimate=pl.CostEstimate(
            flops=0, bytes_accessed=4 * sg * total * (keys + rows) * width, transcendentals=0
        ),
        compiler_params=pltpu.CompilerParams(vmem_limit_bytes=12 * MIB),
        name="pack",
    )(group.reshape(1), *([key_groups] * sg), *([query_groups] * sg))
    return [outs[i * sg : (i + 1) * sg] for i in range(len(sizes))]


def stack_kernel(*refs):
    for i, ref in enumerate(refs[:-1]):
        refs[-1][i] = ref[...]


def stacked(parts):
    count, shape = len(parts), parts[0].shape
    rest = (0,) * (len(shape) - 1)
    block = (1,) + shape[1:] if len(shape) == 3 else shape
    steps = shape[0] if len(shape) == 3 else 1
    return pl.pallas_call(
        stack_kernel,
        grid=(steps,),
        in_specs=[pl.BlockSpec(block, lambda s: (s,) + rest)] * count,
        out_specs=pl.BlockSpec((count,) + block, lambda s: (0, s) + rest),
        out_shape=jax.ShapeDtypeStruct((count,) + shape, BF16),
        cost_estimate=pl.CostEstimate(
            flops=0, bytes_accessed=4 * count * math.prod(shape), transcendentals=0
        ),
        compiler_params=pltpu.CompilerParams(vmem_limit_bytes=8 * MIB),
        name="stack",
    )(*parts)


def order_kernel(hpg, keys, codes, me_ref, owner_ref, qsel_ref, *refs):
    parts, (bias_ref, mask_ref, inv_ref, x_ref) = refs[:-4], refs[-4:]
    n = len(codes)
    each = n // len(parts)
    for k, part_ref in enumerate(parts):
        x_ref[k * each : (k + 1) * each] = part_ref[...]
    fold = 128 // keys
    me = me_ref[0]
    rows = (x_ref.shape[1] - 16) // hpg
    slots = bias_ref.shape[1] // 16
    for d in range(n):
        inv_ref[owner_ref[d]] = d
    lane = lax.broadcasted_iota(jnp.int32, (16, 128), 1) // keys

    def of_tile(t):
        stored = [inv_ref[me ^ codes[t * fold + f]] ^ me for f in range(fold)]
        masks = x_ref[codes[t * fold], hpg * rows : hpg * rows + 16, :].astype(F32)
        for f in range(1, fold):
            part = x_ref[codes[t * fold + f], hpg * rows : hpg * rows + 16, :].astype(F32)
            masks = jnp.where(lane == f, part, masks)
        mask_ref[:, t * 128 : (t + 1) * 128] = masks[:8]
        return stored, masks > 0

    tiles = [of_tile(t) for t in range(n // fold)]

    def query_slot(p, carry):
        a = qsel_ref[p]
        part = a // (rows // 16)
        row = a % (rows // 16) * 16
        out = pl.multiple_of(p * 16, 16)
        for h in range(hpg):
            start = pl.multiple_of(h * rows + row, 16)
            for t, (stored, present) in enumerate(tiles):
                value = None
                for f in range(fold):
                    block = x_ref[stored[f], pl.ds(start, 16), :].astype(F32)
                    if fold == 2:
                        block = jnp.where(part == f, block, pltpu.roll(block, keys, 1))
                    value = block if value is None else jnp.where(lane == f, block, value)
                value = jnp.where(present, value * LOG2E, NEG * LOG2E)
                bias_ref[h, pl.ds(out, 16), t * 128 : (t + 1) * 128] = value
        return carry

    lax.fori_loop(0, slots, query_slot, 0)


def ordered_bias(parts, me, span_owner, qsel, hpg, keys, codes, window):
    n = len(codes)
    limit = (40 if n * keys > 2048 else 14) * MIB
    smem = pl.BlockSpec(memory_space=pltpu.SMEM)
    vmem = pl.BlockSpec(memory_space=pltpu.VMEM)
    return pl.pallas_call(
        functools.partial(order_kernel, hpg, keys, codes),
        in_specs=[smem, smem, smem] + [vmem] * len(parts),
        out_specs=[vmem, vmem],
        out_shape=[
            jax.ShapeDtypeStruct((hpg, window, n * keys), F32),
            jax.ShapeDtypeStruct((8, n * keys), F32),
        ],
        scratch_shapes=[
            pltpu.SMEM((n,), jnp.int32),
            pltpu.VMEM((n,) + parts[0].shape[1:], BF16),
        ],
        cost_estimate=pl.CostEstimate(
            flops=hpg * window * n * keys * 8, bytes_accessed=hpg * window * n * keys * 6, transcendentals=0
        ),
        compiler_params=pltpu.CompilerParams(vmem_limit_bytes=limit),
        name="bias_order",
    )(me.reshape(1), span_owner, qsel, *parts)


def attention_kernel(pieces, hpg, direct, keys, *refs):
    token_refs, refs = refs[:pieces], refs[pieces:]
    if not direct:
        query_ref, refs = refs[0], refs[1:]
    count = pieces if direct else 1
    bias_ref, mask_ref, wq_ref, wk_ref, wv_ref, wg_ref = refs[:6]
    out_refs, gate_ref = refs[6 : 6 + count], refs[6 + count]
    q_ref, k_ref, v_ref = refs[7 + count :]
    sg, _, _, width = token_refs[0].shape
    feats = wq_ref.shape[1]
    head_size = feats // hpg
    scale = LOG2E / math.sqrt(head_size)

    def rows_of(ref, start, stop):
        block = ref[:, 0, start:stop]
        return block.reshape(block.shape[0] * block.shape[1], width)

    for m in range(pieces):
        block = rows_of(token_refs[m], 0, keys)
        span = slice(m * sg * keys, (m + 1) * sg * keys)
        k_t = nn_dot(block, wk_ref[...]).T
        k_ref[:, span] = jnp.where(mask_ref[:1, span] > 0, k_t, 0.0).astype(BF16)
        v_ref[span, :] = nn_dot(block, wv_ref[...]).astype(BF16)
    if direct:
        for m in range(pieces):
            block = rows_of(token_refs[m], keys, token_refs[m].shape[2])
            span = slice(m * block.shape[0], (m + 1) * block.shape[0])
            q_ref[span, :] = nn_dot(block, wq_ref[...]).astype(BF16)
            if m == 0:
                gate_ref[0] = jax.nn.sigmoid(nn_dot(block, wg_ref[...]))
    else:
        q_ref[...] = nn_dot(query_ref[0], wq_ref[...]).astype(BF16)
        gate_ref[...] = jnp.zeros_like(gate_ref)
    q = q_ref[...]
    owner = lax.broadcasted_iota(jnp.int32, q.shape, 1) // head_size
    total = None
    for h in range(hpg):
        mine = owner == h
        scores = nn_dot(jnp.where(mine, q, jnp.zeros_like(q)), k_ref[...])
        scores = scores * scale + bias_ref[h]
        weights = jnp.exp2(scores - jnp.max(scores, axis=-1, keepdims=True))
        norm = 1.0 / jnp.sum(weights, axis=-1, keepdims=True)
        result = nn_dot((weights * norm).astype(BF16), v_ref[...])
        total = result if total is None else jnp.where(mine, result, total)
    rows = total.shape[0] // count
    for m in range(count):
        out_refs[m][0] = total[m * rows : (m + 1) * rows].astype(BF16)


def attention(arrays, queries, bias, mask, wq, wk, wv, w_gate, hpg, keys, query_rows):
    pieces = len(arrays)
    sg, size, rows, width = arrays[0].shape
    window = bias.shape[1]
    tokens = bias.shape[2]
    feats = wq.shape[1]
    direct = queries is None
    whole = pl.BlockSpec(memory_space=pltpu.VMEM)
    specs = [pl.BlockSpec((sg, 1, rows, width), lambda s: (0, s, 0, 0))] * pieces
    args = list(arrays)
    out_rows = [sg * query_rows] * pieces
    if not direct:
        specs.append(pl.BlockSpec((1, window, width), lambda s: (s, 0, 0)))
        args.append(queries)
        out_rows = [window]
    consts = [bias, mask, wq, wk, wv, w_gate]
    gate_rows = sg * query_rows
    limit = (60 if tokens > 2048 else 26) * MIB
    flops = 2 * size * (tokens * width * feats * 2 + hpg * window * tokens * 512)
    return pl.pallas_call(
        functools.partial(attention_kernel, pieces, hpg, direct, keys),
        grid=(size,),
        in_specs=specs + [whole] * len(consts),
        out_specs=[pl.BlockSpec((1, r, feats), lambda s: (s, 0, 0)) for r in out_rows]
        + [pl.BlockSpec((1, gate_rows, width), lambda s: (s, 0, 0))],
        out_shape=[jax.ShapeDtypeStruct((size, r, feats), BF16) for r in out_rows]
        + [jax.ShapeDtypeStruct((size, gate_rows, width), F32)],
        scratch_shapes=[
            pltpu.VMEM((window, feats), BF16),
            pltpu.VMEM((feats, tokens), BF16),
            pltpu.VMEM((tokens, feats), BF16),
        ],
        cost_estimate=pl.CostEstimate(
            flops=flops,
            bytes_accessed=size * tokens * width * 2 + hpg * window * tokens * 4,
            transcendentals=size * hpg * window * tokens,
        ),
        compiler_params=pltpu.CompilerParams(vmem_limit_bytes=limit),
        name="attend",
    )(*args, *consts)


def project_kernel(labels, sizes, lane_ref, *refs):
    count = len(labels)
    chunks = len(sizes)
    head_refs, refs = refs[: count * chunks], refs[count * chunks :]
    gate_refs, w_ref, refs = refs[:chunks], refs[chunks], refs[chunks + 1 :]
    out_refs, joined_ref = refs[:-1], refs[-1]
    lane = lane_ref[0]
    width = w_ref.shape[1]
    first = 0
    for c, size in enumerate(sizes):
        parts = head_refs[c * count : (c + 1) * count]
        _, rows, feats = parts[0].shape
        values = [ref[...].astype(F32).reshape(size * rows, feats) for ref in parts]
        for g in range(count):
            value = values[0]
            for label, other in zip(labels[1:], values[1:]):
                value = jnp.where(lane == g ^ label, other, value)
            joined_ref[: size * rows, g * feats : (g + 1) * feats] = value
        gate = gate_refs[c][...].reshape(size * rows, width)
        gated = (gate * joined_ref[: size * rows]).astype(BF16)
        result = nn_dot(gated, w_ref[...]).astype(BF16)
        result = result.reshape(size, len(out_refs), rows // len(out_refs), width)
        for k, out_ref in enumerate(out_refs):
            out_ref[first : first + size] = result[:, k]
        first += size


def projected(lane, heads, gates, w_out, labels, sg, query_rows):
    sizes = [x[0].shape[0] for x in heads]
    _, rows, _ = heads[0][0].shape
    width = w_out.shape[1]
    vmem = pl.BlockSpec(memory_space=pltpu.VMEM)
    flat = [x for chunk in heads for x in chunk]
    return pl.pallas_call(
        functools.partial(project_kernel, labels, sizes),
        in_specs=[pl.BlockSpec(memory_space=pltpu.SMEM)] + [vmem] * (len(flat) + len(gates) + 1),
        out_specs=[vmem] * sg,
        out_shape=[jax.ShapeDtypeStruct((sum(sizes), query_rows, width), BF16)] * sg,
        scratch_shapes=[pltpu.VMEM((max(sizes) * rows, width), F32)],
        cost_estimate=pl.CostEstimate(
            flops=2 * sum(sizes) * rows * width * width, bytes_accessed=2 * width * width, transcendentals=0
        ),
        compiler_params=pltpu.CompilerParams(vmem_limit_bytes=12 * MIB),
        name="project",
    )(lane.reshape(1), *flat, *gates, w_out)


def assemble_kernel(sg, firsts, group_ref, *refs):
    out_ref = refs[-1]
    group = group_ref[0]
    for i, ref in enumerate(refs[:-1]):
        first, k = firsts[i // sg], i % sg
        out_ref[group ^ k, first : first + ref.shape[0]] = ref[...]


def assembled(group, parts, firsts, shape):
    vmem = pl.BlockSpec(memory_space=pltpu.VMEM)
    return pl.pallas_call(
        functools.partial(assemble_kernel, shape[0], firsts),
        in_specs=[pl.BlockSpec(memory_space=pltpu.SMEM)] + [vmem] * len(parts),
        out_specs=vmem,
        out_shape=jax.ShapeDtypeStruct(shape, BF16),
        compiler_params=pltpu.CompilerParams(vmem_limit_bytes=8 * MIB),
        name="assemble",
    )(group.reshape(1), *parts)


def head_groups(n, samples):
    hg = 1
    while hg * hg < n or H % hg or samples % (n // hg):
        hg *= 2
    return hg


def chunk_sizes(group_samples):
    last = max(group_samples // 6, 1)
    middle = max(group_samples // 3, 1)
    return [group_samples - middle - last, middle, last]


def local(
    query_tokens,
    key_tokens,
    pair,
    key_mask,
    span_owner,
    pair_gain,
    pair_proj,
    w_query,
    w_key,
    w_value,
    w_gate,
    w_out,
):
    n = lax.axis_size("key")
    samples, query_rows, width = query_tokens.shape
    keys = key_tokens.shape[1]
    window = pair.shape[0]
    hg = head_groups(n, samples)
    sg = n // hg
    hpg = H // hg
    feats = width // hg
    group_samples = samples // sg
    sizes = chunk_sizes(group_samples)
    firsts = [sum(sizes[:c]) for c in range(len(sizes))]
    direct = query_rows % 16 == 0
    me = lax.axis_index("key")
    group, lane = me // hg, me % hg

    def across(x, code):
        if code == 0:
            return x
        return lax.ppermute(x, "key", [(i, i ^ code) for i in range(n)])

    labels = [0]
    bit = hg // 2
    while bit:
        labels = labels + [m ^ bit for m in labels]
        bit //= 2
    codes = [k * hg + m for m in labels for k in range(sg)]
    code_list = jnp.array(codes, jnp.int32)
    slot_of = [0] * n
    for p, code in enumerate(codes):
        slot_of[code] = p

    key_groups = key_tokens.reshape(sg, group_samples, keys, width)
    query_groups = query_tokens.reshape(sg, group_samples, query_rows, width)

    packed = pack(group, key_groups, query_groups, 0, sizes[:1])
    packed = packed + pack(group, key_groups, query_groups, firsts[1], sizes[1:])
    got = [[across(x, k * hg) for k, x in enumerate(sent)] for sent in packed]

    relative = jnp.arange(hg) ^ lane
    proj_t = jnp.take(pair_proj.T.reshape(hg, hpg, -1), relative, axis=0).reshape(H, -1)
    pieces = local_bias(pair, key_mask, pair_gain, proj_t, hpg)
    pieces = [across(x, m) for m, x in enumerate(pieces)]
    parts = {0: stacked(pieces)}
    bit = sg // 2
    while bit:
        parts.update({k ^ bit: across(x, bit * hg) for k, x in parts.items()})
        bit //= 2
    if direct:
        each = query_rows // 16
        qsel = ((code_list ^ me)[:, None] * each + jnp.arange(each)).reshape(window // 16)
    else:
        qsel = jnp.arange(window // 16, dtype=jnp.int32)
    bias, mask = ordered_bias(
        [parts[k] for k in range(sg)], me, span_owner, qsel, hpg, keys, codes, window
    )

    def own(w):
        return lax.dynamic_slice_in_dim(w, lane * feats, feats, 1)

    wq, wk, wv = own(w_query), own(w_key), own(w_value)

    heads, gates = [], []
    previous = None
    for c, size in enumerate(sizes):
        arrays = [stacked(got[c])]
        bit = hg // 2
        while bit:
            arrays = arrays + [across(x, bit) for x in arrays]
            bit //= 2
        queries = None
        if not direct:
            order = jnp.array(slot_of, jnp.int32)[me ^ jnp.arange(n)]
            queries = jnp.concatenate([x[:, :, keys:] for x in arrays], axis=0)
            queries = jnp.swapaxes(jnp.take(queries, order, axis=0), 0, 1).reshape(size, window, width)
        if previous is not None:
            arrays, previous = lax.optimization_barrier((arrays, previous))
        results = attention(arrays, queries, bias, mask, wq, wk, wv, w_gate, hpg, keys, query_rows)
        results, gate = results[:-1], results[-1]
        previous = gate
        if not direct:
            blocks = jnp.take(results[0].reshape(size, n, query_rows, feats), code_list ^ me, axis=1)
            results = [
                blocks[:, i * sg : (i + 1) * sg].reshape(size, sg * query_rows, feats) for i in range(hg)
            ]
            tokens = jnp.swapaxes(arrays[0][:, :, keys:], 0, 1).reshape(size, sg * query_rows, width)
            gate = jax.nn.sigmoid(nn_dot(tokens, w_gate))
        heads.append([across(r, m) for r, m in zip(results, labels)])
        gates.append(gate)
    outs = []
    for span in (slice(0, 1), slice(1, len(sizes))):
        back = projected(lane, heads[span], gates[span], w_out, labels, sg, query_rows)
        outs.extend(across(x, k * hg) for k, x in enumerate(back))
    out = assembled(group, outs, [0, sizes[0]], (sg, group_samples, query_rows, width))
    return out.reshape(samples, query_rows, width)


def solution(mesh):
    return jax.shard_map(
        local,
        mesh=mesh,
        in_specs=(
            P("rep", "key", None),
            P("rep", "key", None),
            P("rep", "key", None),
            P(("rep", "key")),
            P("rep"),
            P(),
            P(),
            P(),
            P(),
            P(),
            P(),
            P(),
        ),
        out_specs=P("rep", "key", None),
        check_vma=False,
    )
```

```python
import functools
import math

import jax
import jax.numpy as jnp
from jax import lax
from jax.experimental import pallas as pl
from jax.experimental.pallas import tpu as pltpu
from jax.sharding import PartitionSpec as P


H = 16
LOG2E = 1.4426950408889634
NEG = -1e9
MIB = 1024 * 1024
F32 = jnp.float32
BF16 = jnp.bfloat16


def nt_dot(a, b):
    return lax.dot_general(a, b, (((1,), (1,)), ((), ())), preferred_element_type=F32)


def nn_dot(a, b):
    return jnp.dot(a, b, preferred_element_type=F32)


def bias_kernel(hpg, mask_ref, pair_ref, gain_ref, proj_ref, *out_refs):
    fold, rows, keys, c = pair_ref.shape
    heads = proj_ref.shape[0]
    step = pl.program_id(0)
    total_rows = (out_refs[0].shape[0] - 16) // hpg
    x = jnp.swapaxes(pair_ref[...], 0, 1).reshape(rows * fold * keys, c).astype(F32)
    center = x - jnp.mean(x, axis=-1, keepdims=True)
    spread = jnp.mean(center * center, axis=-1, keepdims=True)
    normed = (center * lax.rsqrt(spread + 1e-5) * gain_ref[...]).astype(BF16)
    bias = nt_dot(proj_ref[...], normed)
    bias = bias.reshape(heads, rows, fold * keys).astype(BF16)
    for h in range(heads):
        start = pl.multiple_of((h % hpg) * total_rows + step * rows, 16)
        out_refs[h // hpg][pl.ds(start, rows), :] = bias[h]

    @pl.when(step == 0)
    def _():
        row = jnp.broadcast_to(mask_ref[...], (16, fold * keys)).astype(BF16)
        for out_ref in out_refs:
            out_ref[hpg * total_rows :, :] = row


def local_bias(pair, key_mask, pair_gain, proj_t, hpg):
    window, keys, c = pair.shape
    heads = proj_t.shape[0]
    fold = 128 // keys
    rows = window // fold
    tile = 16
    mask = jnp.tile(key_mask.astype(F32), fold)[None]
    shape = (hpg * rows + 16, 128)
    return pl.pallas_call(
        functools.partial(bias_kernel, hpg),
        grid=(rows // tile,),
        in_specs=[
            pl.BlockSpec((1, 128), lambda i: (0, 0)),
            pl.BlockSpec((fold, tile, keys, c), lambda i: (0, i, 0, 0)),
            pl.BlockSpec((1, c), lambda i: (0, 0)),
            pl.BlockSpec((heads, c), lambda i: (0, 0)),
        ],
        out_specs=[pl.BlockSpec(shape, lambda i: (0, 0))] * (heads // hpg),
        out_shape=[jax.ShapeDtypeStruct(shape, BF16)] * (heads // hpg),
        cost_estimate=pl.CostEstimate(
            flops=2 * window * keys * c * 256, bytes_accessed=window * keys * c * 2, transcendentals=0
        ),
        compiler_params=pltpu.CompilerParams(vmem_limit_bytes=16 * MIB),
        name="bias_local",
    )(mask, pair.reshape(fold, rows, keys, c), pair_gain[None], proj_t)


def pack_kernel(sizes, count, group_ref, *refs):
    step = pl.program_id(0)
    start = 0
    for i, size in enumerate(sizes):

        @pl.when((step >= start) & (step < start + size))
        def _(i=i):
            for k in range(count):
                out_ref = refs[(2 + i) * count + k]
                keys = refs[k].shape[2]
                out_ref[0, :keys] = refs[k][0, 0]
                out_ref[0, keys:] = refs[count + k][0, 0]

        start += size


def pack(group, key_groups, query_groups, first, sizes, steps, limit):
    _, _, keys, width = key_groups.shape
    rows = query_groups.shape[2]
    total = sum(sizes)
    count = len(steps)

    def spec(length, k):
        return pl.BlockSpec((1, 1, length, width), lambda s, g: (g[0] ^ k, first + s, 0, 0))

    def out_spec(i):
        start = sum(sizes[:i])
        return pl.BlockSpec(
            (1, keys + rows, width), lambda s, g: (jnp.clip(s - start, 0, sizes[i] - 1), 0, 0)
        )

    outs = pl.pallas_call(
        functools.partial(pack_kernel, sizes, count),
        grid_spec=pltpu.PrefetchScalarGridSpec(
            num_scalar_prefetch=1,
            grid=(total,),
            in_specs=[spec(keys, k) for k in steps] + [spec(rows, k) for k in steps],
            out_specs=[out_spec(i) for i in range(len(sizes)) for _ in steps],
        ),
        out_shape=[jax.ShapeDtypeStruct((size, keys + rows, width), BF16) for size in sizes for _ in steps],
        cost_estimate=pl.CostEstimate(
            flops=0, bytes_accessed=4 * count * total * (keys + rows) * width, transcendentals=0
        ),
        compiler_params=pltpu.CompilerParams(vmem_limit_bytes=limit),
        name="pack",
    )(group.reshape(1), *([key_groups] * count), *([query_groups] * count))
    return [outs[i * count : (i + 1) * count] for i in range(len(sizes))]


def stack_kernel(*refs):
    for i, ref in enumerate(refs[:-1]):
        refs[-1][i] = ref[...]


def stacked(parts):
    count, shape = len(parts), parts[0].shape
    rest = (0,) * (len(shape) - 1)
    block = (1,) + shape[1:] if len(shape) == 3 else shape
    steps = shape[0] if len(shape) == 3 else 1
    return pl.pallas_call(
        stack_kernel,
        grid=(steps,),
        in_specs=[pl.BlockSpec(block, lambda s: (s,) + rest)] * count,
        out_specs=pl.BlockSpec((count,) + block, lambda s: (0, s) + rest),
        out_shape=jax.ShapeDtypeStruct((count,) + shape, BF16),
        cost_estimate=pl.CostEstimate(
            flops=0, bytes_accessed=4 * count * math.prod(shape), transcendentals=0
        ),
        compiler_params=pltpu.CompilerParams(vmem_limit_bytes=8 * MIB),
        name="stack",
    )(*parts)


def order_kernel(hpg, keys, codes, me_ref, owner_ref, qsel_ref, *refs):
    parts, (bias_ref, mask_ref, inv_ref, x_ref) = refs[:-4], refs[-4:]
    n = len(codes)
    each = n // len(parts)
    for k, part_ref in enumerate(parts):
        x_ref[k * each : (k + 1) * each] = part_ref[...]
    fold = 128 // keys
    me = me_ref[0]
    rows = (x_ref.shape[1] - 16) // hpg
    slots = bias_ref.shape[1] // 16
    for d in range(n):
        inv_ref[owner_ref[d]] = d
    lane = lax.broadcasted_iota(jnp.int32, (16, 128), 1) // keys

    def of_tile(t):
        stored = [inv_ref[me ^ codes[t * fold + f]] ^ me for f in range(fold)]
        masks = x_ref[codes[t * fold], hpg * rows : hpg * rows + 16, :].astype(F32)
        for f in range(1, fold):
            part = x_ref[codes[t * fold + f], hpg * rows : hpg * rows + 16, :].astype(F32)
            masks = jnp.where(lane == f, part, masks)
        mask_ref[:, t * 128 : (t + 1) * 128] = masks[:8]
        return stored, masks > 0

    tiles = [of_tile(t) for t in range(n // fold)]

    def query_slot(p, carry):
        a = qsel_ref[p]
        part = a // (rows // 16)
        row = a % (rows // 16) * 16
        out = pl.multiple_of(p * 16, 16)
        for h in range(hpg):
            start = pl.multiple_of(h * rows + row, 16)
            for t, (stored, present) in enumerate(tiles):
                value = None
                for f in range(fold):
                    block = x_ref[stored[f], pl.ds(start, 16), :].astype(F32)
                    if fold == 2:
                        block = jnp.where(part == f, block, pltpu.roll(block, keys, 1))
                    value = block if value is None else jnp.where(lane == f, block, value)
                value = jnp.where(present, value * LOG2E, NEG * LOG2E)
                bias_ref[h, pl.ds(out, 16), t * 128 : (t + 1) * 128] = value
        return carry

    lax.fori_loop(0, slots, query_slot, 0)


def ordered_bias(parts, me, span_owner, qsel, hpg, keys, codes, window):
    n = len(codes)
    limit = (40 if n * keys > 2048 else 14) * MIB
    smem = pl.BlockSpec(memory_space=pltpu.SMEM)
    vmem = pl.BlockSpec(memory_space=pltpu.VMEM)
    return pl.pallas_call(
        functools.partial(order_kernel, hpg, keys, codes),
        in_specs=[smem, smem, smem] + [vmem] * len(parts),
        out_specs=[vmem, vmem],
        out_shape=[
            jax.ShapeDtypeStruct((hpg, window, n * keys), F32),
            jax.ShapeDtypeStruct((8, n * keys), F32),
        ],
        scratch_shapes=[
            pltpu.SMEM((n,), jnp.int32),
            pltpu.VMEM((n,) + parts[0].shape[1:], BF16),
        ],
        cost_estimate=pl.CostEstimate(
            flops=hpg * window * n * keys * 8, bytes_accessed=hpg * window * n * keys * 6, transcendentals=0
        ),
        compiler_params=pltpu.CompilerParams(vmem_limit_bytes=limit),
        name="bias_order",
    )(me.reshape(1), span_owner, qsel, *parts)


def attention_kernel(pieces, hpg, direct, keys, *refs):
    own_refs, far_refs, refs = refs[:pieces], refs[pieces : 2 * pieces], refs[2 * pieces :]
    if not direct:
        query_ref, refs = refs[0], refs[1:]
    count = pieces if direct else 1
    bias_ref, mask_ref, wq_ref, wk_ref, wv_ref, wg_ref = refs[:6]
    out_refs, gate_ref = refs[6 : 6 + count], refs[6 + count]
    q_ref, k_ref, v_ref = refs[7 + count :]
    total_rows, width = own_refs[0].shape[1:]
    feats = wq_ref.shape[1]
    head_size = feats // hpg
    scale = LOG2E / math.sqrt(head_size)

    def own_rows(start, stop):
        return jnp.concatenate([ref[0, start:stop] for ref in own_refs], axis=0)

    def far_rows(ref, start, stop):
        block = ref[:, 0, start:stop]
        return block.reshape(block.shape[0] * block.shape[1], width)

    at = 0
    for m in range(-1, pieces):
        block = own_rows(0, keys) if m < 0 else far_rows(far_refs[m], 0, keys)
        span = slice(at, at + block.shape[0])
        k_t = nn_dot(block, wk_ref[...]).T
        k_ref[:, span] = jnp.where(mask_ref[:1, span] > 0, k_t, 0.0).astype(BF16)
        v_ref[span, :] = nn_dot(block, wv_ref[...]).astype(BF16)
        at += block.shape[0]
    if direct:
        at = 0
        for m in range(-1, pieces):
            block = own_rows(keys, total_rows) if m < 0 else far_rows(far_refs[m], keys, total_rows)
            q_ref[at : at + block.shape[0], :] = nn_dot(block, wq_ref[...]).astype(BF16)
            at += block.shape[0]
        block = jnp.concatenate([own_refs[0][0, keys:], far_rows(far_refs[0], keys, total_rows)], axis=0)
        gate_ref[0] = jax.nn.sigmoid(nn_dot(block, wg_ref[...]))
    else:
        q_ref[...] = nn_dot(query_ref[0], wq_ref[...]).astype(BF16)
        gate_ref[...] = jnp.zeros_like(gate_ref)
    q = q_ref[...]
    owner = lax.broadcasted_iota(jnp.int32, q.shape, 1) // head_size
    total = None
    for h in range(hpg):
        mine = owner == h
        scores = nn_dot(jnp.where(mine, q, jnp.zeros_like(q)), k_ref[...])
        scores = scores * scale + bias_ref[h]
        weights = jnp.exp2(scores - jnp.max(scores, axis=-1, keepdims=True))
        norm = 1.0 / jnp.sum(weights, axis=-1, keepdims=True)
        result = nn_dot((weights * norm).astype(BF16), v_ref[...])
        total = result if total is None else jnp.where(mine, result, total)
    total = total.astype(BF16)
    if not direct:
        out_refs[0][0] = total
        return
    own = total_rows - keys
    far = out_refs[0].shape[1] - own
    for m, out_ref in enumerate(out_refs):
        out_ref[0, :own] = total[m * own : (m + 1) * own]
        out_ref[0, own:] = total[pieces * own + m * far : pieces * own + (m + 1) * far]


def attention(first, own, far, queries, bias, mask, wq, wk, wv, w_gate, hpg, keys, query_rows):
    pieces = len(far)
    others, size, rows, width = far[0].shape
    window = bias.shape[1]
    tokens = bias.shape[2]
    feats = wq.shape[1]
    direct = queries is None
    whole = pl.BlockSpec(memory_space=pltpu.VMEM)
    specs = [pl.BlockSpec((1, rows, width), lambda s: (first + s, 0, 0))] * pieces
    specs += [pl.BlockSpec((others, 1, rows, width), lambda s: (0, s, 0, 0))] * pieces
    args = list(own) + list(far)
    gate_rows = (others + 1) * query_rows
    out_rows = [gate_rows] * pieces
    if not direct:
        specs.append(pl.BlockSpec((1, window, width), lambda s: (s, 0, 0)))
        args.append(queries)
        out_rows = [window]
    consts = [bias, mask, wq, wk, wv, w_gate]
    limit = (60 if tokens > 2048 else 26) * MIB
    flops = 2 * size * (tokens * width * feats * 2 + hpg * window * tokens * 512)
    return pl.pallas_call(
        functools.partial(attention_kernel, pieces, hpg, direct, keys),
        grid=(size,),
        in_specs=specs + [whole] * len(consts),
        out_specs=[pl.BlockSpec((1, r, feats), lambda s: (s, 0, 0)) for r in out_rows]
        + [pl.BlockSpec((1, gate_rows, width), lambda s: (s, 0, 0))],
        out_shape=[jax.ShapeDtypeStruct((size, r, feats), BF16) for r in out_rows]
        + [jax.ShapeDtypeStruct((size, gate_rows, width), F32)],
        scratch_shapes=[
            pltpu.VMEM((window, feats), BF16),
            pltpu.VMEM((feats, tokens), BF16),
            pltpu.VMEM((tokens, feats), BF16),
        ],
        cost_estimate=pl.CostEstimate(
            flops=flops,
            bytes_accessed=size * tokens * width * 2 + hpg * window * tokens * 4,
            transcendentals=size * hpg * window * tokens,
        ),
        compiler_params=pltpu.CompilerParams(vmem_limit_bytes=limit),
        name="attend",
    )(*args, *consts)


def project_kernel(labels, sizes, lane_ref, *refs):
    count = len(labels)
    chunks = len(sizes)
    head_refs, refs = refs[: count * chunks], refs[count * chunks :]
    gate_refs, w_ref, refs = refs[:chunks], refs[chunks], refs[chunks + 1 :]
    out_refs, joined_ref = refs[:-1], refs[-1]
    lane = lane_ref[0]
    width = w_ref.shape[1]
    first = 0
    for c, size in enumerate(sizes):
        parts = head_refs[c * count : (c + 1) * count]
        _, rows, feats = parts[0].shape
        values = [ref[...].astype(F32).reshape(size * rows, feats) for ref in parts]
        for g in range(count):
            value = values[0]
            for label, other in zip(labels[1:], values[1:]):
                value = jnp.where(lane == g ^ label, other, value)
            joined_ref[: size * rows, g * feats : (g + 1) * feats] = value
        gate = gate_refs[c][...].reshape(size * rows, width)
        gated = (gate * joined_ref[: size * rows]).astype(BF16)
        result = nn_dot(gated, w_ref[...]).astype(BF16)
        result = result.reshape(size, len(out_refs), rows // len(out_refs), width)
        for k, out_ref in enumerate(out_refs):
            out_ref[first : first + size] = result[:, k]
        first += size


def projected(lane, heads, gates, w_out, labels, sg, query_rows):
    sizes = [x[0].shape[0] for x in heads]
    _, rows, _ = heads[0][0].shape
    width = w_out.shape[1]
    vmem = pl.BlockSpec(memory_space=pltpu.VMEM)
    flat = [x for chunk in heads for x in chunk]
    return pl.pallas_call(
        functools.partial(project_kernel, labels, sizes),
        in_specs=[pl.BlockSpec(memory_space=pltpu.SMEM)] + [vmem] * (len(flat) + len(gates) + 1),
        out_specs=[vmem] * sg,
        out_shape=[jax.ShapeDtypeStruct((sum(sizes), query_rows, width), BF16)] * sg,
        scratch_shapes=[pltpu.VMEM((max(sizes) * rows, width), F32)],
        cost_estimate=pl.CostEstimate(
            flops=2 * sum(sizes) * rows * width * width, bytes_accessed=2 * width * width, transcendentals=0
        ),
        compiler_params=pltpu.CompilerParams(vmem_limit_bytes=12 * MIB),
        name="project",
    )(lane.reshape(1), *flat, *gates, w_out)


def assemble_kernel(sg, firsts, group_ref, *refs):
    out_ref = refs[-1]
    group = group_ref[0]
    for i, ref in enumerate(refs[:-1]):
        first, k = firsts[i // sg], i % sg
        out_ref[group ^ k, first : first + ref.shape[0]] = ref[...]


def assembled(group, parts, firsts, shape):
    vmem = pl.BlockSpec(memory_space=pltpu.VMEM)
    return pl.pallas_call(
        functools.partial(assemble_kernel, shape[0], firsts),
        in_specs=[pl.BlockSpec(memory_space=pltpu.SMEM)] + [vmem] * len(parts),
        out_specs=vmem,
        out_shape=jax.ShapeDtypeStruct(shape, BF16),
        compiler_params=pltpu.CompilerParams(vmem_limit_bytes=8 * MIB),
        name="assemble",
    )(group.reshape(1), *parts)


def head_groups(n, samples):
    hg = 1
    while hg * hg < n or H % hg or samples % (n // hg):
        hg *= 2
    return hg


def chunk_sizes(group_samples):
    last = max(group_samples // 6, 1)
    middle = max(group_samples // 3, 1)
    return [group_samples - middle - last, middle, last]


def local(
    query_tokens,
    key_tokens,
    pair,
    key_mask,
    span_owner,
    pair_gain,
    pair_proj,
    w_query,
    w_key,
    w_value,
    w_gate,
    w_out,
):
    n = lax.axis_size("key")
    samples, query_rows, width = query_tokens.shape
    keys = key_tokens.shape[1]
    window = pair.shape[0]
    hg = head_groups(n, samples)
    sg = n // hg
    hpg = H // hg
    feats = width // hg
    group_samples = samples // sg
    sizes = chunk_sizes(group_samples)
    firsts = [sum(sizes[:c]) for c in range(len(sizes))]
    direct = query_rows % 16 == 0
    me = lax.axis_index("key")
    group, lane = me // hg, me % hg

    def across(x, code):
        if code == 0:
            return x
        return lax.ppermute(x, "key", [(i, i ^ code) for i in range(n)])

    labels = [0]
    bit = hg // 2
    while bit:
        labels = labels + [m ^ bit for m in labels]
        bit //= 2
    codes = labels + [k * hg + m for m in labels for k in range(1, sg)]
    code_list = jnp.array(codes, jnp.int32)
    slot_of = [0] * n
    for p, code in enumerate(codes):
        slot_of[code] = p

    key_groups = key_tokens.reshape(sg, group_samples, keys, width)
    query_groups = query_tokens.reshape(sg, group_samples, query_rows, width)

    others = range(1, sg)
    packed = pack(group, key_groups, query_groups, 0, sizes[:1], others, 56 * MIB)
    own_tokens = pack(group, key_groups, query_groups, 0, [group_samples], [0], 8 * MIB)[0]
    packed = packed + pack(group, key_groups, query_groups, firsts[1], sizes[1:], others, 12 * MIB)
    got = [[across(x, k * hg) for k, x in zip(others, sent)] for sent in packed]

    def over_lanes(arrays):
        bit = hg // 2
        while bit:
            arrays = arrays + [across(x, bit) for x in arrays]
            bit //= 2
        return arrays

    own_tokens = over_lanes(list(own_tokens))

    relative = jnp.arange(hg) ^ lane
    proj_t = jnp.take(pair_proj.T.reshape(hg, hpg, -1), relative, axis=0).reshape(H, -1)
    pieces = local_bias(pair, key_mask, pair_gain, proj_t, hpg)
    pieces = [across(x, m) for m, x in enumerate(pieces)]
    parts = {0: stacked(pieces)}
    bit = sg // 2
    while bit:
        parts.update({k ^ bit: across(x, bit * hg) for k, x in parts.items()})
        bit //= 2
    if direct:
        each = query_rows // 16
        qsel = ((code_list ^ me)[:, None] * each + jnp.arange(each)).reshape(window // 16)
    else:
        qsel = jnp.arange(window // 16, dtype=jnp.int32)
    bias, mask = ordered_bias(
        [parts[k] for k in range(sg)], me, span_owner, qsel, hpg, keys, codes, window
    )

    def own(w):
        return lax.dynamic_slice_in_dim(w, lane * feats, feats, 1)

    wq, wk, wv = own(w_query), own(w_key), own(w_value)

    heads, gates = [], []
    previous = None
    for c, size in enumerate(sizes):
        far = [stacked(got[c])]
        far = over_lanes(far)
        queries = None
        if not direct:
            order = jnp.array(slot_of, jnp.int32)[me ^ jnp.arange(n)]
            mine = [x[None, firsts[c] : firsts[c] + size, keys:] for x in own_tokens]
            queries = jnp.concatenate(mine + [x[:, :, keys:] for x in far], axis=0)
            queries = jnp.swapaxes(jnp.take(queries, order, axis=0), 0, 1).reshape(size, window, width)
        if previous is not None:
            far, previous = lax.optimization_barrier((far, previous))
        results = attention(firsts[c], own_tokens, far, queries, bias, mask, wq, wk, wv, w_gate, hpg, keys, query_rows)
        results, gate = results[:-1], results[-1]
        previous = gate
        if not direct:
            blocks = jnp.take(results[0].reshape(size, n, query_rows, feats), code_list ^ me, axis=1)
            results = []
            for i in range(hg):
                start = hg + i * (sg - 1)
                part = jnp.concatenate([blocks[:, i : i + 1], blocks[:, start : start + sg - 1]], axis=1)
                results.append(part.reshape(size, sg * query_rows, feats))
            mine = own_tokens[0][None, firsts[c] : firsts[c] + size, keys:]
            tokens = jnp.concatenate([mine, far[0][:, :, keys:]], axis=0)
            tokens = jnp.swapaxes(tokens, 0, 1).reshape(size, sg * query_rows, width)
            gate = jax.nn.sigmoid(nn_dot(tokens, w_gate))
        heads.append([across(r, m) for r, m in zip(results, labels)])
        gates.append(gate)
    outs = []
    for span in (slice(0, 1), slice(1, len(sizes))):
        back = projected(lane, heads[span], gates[span], w_out, labels, sg, query_rows)
        outs.extend(across(x, k * hg) for k, x in enumerate(back))
    out = assembled(group, outs, [0, sizes[0]], (sg, group_samples, query_rows, width))
    return out.reshape(samples, query_rows, width)


def solution(mesh):
    return jax.shard_map(
        local,
        mesh=mesh,
        in_specs=(
            P("rep", "key", None),
            P("rep", "key", None),
            P("rep", "key", None),
            P(("rep", "key")),
            P("rep"),
            P(),
            P(),
            P(),
            P(),
            P(),
            P(),
            P(),
        ),
        out_specs=P("rep", "key", None),
        check_vma=False,
    )
```

```python
import functools
import math

import jax
import jax.numpy as jnp
from jax import lax
from jax.experimental import pallas as pl
from jax.experimental.pallas import tpu as pltpu
from jax.sharding import PartitionSpec as P


H = 16
LOG2E = 1.4426950408889634
NEG = -1e9
MIB = 1024 * 1024
F32 = jnp.float32
BF16 = jnp.bfloat16


def nt_dot(a, b):
    return lax.dot_general(a, b, (((1,), (1,)), ((), ())), preferred_element_type=F32)


def nn_dot(a, b):
    return jnp.dot(a, b, preferred_element_type=F32)


def bias_kernel(hpg, mask_ref, pair_ref, gain_ref, proj_ref, *out_refs):
    fold, rows, keys, c = pair_ref.shape
    heads = proj_ref.shape[0]
    step = pl.program_id(0)
    total_rows = (out_refs[0].shape[0] - 16) // hpg
    x = jnp.swapaxes(pair_ref[...], 0, 1).reshape(rows * fold * keys, c).astype(F32)
    center = x - jnp.mean(x, axis=-1, keepdims=True)
    spread = jnp.mean(center * center, axis=-1, keepdims=True)
    normed = (center * lax.rsqrt(spread + 1e-5) * gain_ref[...]).astype(BF16)
    bias = nt_dot(proj_ref[...], normed)
    bias = bias.reshape(heads, rows, fold * keys).astype(BF16)
    for h in range(heads):
        start = pl.multiple_of((h % hpg) * total_rows + step * rows, 16)
        out_refs[h // hpg][pl.ds(start, rows), :] = bias[h]

    @pl.when(step == 0)
    def _():
        row = jnp.broadcast_to(mask_ref[...], (16, fold * keys)).astype(BF16)
        for out_ref in out_refs:
            out_ref[hpg * total_rows :, :] = row


def local_bias(pair, key_mask, pair_gain, proj_t, hpg):
    window, keys, c = pair.shape
    heads = proj_t.shape[0]
    fold = 128 // keys
    rows = window // fold
    tile = 16
    mask = jnp.tile(key_mask.astype(F32), fold)[None]
    shape = (hpg * rows + 16, 128)
    return pl.pallas_call(
        functools.partial(bias_kernel, hpg),
        grid=(rows // tile,),
        in_specs=[
            pl.BlockSpec((1, 128), lambda i: (0, 0)),
            pl.BlockSpec((fold, tile, keys, c), lambda i: (0, i, 0, 0)),
            pl.BlockSpec((1, c), lambda i: (0, 0)),
            pl.BlockSpec((heads, c), lambda i: (0, 0)),
        ],
        out_specs=[pl.BlockSpec(shape, lambda i: (0, 0))] * (heads // hpg),
        out_shape=[jax.ShapeDtypeStruct(shape, BF16)] * (heads // hpg),
        cost_estimate=pl.CostEstimate(
            flops=2 * window * keys * c * 256, bytes_accessed=window * keys * c * 2, transcendentals=0
        ),
        compiler_params=pltpu.CompilerParams(vmem_limit_bytes=16 * MIB),
        name="bias_local",
    )(mask, pair.reshape(fold, rows, keys, c), pair_gain[None], proj_t)


def pack_kernel(sizes, count, group_ref, *refs):
    step = pl.program_id(0)
    start = 0
    for i, size in enumerate(sizes):

        @pl.when((step >= start) & (step < start + size))
        def _(i=i):
            for k in range(count):
                out_ref = refs[(2 + i) * count + k]
                keys = refs[k].shape[2]
                out_ref[0, :keys] = refs[k][0, 0]
                out_ref[0, keys:] = refs[count + k][0, 0]

        start += size


def pack(group, key_groups, query_groups, first, sizes, steps, limit):
    _, _, keys, width = key_groups.shape
    rows = query_groups.shape[2]
    total = sum(sizes)
    count = len(steps)

    def spec(length, k):
        return pl.BlockSpec((1, 1, length, width), lambda s, g: (g[0] ^ k, first + s, 0, 0))

    def out_spec(i):
        start = sum(sizes[:i])
        return pl.BlockSpec(
            (1, keys + rows, width), lambda s, g: (jnp.clip(s - start, 0, sizes[i] - 1), 0, 0)
        )

    outs = pl.pallas_call(
        functools.partial(pack_kernel, sizes, count),
        grid_spec=pltpu.PrefetchScalarGridSpec(
            num_scalar_prefetch=1,
            grid=(total,),
            in_specs=[spec(keys, k) for k in steps] + [spec(rows, k) for k in steps],
            out_specs=[out_spec(i) for i in range(len(sizes)) for _ in steps],
        ),
        out_shape=[jax.ShapeDtypeStruct((size, keys + rows, width), BF16) for size in sizes for _ in steps],
        cost_estimate=pl.CostEstimate(
            flops=0, bytes_accessed=4 * count * total * (keys + rows) * width, transcendentals=0
        ),
        compiler_params=pltpu.CompilerParams(vmem_limit_bytes=limit),
        name="pack",
    )(group.reshape(1), *([key_groups] * count), *([query_groups] * count))
    return [outs[i * count : (i + 1) * count] for i in range(len(sizes))]


def stack_kernel(*refs):
    for i, ref in enumerate(refs[:-1]):
        refs[-1][i] = ref[...]


def stacked(parts):
    count, shape = len(parts), parts[0].shape
    rest = (0,) * (len(shape) - 1)
    block = (1,) + shape[1:] if len(shape) == 3 else shape
    steps = shape[0] if len(shape) == 3 else 1
    return pl.pallas_call(
        stack_kernel,
        grid=(steps,),
        in_specs=[pl.BlockSpec(block, lambda s: (s,) + rest)] * count,
        out_specs=pl.BlockSpec((count,) + block, lambda s: (0, s) + rest),
        out_shape=jax.ShapeDtypeStruct((count,) + shape, BF16),
        cost_estimate=pl.CostEstimate(
            flops=0, bytes_accessed=4 * count * math.prod(shape), transcendentals=0
        ),
        compiler_params=pltpu.CompilerParams(vmem_limit_bytes=8 * MIB),
        name="stack",
    )(*parts)


def order_kernel(hpg, keys, codes, me_ref, owner_ref, qsel_ref, *refs):
    parts, (bias_ref, mask_ref, inv_ref, x_ref) = refs[:-4], refs[-4:]
    n = len(codes)
    each = n // len(parts)
    for k, part_ref in enumerate(parts):
        x_ref[k * each : (k + 1) * each] = part_ref[...]
    fold = 128 // keys
    me = me_ref[0]
    rows = (x_ref.shape[1] - 16) // hpg
    slots = bias_ref.shape[1] // 16
    for d in range(n):
        inv_ref[owner_ref[d]] = d
    lane = lax.broadcasted_iota(jnp.int32, (16, 128), 1) // keys

    def of_tile(t):
        stored = [inv_ref[me ^ codes[t * fold + f]] ^ me for f in range(fold)]
        masks = x_ref[codes[t * fold], hpg * rows : hpg * rows + 16, :].astype(F32)
        for f in range(1, fold):
            part = x_ref[codes[t * fold + f], hpg * rows : hpg * rows + 16, :].astype(F32)
            masks = jnp.where(lane == f, part, masks)
        mask_ref[:, t * 128 : (t + 1) * 128] = masks[:8]
        return stored, masks > 0

    tiles = [of_tile(t) for t in range(n // fold)]

    def query_slot(p, carry):
        a = qsel_ref[p]
        part = a // (rows // 16)
        row = a % (rows // 16) * 16
        out = pl.multiple_of(p * 16, 16)
        for h in range(hpg):
            start = pl.multiple_of(h * rows + row, 16)
            for t, (stored, present) in enumerate(tiles):
                value = None
                for f in range(fold):
                    block = x_ref[stored[f], pl.ds(start, 16), :].astype(F32)
                    if fold == 2:
                        block = jnp.where(part == f, block, pltpu.roll(block, keys, 1))
                    value = block if value is None else jnp.where(lane == f, block, value)
                value = jnp.where(present, value * LOG2E, NEG * LOG2E)
                bias_ref[h, pl.ds(out, 16), t * 128 : (t + 1) * 128] = value
        return carry

    lax.fori_loop(0, slots, query_slot, 0)


def ordered_bias(parts, me, span_owner, qsel, hpg, keys, codes, window):
    n = len(codes)
    limit = (40 if n * keys > 2048 else 14) * MIB
    smem = pl.BlockSpec(memory_space=pltpu.SMEM)
    vmem = pl.BlockSpec(memory_space=pltpu.VMEM)
    return pl.pallas_call(
        functools.partial(order_kernel, hpg, keys, codes),
        in_specs=[smem, smem, smem] + [vmem] * len(parts),
        out_specs=[vmem, vmem],
        out_shape=[
            jax.ShapeDtypeStruct((hpg, window, n * keys), F32),
            jax.ShapeDtypeStruct((8, n * keys), F32),
        ],
        scratch_shapes=[
            pltpu.SMEM((n,), jnp.int32),
            pltpu.VMEM((n,) + parts[0].shape[1:], BF16),
        ],
        cost_estimate=pl.CostEstimate(
            flops=hpg * window * n * keys * 8, bytes_accessed=hpg * window * n * keys * 6, transcendentals=0
        ),
        compiler_params=pltpu.CompilerParams(vmem_limit_bytes=limit),
        name="bias_order",
    )(me.reshape(1), span_owner, qsel, *parts)


def attention_kernel(pieces, hpg, direct, keys, *refs):
    own_refs, far_refs, refs = refs[:pieces], refs[pieces : 2 * pieces], refs[2 * pieces :]
    if not direct:
        query_ref, refs = refs[0], refs[1:]
    count = pieces if direct else 1
    bias_ref, mask_ref, wq_ref, wk_ref, wv_ref, wg_ref = refs[:6]
    out_refs, gate_ref = refs[6 : 6 + count], refs[6 + count]
    q_ref, k_ref, v_ref = refs[7 + count :]
    total_rows, width = own_refs[0].shape[1:]
    feats = wq_ref.shape[1]
    head_size = feats // hpg
    scale = LOG2E / math.sqrt(head_size)

    def own_rows(start, stop):
        return jnp.concatenate([ref[0, start:stop] for ref in own_refs], axis=0)

    def far_rows(ref, start, stop):
        block = ref[:, 0, start:stop]
        return block.reshape(block.shape[0] * block.shape[1], width)

    at = 0
    for m in range(-1, pieces):
        block = own_rows(0, keys) if m < 0 else far_rows(far_refs[m], 0, keys)
        span = slice(at, at + block.shape[0])
        k_t = nn_dot(block, wk_ref[...]).T
        k_ref[:, span] = jnp.where(mask_ref[:1, span] > 0, k_t, 0.0).astype(BF16)
        v_ref[span, :] = nn_dot(block, wv_ref[...]).astype(BF16)
        at += block.shape[0]
    if direct:
        at = 0
        for m in range(-1, pieces):
            block = own_rows(keys, total_rows) if m < 0 else far_rows(far_refs[m], keys, total_rows)
            q_ref[at : at + block.shape[0], :] = nn_dot(block, wq_ref[...]).astype(BF16)
            at += block.shape[0]
        block = jnp.concatenate([own_refs[0][0, keys:], far_rows(far_refs[0], keys, total_rows)], axis=0)
        gate_ref[0] = jax.nn.sigmoid(nn_dot(block, wg_ref[...]))
    else:
        q_ref[...] = nn_dot(query_ref[0], wq_ref[...]).astype(BF16)
        gate_ref[...] = jnp.zeros_like(gate_ref)
    q = q_ref[...]
    owner = lax.broadcasted_iota(jnp.int32, q.shape, 1) // head_size
    total = None
    for h in range(hpg):
        mine = owner == h
        scores = nn_dot(jnp.where(mine, q, jnp.zeros_like(q)), k_ref[...])
        scores = scores * scale + bias_ref[h]
        weights = jnp.exp2(scores - jnp.max(scores, axis=-1, keepdims=True))
        norm = 1.0 / jnp.sum(weights, axis=-1, keepdims=True)
        result = nn_dot((weights * norm).astype(BF16), v_ref[...])
        total = result if total is None else jnp.where(mine, result, total)
    total = total.astype(BF16)
    if not direct:
        out_refs[0][0] = total
        return
    own = total_rows - keys
    far = out_refs[0].shape[1] - own
    for m, out_ref in enumerate(out_refs):
        out_ref[0, :own] = total[m * own : (m + 1) * own]
        out_ref[0, own:] = total[pieces * own + m * far : pieces * own + (m + 1) * far]


def attention(first, own, far, queries, bias, mask, wq, wk, wv, w_gate, hpg, keys, query_rows):
    pieces = len(far)
    others, size, rows, width = far[0].shape
    window = bias.shape[1]
    tokens = bias.shape[2]
    feats = wq.shape[1]
    direct = queries is None
    whole = pl.BlockSpec(memory_space=pltpu.VMEM)
    specs = [pl.BlockSpec((1, rows, width), lambda s: (first + s, 0, 0))] * pieces
    specs += [pl.BlockSpec((others, 1, rows, width), lambda s: (0, s, 0, 0))] * pieces
    args = list(own) + list(far)
    gate_rows = (others + 1) * query_rows
    out_rows = [gate_rows] * pieces
    if not direct:
        specs.append(pl.BlockSpec((1, window, width), lambda s: (s, 0, 0)))
        args.append(queries)
        out_rows = [window]
    consts = [bias, mask, wq, wk, wv, w_gate]
    limit = (60 if tokens > 2048 else 26) * MIB
    flops = 2 * size * (tokens * width * feats * 2 + hpg * window * tokens * 512)
    return pl.pallas_call(
        functools.partial(attention_kernel, pieces, hpg, direct, keys),
        grid=(size,),
        in_specs=specs + [whole] * len(consts),
        out_specs=[pl.BlockSpec((1, r, feats), lambda s: (s, 0, 0)) for r in out_rows]
        + [pl.BlockSpec((1, gate_rows, width), lambda s: (s, 0, 0))],
        out_shape=[jax.ShapeDtypeStruct((size, r, feats), BF16) for r in out_rows]
        + [jax.ShapeDtypeStruct((size, gate_rows, width), F32)],
        scratch_shapes=[
            pltpu.VMEM((window, feats), BF16),
            pltpu.VMEM((feats, tokens), BF16),
            pltpu.VMEM((tokens, feats), BF16),
        ],
        cost_estimate=pl.CostEstimate(
            flops=flops,
            bytes_accessed=size * tokens * width * 2 + hpg * window * tokens * 4,
            transcendentals=size * hpg * window * tokens,
        ),
        compiler_params=pltpu.CompilerParams(vmem_limit_bytes=limit),
        name="attend",
    )(*args, *consts)


def project_kernel(labels, sizes, lane_ref, *refs):
    count = len(labels)
    chunks = len(sizes)
    head_refs, refs = refs[: count * chunks], refs[count * chunks :]
    gate_refs, w_ref, refs = refs[:chunks], refs[chunks], refs[chunks + 1 :]
    out_refs, joined_ref = refs[:-1], refs[-1]
    lane = lane_ref[0]
    width = w_ref.shape[1]
    first = 0
    for c, size in enumerate(sizes):
        parts = head_refs[c * count : (c + 1) * count]
        _, rows, feats = parts[0].shape
        values = [ref[...].astype(F32).reshape(size * rows, feats) for ref in parts]
        for g in range(count):
            value = values[0]
            for label, other in zip(labels[1:], values[1:]):
                value = jnp.where(lane == g ^ label, other, value)
            joined_ref[: size * rows, g * feats : (g + 1) * feats] = value
        gate = gate_refs[c][...].reshape(size * rows, width)
        gated = (gate * joined_ref[: size * rows]).astype(BF16)
        result = nn_dot(gated, w_ref[...]).astype(BF16)
        result = result.reshape(size, len(out_refs), rows // len(out_refs), width)
        for k, out_ref in enumerate(out_refs):
            out_ref[first : first + size] = result[:, k]
        first += size


def projected(lane, heads, gates, w_out, labels, sg, query_rows):
    sizes = [x[0].shape[0] for x in heads]
    _, rows, _ = heads[0][0].shape
    width = w_out.shape[1]
    vmem = pl.BlockSpec(memory_space=pltpu.VMEM)
    flat = [x for chunk in heads for x in chunk]
    return pl.pallas_call(
        functools.partial(project_kernel, labels, sizes),
        in_specs=[pl.BlockSpec(memory_space=pltpu.SMEM)] + [vmem] * (len(flat) + len(gates) + 1),
        out_specs=[vmem] * sg,
        out_shape=[jax.ShapeDtypeStruct((sum(sizes), query_rows, width), BF16)] * sg,
        scratch_shapes=[pltpu.VMEM((max(sizes) * rows, width), F32)],
        cost_estimate=pl.CostEstimate(
            flops=2 * sum(sizes) * rows * width * width, bytes_accessed=2 * width * width, transcendentals=0
        ),
        compiler_params=pltpu.CompilerParams(vmem_limit_bytes=12 * MIB),
        name="project",
    )(lane.reshape(1), *flat, *gates, w_out)


def assemble_kernel(sg, firsts, group_ref, *refs):
    out_ref = refs[-1]
    group = group_ref[0]
    for i, ref in enumerate(refs[:-1]):
        first, k = firsts[i // sg], i % sg
        out_ref[group ^ k, first : first + ref.shape[0]] = ref[...]


def assembled(group, parts, firsts, shape):
    vmem = pl.BlockSpec(memory_space=pltpu.VMEM)
    return pl.pallas_call(
        functools.partial(assemble_kernel, shape[0], firsts),
        in_specs=[pl.BlockSpec(memory_space=pltpu.SMEM)] + [vmem] * len(parts),
        out_specs=vmem,
        out_shape=jax.ShapeDtypeStruct(shape, BF16),
        compiler_params=pltpu.CompilerParams(vmem_limit_bytes=8 * MIB),
        name="assemble",
    )(group.reshape(1), *parts)


def head_groups(n, samples):
    hg = 1
    while hg * hg < n or H % hg or samples % (n // hg):
        hg *= 2
    return hg


def chunk_sizes(group_samples):
    last = max(group_samples // 3, 1)
    return [group_samples - last, last]


def local(
    query_tokens,
    key_tokens,
    pair,
    key_mask,
    span_owner,
    pair_gain,
    pair_proj,
    w_query,
    w_key,
    w_value,
    w_gate,
    w_out,
):
    n = lax.axis_size("key")
    samples, query_rows, width = query_tokens.shape
    keys = key_tokens.shape[1]
    window = pair.shape[0]
    hg = head_groups(n, samples)
    sg = n // hg
    hpg = H // hg
    feats = width // hg
    group_samples = samples // sg
    sizes = chunk_sizes(group_samples)
    firsts = [sum(sizes[:c]) for c in range(len(sizes))]
    direct = query_rows % 16 == 0
    me = lax.axis_index("key")
    group, lane = me // hg, me % hg

    def across(x, code):
        if code == 0:
            return x
        return lax.ppermute(x, "key", [(i, i ^ code) for i in range(n)])

    labels = [0]
    bit = hg // 2
    while bit:
        labels = labels + [m ^ bit for m in labels]
        bit //= 2
    codes = labels + [k * hg + m for m in labels for k in range(1, sg)]
    code_list = jnp.array(codes, jnp.int32)
    slot_of = [0] * n
    for p, code in enumerate(codes):
        slot_of[code] = p

    key_groups = key_tokens.reshape(sg, group_samples, keys, width)
    query_groups = query_tokens.reshape(sg, group_samples, query_rows, width)

    others = range(1, sg)
    packed = pack(group, key_groups, query_groups, 0, sizes[:1], others, 56 * MIB)
    own_tokens = pack(group, key_groups, query_groups, 0, [group_samples], [0], 8 * MIB)[0]
    packed = packed + pack(group, key_groups, query_groups, firsts[1], sizes[1:], others, 12 * MIB)
    got = [[across(x, k * hg) for k, x in zip(others, sent)] for sent in packed]

    def over_lanes(arrays):
        bit = hg // 2
        while bit:
            arrays = arrays + [across(x, bit) for x in arrays]
            bit //= 2
        return arrays

    own_tokens = over_lanes(list(own_tokens))

    relative = jnp.arange(hg) ^ lane
    proj_t = jnp.take(pair_proj.T.reshape(hg, hpg, -1), relative, axis=0).reshape(H, -1)
    pieces = local_bias(pair, key_mask, pair_gain, proj_t, hpg)
    pieces = [across(x, m) for m, x in enumerate(pieces)]
    parts = {0: stacked(pieces)}
    bit = sg // 2
    while bit:
        parts.update({k ^ bit: across(x, bit * hg) for k, x in parts.items()})
        bit //= 2
    if direct:
        each = query_rows // 16
        qsel = ((code_list ^ me)[:, None] * each + jnp.arange(each)).reshape(window // 16)
    else:
        qsel = jnp.arange(window // 16, dtype=jnp.int32)
    bias, mask = ordered_bias(
        [parts[k] for k in range(sg)], me, span_owner, qsel, hpg, keys, codes, window
    )

    def own(w):
        return lax.dynamic_slice_in_dim(w, lane * feats, feats, 1)

    wq, wk, wv = own(w_query), own(w_key), own(w_value)

    heads, gates = [], []
    previous = None
    for c, size in enumerate(sizes):
        far = [stacked(got[c])]
        far = over_lanes(far)
        queries = None
        if not direct:
            order = jnp.array(slot_of, jnp.int32)[me ^ jnp.arange(n)]
            mine = [x[None, firsts[c] : firsts[c] + size, keys:] for x in own_tokens]
            queries = jnp.concatenate(mine + [x[:, :, keys:] for x in far], axis=0)
            queries = jnp.swapaxes(jnp.take(queries, order, axis=0), 0, 1).reshape(size, window, width)
        if previous is not None:
            far, previous = lax.optimization_barrier((far, previous))
        results = attention(firsts[c], own_tokens, far, queries, bias, mask, wq, wk, wv, w_gate, hpg, keys, query_rows)
        results, gate = results[:-1], results[-1]
        previous = gate
        if not direct:
            blocks = jnp.take(results[0].reshape(size, n, query_rows, feats), code_list ^ me, axis=1)
            results = []
            for i in range(hg):
                start = hg + i * (sg - 1)
                part = jnp.concatenate([blocks[:, i : i + 1], blocks[:, start : start + sg - 1]], axis=1)
                results.append(part.reshape(size, sg * query_rows, feats))
            mine = own_tokens[0][None, firsts[c] : firsts[c] + size, keys:]
            tokens = jnp.concatenate([mine, far[0][:, :, keys:]], axis=0)
            tokens = jnp.swapaxes(tokens, 0, 1).reshape(size, sg * query_rows, width)
            gate = jax.nn.sigmoid(nn_dot(tokens, w_gate))
        heads.append([across(r, m) for r, m in zip(results, labels)])
        gates.append(gate)
    outs = []
    for span in (slice(0, 1), slice(1, len(sizes))):
        back = projected(lane, heads[span], gates[span], w_out, labels, sg, query_rows)
        outs.extend(across(x, k * hg) for k, x in enumerate(back))
    out = assembled(group, outs, [0, sizes[0]], (sg, group_samples, query_rows, width))
    return out.reshape(samples, query_rows, width)


def solution(mesh):
    return jax.shard_map(
        local,
        mesh=mesh,
        in_specs=(
            P("rep", "key", None),
            P("rep", "key", None),
            P("rep", "key", None),
            P(("rep", "key")),
            P("rep"),
            P(),
            P(),
            P(),
            P(),
            P(),
            P(),
            P(),
        ),
        out_specs=P("rep", "key", None),
        check_vma=False,
    )
```

```python
import functools
import math

import jax
import jax.numpy as jnp
from jax import lax
from jax.experimental import pallas as pl
from jax.experimental.pallas import tpu as pltpu
from jax.sharding import PartitionSpec as P


H = 16
LOG2E = 1.4426950408889634
NEG = -1e9
MIB = 1024 * 1024
F32 = jnp.float32
BF16 = jnp.bfloat16


def nt_dot(a, b):
    return lax.dot_general(a, b, (((1,), (1,)), ((), ())), preferred_element_type=F32)


def nn_dot(a, b):
    return jnp.dot(a, b, preferred_element_type=F32)


def bias_kernel(hpg, mask_ref, pair_ref, gain_ref, proj_ref, *out_refs):
    fold, rows, keys, c = pair_ref.shape
    heads = proj_ref.shape[0]
    step = pl.program_id(0)
    total_rows = (out_refs[0].shape[0] - 16) // hpg
    x = jnp.swapaxes(pair_ref[...], 0, 1).reshape(rows * fold * keys, c).astype(F32)
    center = x - jnp.mean(x, axis=-1, keepdims=True)
    spread = jnp.mean(center * center, axis=-1, keepdims=True)
    normed = (center * lax.rsqrt(spread + 1e-5) * gain_ref[...]).astype(BF16)
    bias = nt_dot(proj_ref[...], normed)
    bias = bias.reshape(heads, rows, fold * keys).astype(BF16)
    for h in range(heads):
        start = pl.multiple_of((h % hpg) * total_rows + step * rows, 16)
        out_refs[h // hpg][pl.ds(start, rows), :] = bias[h]

    @pl.when(step == 0)
    def _():
        row = jnp.broadcast_to(mask_ref[...], (16, fold * keys)).astype(BF16)
        for out_ref in out_refs:
            out_ref[hpg * total_rows :, :] = row


def local_bias(pair, key_mask, pair_gain, proj_t, hpg):
    window, keys, c = pair.shape
    heads = proj_t.shape[0]
    fold = 128 // keys
    rows = window // fold
    tile = 16
    mask = jnp.tile(key_mask.astype(F32), fold)[None]
    shape = (hpg * rows + 16, 128)
    return pl.pallas_call(
        functools.partial(bias_kernel, hpg),
        grid=(rows // tile,),
        in_specs=[
            pl.BlockSpec((1, 128), lambda i: (0, 0)),
            pl.BlockSpec((fold, tile, keys, c), lambda i: (0, i, 0, 0)),
            pl.BlockSpec((1, c), lambda i: (0, 0)),
            pl.BlockSpec((heads, c), lambda i: (0, 0)),
        ],
        out_specs=[pl.BlockSpec(shape, lambda i: (0, 0))] * (heads // hpg),
        out_shape=[jax.ShapeDtypeStruct(shape, BF16)] * (heads // hpg),
        cost_estimate=pl.CostEstimate(
            flops=2 * window * keys * c * 256, bytes_accessed=window * keys * c * 2, transcendentals=0
        ),
        compiler_params=pltpu.CompilerParams(vmem_limit_bytes=16 * MIB),
        name="bias_local",
    )(mask, pair.reshape(fold, rows, keys, c), pair_gain[None], proj_t)


def pack_kernel(sizes, count, group_ref, *refs):
    step = pl.program_id(0)
    start = 0
    for i, size in enumerate(sizes):

        @pl.when((step >= start) & (step < start + size))
        def _(i=i):
            for k in range(count):
                out_ref = refs[(2 + i) * count + k]
                keys = refs[k].shape[2]
                out_ref[0, :keys] = refs[k][0, 0]
                out_ref[0, keys:] = refs[count + k][0, 0]

        start += size


def pack(group, key_groups, query_groups, first, sizes, steps, limit):
    _, _, keys, width = key_groups.shape
    rows = query_groups.shape[2]
    total = sum(sizes)
    count = len(steps)

    def spec(length, k):
        return pl.BlockSpec((1, 1, length, width), lambda s, g: (g[0] ^ k, first + s, 0, 0))

    def out_spec(i):
        start = sum(sizes[:i])
        return pl.BlockSpec(
            (1, keys + rows, width), lambda s, g: (jnp.clip(s - start, 0, sizes[i] - 1), 0, 0)
        )

    outs = pl.pallas_call(
        functools.partial(pack_kernel, sizes, count),
        grid_spec=pltpu.PrefetchScalarGridSpec(
            num_scalar_prefetch=1,
            grid=(total,),
            in_specs=[spec(keys, k) for k in steps] + [spec(rows, k) for k in steps],
            out_specs=[out_spec(i) for i in range(len(sizes)) for _ in steps],
        ),
        out_shape=[jax.ShapeDtypeStruct((size, keys + rows, width), BF16) for size in sizes for _ in steps],
        cost_estimate=pl.CostEstimate(
            flops=0, bytes_accessed=4 * count * total * (keys + rows) * width, transcendentals=0
        ),
        compiler_params=pltpu.CompilerParams(vmem_limit_bytes=limit),
        name="pack",
    )(group.reshape(1), *([key_groups] * count), *([query_groups] * count))
    return [outs[i * count : (i + 1) * count] for i in range(len(sizes))]


def stack_kernel(*refs):
    for i, ref in enumerate(refs[:-1]):
        refs[-1][i] = ref[...]


def stacked(parts):
    count, shape = len(parts), parts[0].shape
    rest = (0,) * (len(shape) - 1)
    block = (1,) + shape[1:] if len(shape) == 3 else shape
    steps = shape[0] if len(shape) == 3 else 1
    return pl.pallas_call(
        stack_kernel,
        grid=(steps,),
        in_specs=[pl.BlockSpec(block, lambda s: (s,) + rest)] * count,
        out_specs=pl.BlockSpec((count,) + block, lambda s: (0, s) + rest),
        out_shape=jax.ShapeDtypeStruct((count,) + shape, BF16),
        cost_estimate=pl.CostEstimate(
            flops=0, bytes_accessed=4 * count * math.prod(shape), transcendentals=0
        ),
        compiler_params=pltpu.CompilerParams(vmem_limit_bytes=8 * MIB),
        name="stack",
    )(*parts)


def order_kernel(hpg, keys, codes, me_ref, owner_ref, qsel_ref, *refs):
    parts, (bias_ref, mask_ref, inv_ref, x_ref) = refs[:-4], refs[-4:]
    n = len(codes)
    each = n // len(parts)
    for k, part_ref in enumerate(parts):
        x_ref[k * each : (k + 1) * each] = part_ref[...]
    fold = 128 // keys
    me = me_ref[0]
    rows = (x_ref.shape[1] - 16) // hpg
    slots = bias_ref.shape[1] // 16
    for d in range(n):
        inv_ref[owner_ref[d]] = d
    lane = lax.broadcasted_iota(jnp.int32, (16, 128), 1) // keys

    def of_tile(t):
        stored = [inv_ref[me ^ codes[t * fold + f]] ^ me for f in range(fold)]
        masks = x_ref[codes[t * fold], hpg * rows : hpg * rows + 16, :].astype(F32)
        for f in range(1, fold):
            part = x_ref[codes[t * fold + f], hpg * rows : hpg * rows + 16, :].astype(F32)
            masks = jnp.where(lane == f, part, masks)
        mask_ref[:, t * 128 : (t + 1) * 128] = masks[:8]
        return stored, masks > 0

    tiles = [of_tile(t) for t in range(n // fold)]

    def query_slot(p, carry):
        a = qsel_ref[p]
        part = a // (rows // 16)
        row = a % (rows // 16) * 16
        out = pl.multiple_of(p * 16, 16)
        for h in range(hpg):
            start = pl.multiple_of(h * rows + row, 16)
            for t, (stored, present) in enumerate(tiles):
                value = None
                for f in range(fold):
                    block = x_ref[stored[f], pl.ds(start, 16), :].astype(F32)
                    if fold == 2:
                        block = jnp.where(part == f, block, pltpu.roll(block, keys, 1))
                    value = block if value is None else jnp.where(lane == f, block, value)
                value = jnp.where(present, value * LOG2E, NEG * LOG2E)
                bias_ref[h, pl.ds(out, 16), t * 128 : (t + 1) * 128] = value
        return carry

    lax.fori_loop(0, slots, query_slot, 0)


def ordered_bias(parts, me, span_owner, qsel, hpg, keys, codes, window):
    n = len(codes)
    limit = (40 if n * keys > 2048 else 14) * MIB
    smem = pl.BlockSpec(memory_space=pltpu.SMEM)
    vmem = pl.BlockSpec(memory_space=pltpu.VMEM)
    return pl.pallas_call(
        functools.partial(order_kernel, hpg, keys, codes),
        in_specs=[smem, smem, smem] + [vmem] * len(parts),
        out_specs=[vmem, vmem],
        out_shape=[
            jax.ShapeDtypeStruct((hpg, window, n * keys), F32),
            jax.ShapeDtypeStruct((8, n * keys), F32),
        ],
        scratch_shapes=[
            pltpu.SMEM((n,), jnp.int32),
            pltpu.VMEM((n,) + parts[0].shape[1:], BF16),
        ],
        cost_estimate=pl.CostEstimate(
            flops=hpg * window * n * keys * 8, bytes_accessed=hpg * window * n * keys * 6, transcendentals=0
        ),
        compiler_params=pltpu.CompilerParams(vmem_limit_bytes=limit),
        name="bias_order",
    )(me.reshape(1), span_owner, qsel, *parts)


def heads_kernel(pieces, direct, keys, *refs):
    own_refs, far_refs, refs = refs[:pieces], refs[pieces : 2 * pieces], refs[2 * pieces :]
    if not direct:
        query_ref, refs = refs[0], refs[1:]
    wq_ref, wk_ref, wv_ref, wg_ref, q_ref, k_ref, v_ref, gate_ref = refs
    total_rows, width = own_refs[0].shape[1:]

    def own_rows(start, stop):
        return jnp.concatenate([ref[0, start:stop] for ref in own_refs], axis=0)

    def far_rows(ref, start, stop):
        block = ref[:, 0, start:stop]
        return block.reshape(block.shape[0] * block.shape[1], width)

    at = 0
    for m in range(-1, pieces):
        block = own_rows(0, keys) if m < 0 else far_rows(far_refs[m], 0, keys)
        span = slice(at, at + block.shape[0])
        k_ref[0, :, span] = nn_dot(block, wk_ref[...]).T.astype(BF16)
        v_ref[0, span, :] = nn_dot(block, wv_ref[...]).astype(BF16)
        at += block.shape[0]
    if direct:
        at = 0
        for m in range(-1, pieces):
            block = own_rows(keys, total_rows) if m < 0 else far_rows(far_refs[m], keys, total_rows)
            q_ref[0, at : at + block.shape[0], :] = nn_dot(block, wq_ref[...]).astype(BF16)
            at += block.shape[0]
        block = jnp.concatenate([own_refs[0][0, keys:], far_rows(far_refs[0], keys, total_rows)], axis=0)
        gate_ref[0] = jax.nn.sigmoid(nn_dot(block, wg_ref[...]))
    else:
        q_ref[0] = nn_dot(query_ref[0], wq_ref[...]).astype(BF16)
        gate_ref[...] = jnp.zeros_like(gate_ref)


def projections(first, own, far, queries, wq, wk, wv, w_gate, keys, query_rows, window, tokens):
    pieces = len(far)
    others, size, rows, width = far[0].shape
    feats = wq.shape[1]
    direct = queries is None
    whole = pl.BlockSpec(memory_space=pltpu.VMEM)
    specs = [pl.BlockSpec((1, rows, width), lambda s: (first + s, 0, 0))] * pieces
    specs += [pl.BlockSpec((others, 1, rows, width), lambda s: (0, s, 0, 0))] * pieces
    args = list(own) + list(far)
    gate_rows = (others + 1) * query_rows
    if not direct:
        specs.append(pl.BlockSpec((1, window, width), lambda s: (s, 0, 0)))
        args.append(queries)
    consts = [wq, wk, wv, w_gate]
    shapes = [(window, feats), (feats, tokens), (tokens, feats), (gate_rows, width)]
    return pl.pallas_call(
        functools.partial(heads_kernel, pieces, direct, keys),
        grid=(size,),
        in_specs=specs + [whole] * len(consts),
        out_specs=[pl.BlockSpec((1,) + x, lambda s: (s, 0, 0)) for x in shapes],
        out_shape=[
            jax.ShapeDtypeStruct((size,) + x, F32 if i == 3 else BF16) for i, x in enumerate(shapes)
        ],
        cost_estimate=pl.CostEstimate(
            flops=4 * size * tokens * width * feats, bytes_accessed=size * tokens * width * 3, transcendentals=0
        ),
        compiler_params=pltpu.CompilerParams(vmem_limit_bytes=(48 if tokens > 2048 else 16) * MIB),
        name="heads",
    )(*args, *consts)


def attention_kernel(hpg, splits, q_ref, k_ref, v_ref, bias_ref, mask_ref, *out_refs):
    q = q_ref[0]
    k = k_ref[0] * mask_ref[:1].astype(BF16)
    head_size = q.shape[1] // hpg
    scale = LOG2E / math.sqrt(head_size)
    owner = lax.broadcasted_iota(jnp.int32, q.shape, 1) // head_size
    total = None
    for h in range(hpg):
        mine = owner == h
        scores = nn_dot(jnp.where(mine, q, jnp.zeros_like(q)), k)
        scores = scores * scale + bias_ref[h]
        weights = jnp.exp2(scores - jnp.max(scores, axis=-1, keepdims=True))
        norm = 1.0 / jnp.sum(weights, axis=-1, keepdims=True)
        result = nn_dot((weights * norm).astype(BF16), v_ref[0])
        total = result if total is None else jnp.where(mine, result, total)
    total = total.astype(BF16)
    if splits is None:
        out_refs[0][0] = total
        return
    own, far = splits
    pieces = len(out_refs)
    for m, out_ref in enumerate(out_refs):
        out_ref[0, :own] = total[m * own : (m + 1) * own]
        out_ref[0, own:] = total[pieces * own + m * far : pieces * own + (m + 1) * far]


def attention(q, k, v, bias, mask, hpg, splits, pieces):
    size, window, feats = q.shape
    tokens = k.shape[2]
    out_rows = [window] if splits is None else [sum(splits)] * pieces
    return pl.pallas_call(
        functools.partial(attention_kernel, hpg, splits),
        grid=(size,),
        in_specs=[pl.BlockSpec((1,) + x.shape[1:], lambda s: (s, 0, 0)) for x in (q, k, v)]
        + [pl.BlockSpec(memory_space=pltpu.VMEM)] * 2,
        out_specs=[pl.BlockSpec((1, r, feats), lambda s: (s, 0, 0)) for r in out_rows],
        out_shape=[jax.ShapeDtypeStruct((size, r, feats), BF16) for r in out_rows],
        cost_estimate=pl.CostEstimate(
            flops=2 * size * hpg * window * tokens * 512,
            bytes_accessed=size * tokens * feats * 4 + hpg * window * tokens * 4,
            transcendentals=size * hpg * window * tokens,
        ),
        compiler_params=pltpu.CompilerParams(vmem_limit_bytes=(58 if tokens > 2048 else 20) * MIB),
        name="attend",
    )(q, k, v, bias, mask)


def project_kernel(labels, sizes, lane_ref, *refs):
    count = len(labels)
    chunks = len(sizes)
    head_refs, refs = refs[: count * chunks], refs[count * chunks :]
    gate_refs, w_ref, refs = refs[:chunks], refs[chunks], refs[chunks + 1 :]
    out_refs, joined_ref = refs[:-1], refs[-1]
    lane = lane_ref[0]
    width = w_ref.shape[1]
    first = 0
    for c, size in enumerate(sizes):
        parts = head_refs[c * count : (c + 1) * count]
        _, rows, feats = parts[0].shape
        values = [ref[...].astype(F32).reshape(size * rows, feats) for ref in parts]
        for g in range(count):
            value = values[0]
            for label, other in zip(labels[1:], values[1:]):
                value = jnp.where(lane == g ^ label, other, value)
            joined_ref[: size * rows, g * feats : (g + 1) * feats] = value
        gate = gate_refs[c][...].reshape(size * rows, width)
        gated = (gate * joined_ref[: size * rows]).astype(BF16)
        result = nn_dot(gated, w_ref[...]).astype(BF16)
        result = result.reshape(size, len(out_refs), rows // len(out_refs), width)
        for k, out_ref in enumerate(out_refs):
            out_ref[first : first + size] = result[:, k]
        first += size


def projected(lane, heads, gates, w_out, labels, sg, query_rows):
    sizes = [x[0].shape[0] for x in heads]
    _, rows, _ = heads[0][0].shape
    width = w_out.shape[1]
    vmem = pl.BlockSpec(memory_space=pltpu.VMEM)
    flat = [x for chunk in heads for x in chunk]
    return pl.pallas_call(
        functools.partial(project_kernel, labels, sizes),
        in_specs=[pl.BlockSpec(memory_space=pltpu.SMEM)] + [vmem] * (len(flat) + len(gates) + 1),
        out_specs=[vmem] * sg,
        out_shape=[jax.ShapeDtypeStruct((sum(sizes), query_rows, width), BF16)] * sg,
        scratch_shapes=[pltpu.VMEM((max(sizes) * rows, width), F32)],
        cost_estimate=pl.CostEstimate(
            flops=2 * sum(sizes) * rows * width * width, bytes_accessed=2 * width * width, transcendentals=0
        ),
        compiler_params=pltpu.CompilerParams(vmem_limit_bytes=12 * MIB),
        name="project",
    )(lane.reshape(1), *flat, *gates, w_out)


def assemble_kernel(sg, firsts, group_ref, *refs):
    out_ref = refs[-1]
    group = group_ref[0]
    for i, ref in enumerate(refs[:-1]):
        first, k = firsts[i // sg], i % sg
        out_ref[group ^ k, first : first + ref.shape[0]] = ref[...]


def assembled(group, parts, firsts, shape):
    vmem = pl.BlockSpec(memory_space=pltpu.VMEM)
    return pl.pallas_call(
        functools.partial(assemble_kernel, shape[0], firsts),
        in_specs=[pl.BlockSpec(memory_space=pltpu.SMEM)] + [vmem] * len(parts),
        out_specs=vmem,
        out_shape=jax.ShapeDtypeStruct(shape, BF16),
        compiler_params=pltpu.CompilerParams(vmem_limit_bytes=8 * MIB),
        name="assemble",
    )(group.reshape(1), *parts)


def head_groups(n, samples):
    hg = 1
    while hg * hg < n or H % hg or samples % (n // hg):
        hg *= 2
    return hg


def chunk_sizes(group_samples):
    last = max(group_samples // 3, 1)
    return [group_samples - last, last]


def local(
    query_tokens,
    key_tokens,
    pair,
    key_mask,
    span_owner,
    pair_gain,
    pair_proj,
    w_query,
    w_key,
    w_value,
    w_gate,
    w_out,
):
    n = lax.axis_size("key")
    samples, query_rows, width = query_tokens.shape
    keys = key_tokens.shape[1]
    window = pair.shape[0]
    hg = head_groups(n, samples)
    sg = n // hg
    hpg = H // hg
    feats = width // hg
    group_samples = samples // sg
    sizes = chunk_sizes(group_samples)
    firsts = [sum(sizes[:c]) for c in range(len(sizes))]
    direct = query_rows % 16 == 0
    me = lax.axis_index("key")
    group, lane = me // hg, me % hg

    def across(x, code):
        if code == 0:
            return x
        return lax.ppermute(x, "key", [(i, i ^ code) for i in range(n)])

    labels = [0]
    bit = hg // 2
    while bit:
        labels = labels + [m ^ bit for m in labels]
        bit //= 2
    codes = labels + [k * hg + m for m in labels for k in range(1, sg)]
    code_list = jnp.array(codes, jnp.int32)
    slot_of = [0] * n
    for p, code in enumerate(codes):
        slot_of[code] = p

    key_groups = key_tokens.reshape(sg, group_samples, keys, width)
    query_groups = query_tokens.reshape(sg, group_samples, query_rows, width)

    others = range(1, sg)
    packed = pack(group, key_groups, query_groups, 0, sizes[:1], others, 56 * MIB)
    own_tokens = pack(group, key_groups, query_groups, 0, [group_samples], [0], 8 * MIB)[0]
    packed = packed + pack(group, key_groups, query_groups, firsts[1], sizes[1:], others, 12 * MIB)
    got = [[across(x, k * hg) for k, x in zip(others, sent)] for sent in packed]

    def over_lanes(arrays):
        bit = hg // 2
        while bit:
            arrays = arrays + [across(x, bit) for x in arrays]
            bit //= 2
        return arrays

    own_tokens = over_lanes(list(own_tokens))

    relative = jnp.arange(hg) ^ lane
    proj_t = jnp.take(pair_proj.T.reshape(hg, hpg, -1), relative, axis=0).reshape(H, -1)
    pieces = local_bias(pair, key_mask, pair_gain, proj_t, hpg)
    pieces = [across(x, m) for m, x in enumerate(pieces)]
    parts = {0: stacked(pieces)}
    bit = sg // 2
    while bit:
        parts.update({k ^ bit: across(x, bit * hg) for k, x in parts.items()})
        bit //= 2
    if direct:
        each = query_rows // 16
        qsel = ((code_list ^ me)[:, None] * each + jnp.arange(each)).reshape(window // 16)
    else:
        qsel = jnp.arange(window // 16, dtype=jnp.int32)
    bias, mask = ordered_bias(
        [parts[k] for k in range(sg)], me, span_owner, qsel, hpg, keys, codes, window
    )

    def own(w):
        return lax.dynamic_slice_in_dim(w, lane * feats, feats, 1)

    wq, wk, wv = own(w_query), own(w_key), own(w_value)

    heads, gates = [], []
    for c, size in enumerate(sizes):
        far = [stacked(got[c])]
        far = over_lanes(far)
        queries = None
        if not direct:
            order = jnp.array(slot_of, jnp.int32)[me ^ jnp.arange(n)]
            mine = [x[None, firsts[c] : firsts[c] + size, keys:] for x in own_tokens]
            queries = jnp.concatenate(mine + [x[:, :, keys:] for x in far], axis=0)
            queries = jnp.swapaxes(jnp.take(queries, order, axis=0), 0, 1).reshape(size, window, width)
        if c:
            far, previous = lax.optimization_barrier((far, previous))
        q, k, v, gate = projections(
            firsts[c], own_tokens, far, queries, wq, wk, wv, w_gate, keys, query_rows, window, n * keys
        )
        splits = (query_rows, (sg - 1) * query_rows) if direct else None
        results = attention(q, k, v, bias, mask, hpg, splits, hg)
        previous = results[0]
        if not direct:
            blocks = jnp.take(results[0].reshape(size, n, query_rows, feats), code_list ^ me, axis=1)
            results = []
            for i in range(hg):
                start = hg + i * (sg - 1)
                part = jnp.concatenate([blocks[:, i : i + 1], blocks[:, start : start + sg - 1]], axis=1)
                results.append(part.reshape(size, sg * query_rows, feats))
            mine = own_tokens[0][None, firsts[c] : firsts[c] + size, keys:]
            tokens = jnp.concatenate([mine, far[0][:, :, keys:]], axis=0)
            tokens = jnp.swapaxes(tokens, 0, 1).reshape(size, sg * query_rows, width)
            gate = jax.nn.sigmoid(nn_dot(tokens, w_gate))
        heads.append([across(r, m) for r, m in zip(results, labels)])
        gates.append(gate)
    outs = []
    for span in (slice(0, 1), slice(1, len(sizes))):
        back = projected(lane, heads[span], gates[span], w_out, labels, sg, query_rows)
        outs.extend(across(x, k * hg) for k, x in enumerate(back))
    out = assembled(group, outs, [0, sizes[0]], (sg, group_samples, query_rows, width))
    return out.reshape(samples, query_rows, width)


def solution(mesh):
    return jax.shard_map(
        local,
        mesh=mesh,
        in_specs=(
            P("rep", "key", None),
            P("rep", "key", None),
            P("rep", "key", None),
            P(("rep", "key")),
            P("rep"),
            P(),
            P(),
            P(),
            P(),
            P(),
            P(),
            P(),
        ),
        out_specs=P("rep", "key", None),
        check_vma=False,
    )
```

```python
import functools
import math

import jax
import jax.numpy as jnp
from jax import lax
from jax.experimental import pallas as pl
from jax.experimental.pallas import tpu as pltpu
from jax.sharding import PartitionSpec as P


H = 16
LOG2E = 1.4426950408889634
NEG = -1e9
MIB = 1024 * 1024
F32 = jnp.float32
BF16 = jnp.bfloat16


def nt_dot(a, b):
    return lax.dot_general(a, b, (((1,), (1,)), ((), ())), preferred_element_type=F32)


def nn_dot(a, b):
    return jnp.dot(a, b, preferred_element_type=F32)


def bias_kernel(hpg, lane_ref, mask_ref, pair_ref, gain_ref, proj_ref, *out_refs):
    fold, rows, keys, c = pair_ref.shape
    groups = proj_ref.shape[0]
    heads = groups * hpg
    step = pl.program_id(0)
    proj = jnp.concatenate([proj_ref[lane_ref[0] ^ m] for m in range(groups)], axis=0).astype(BF16)
    total_rows = (out_refs[0].shape[0] - 16) // hpg
    x = jnp.swapaxes(pair_ref[...], 0, 1).reshape(rows * fold * keys, c).astype(F32)
    center = x - jnp.mean(x, axis=-1, keepdims=True)
    spread = jnp.mean(center * center, axis=-1, keepdims=True)
    normed = (center * lax.rsqrt(spread + 1e-5) * gain_ref[...]).astype(BF16)
    bias = nt_dot(proj, normed)
    bias = bias.reshape(heads, rows, fold * keys).astype(BF16)
    for h in range(heads):
        start = pl.multiple_of((h % hpg) * total_rows + step * rows, 16)
        out_refs[h // hpg][pl.ds(start, rows), :] = bias[h]

    @pl.when(step == 0)
    def _():
        row = jnp.concatenate([mask_ref[...].astype(F32)] * fold, axis=1)
        row = jnp.broadcast_to(row, (16, fold * keys)).astype(BF16)
        for out_ref in out_refs:
            out_ref[hpg * total_rows :, :] = row


def local_bias(lane, pair, key_mask, pair_gain, pair_proj, hpg):
    window, keys, c = pair.shape
    groups = pair_proj.shape[1] // hpg
    fold = 128 // keys
    rows = window // fold
    tile = 16
    proj = pair_proj.T.reshape(groups, hpg, c).astype(F32)
    shape = (hpg * rows + 16, 128)
    return pl.pallas_call(
        functools.partial(bias_kernel, hpg),
        grid=(rows // tile,),
        in_specs=[
            pl.BlockSpec(memory_space=pltpu.SMEM),
            pl.BlockSpec((1, keys), lambda i: (0, 0)),
            pl.BlockSpec((fold, tile, keys, c), lambda i: (0, i, 0, 0)),
            pl.BlockSpec((1, c), lambda i: (0, 0)),
            pl.BlockSpec((groups, hpg, c), lambda i: (0, 0, 0)),
        ],
        out_specs=[pl.BlockSpec(shape, lambda i: (0, 0))] * groups,
        out_shape=[jax.ShapeDtypeStruct(shape, BF16)] * groups,
        cost_estimate=pl.CostEstimate(
            flops=2 * window * keys * c * 256, bytes_accessed=window * keys * c * 2, transcendentals=0
        ),
        compiler_params=pltpu.CompilerParams(vmem_limit_bytes=56 * MIB),
        name="bias_local",
    )(lane.reshape(1), key_mask[None], pair.reshape(fold, rows, keys, c), pair_gain[None], proj)


def pack_kernel(sizes, count, group_ref, *refs):
    step = pl.program_id(0)
    start = 0
    for i, size in enumerate(sizes):

        @pl.when((step >= start) & (step < start + size))
        def _(i=i):
            for k in range(count):
                out_ref = refs[(2 + i) * count + k]
                keys = refs[k].shape[2]
                out_ref[0, :keys] = refs[k][0, 0]
                out_ref[0, keys:] = refs[count + k][0, 0]

        start += size


def pack(group, key_groups, query_groups, first, sizes, steps, limit):
    _, _, keys, width = key_groups.shape
    rows = query_groups.shape[2]
    total = sum(sizes)
    count = len(steps)

    def spec(length, k):
        return pl.BlockSpec((1, 1, length, width), lambda s, g: (g[0] ^ k, first + s, 0, 0))

    def out_spec(i):
        start = sum(sizes[:i])
        return pl.BlockSpec(
            (1, keys + rows, width), lambda s, g: (jnp.clip(s - start, 0, sizes[i] - 1), 0, 0)
        )

    outs = pl.pallas_call(
        functools.partial(pack_kernel, sizes, count),
        grid_spec=pltpu.PrefetchScalarGridSpec(
            num_scalar_prefetch=1,
            grid=(total,),
            in_specs=[spec(keys, k) for k in steps] + [spec(rows, k) for k in steps],
            out_specs=[out_spec(i) for i in range(len(sizes)) for _ in steps],
        ),
        out_shape=[jax.ShapeDtypeStruct((size, keys + rows, width), BF16) for size in sizes for _ in steps],
        cost_estimate=pl.CostEstimate(
            flops=0, bytes_accessed=4 * count * total * (keys + rows) * width, transcendentals=0
        ),
        compiler_params=pltpu.CompilerParams(vmem_limit_bytes=limit),
        name="pack",
    )(group.reshape(1), *([key_groups] * count), *([query_groups] * count))
    return [outs[i * count : (i + 1) * count] for i in range(len(sizes))]


def stack_kernel(*refs):
    for i, ref in enumerate(refs[:-1]):
        refs[-1][i] = ref[...]


def stacked(parts):
    count, shape = len(parts), parts[0].shape
    rest = (0,) * (len(shape) - 1)
    block = (1,) + shape[1:] if len(shape) == 3 else shape
    steps = shape[0] if len(shape) == 3 else 1
    return pl.pallas_call(
        stack_kernel,
        grid=(steps,),
        in_specs=[pl.BlockSpec(block, lambda s: (s,) + rest)] * count,
        out_specs=pl.BlockSpec((count,) + block, lambda s: (0, s) + rest),
        out_shape=jax.ShapeDtypeStruct((count,) + shape, BF16),
        cost_estimate=pl.CostEstimate(
            flops=0, bytes_accessed=4 * count * math.prod(shape), transcendentals=0
        ),
        compiler_params=pltpu.CompilerParams(vmem_limit_bytes=8 * MIB),
        name="stack",
    )(*parts)


def order_kernel(hpg, keys, codes, me_ref, owner_ref, qsel_ref, *refs):
    parts, (bias_ref, mask_ref, inv_ref, x_ref) = refs[:-4], refs[-4:]
    n = len(codes)
    each = n // len(parts)
    for k, part_ref in enumerate(parts):
        x_ref[k * each : (k + 1) * each] = part_ref[...]
    fold = 128 // keys
    me = me_ref[0]
    rows = (x_ref.shape[1] - 16) // hpg
    slots = bias_ref.shape[1] // 16
    for d in range(n):
        inv_ref[owner_ref[d]] = d
    lane = lax.broadcasted_iota(jnp.int32, (16, 128), 1) // keys

    def of_tile(t):
        stored = [inv_ref[me ^ codes[t * fold + f]] ^ me for f in range(fold)]
        masks = x_ref[codes[t * fold], hpg * rows : hpg * rows + 16, :].astype(F32)
        for f in range(1, fold):
            part = x_ref[codes[t * fold + f], hpg * rows : hpg * rows + 16, :].astype(F32)
            masks = jnp.where(lane == f, part, masks)
        mask_ref[:, t * 128 : (t + 1) * 128] = masks[:8]
        return stored, masks > 0

    tiles = [of_tile(t) for t in range(n // fold)]

    def query_slot(p, carry):
        a = qsel_ref[p]
        part = a // (rows // 16)
        row = a % (rows // 16) * 16
        out = pl.multiple_of(p * 16, 16)
        for h in range(hpg):
            start = pl.multiple_of(h * rows + row, 16)
            for t, (stored, present) in enumerate(tiles):
                value = None
                for f in range(fold):
                    block = x_ref[stored[f], pl.ds(start, 16), :].astype(F32)
                    if fold == 2:
                        block = jnp.where(part == f, block, pltpu.roll(block, keys, 1))
                    value = block if value is None else jnp.where(lane == f, block, value)
                value = jnp.where(present, value * LOG2E, NEG * LOG2E)
                bias_ref[h, pl.ds(out, 16), t * 128 : (t + 1) * 128] = value
        return carry

    lax.fori_loop(0, slots, query_slot, 0)


def ordered_bias(parts, me, span_owner, qsel, hpg, keys, codes, window):
    n = len(codes)
    limit = (40 if n * keys > 2048 else 14) * MIB
    smem = pl.BlockSpec(memory_space=pltpu.SMEM)
    vmem = pl.BlockSpec(memory_space=pltpu.VMEM)
    return pl.pallas_call(
        functools.partial(order_kernel, hpg, keys, codes),
        in_specs=[smem, smem, smem] + [vmem] * len(parts),
        out_specs=[vmem, vmem],
        out_shape=[
            jax.ShapeDtypeStruct((hpg, window, n * keys), F32),
            jax.ShapeDtypeStruct((8, n * keys), F32),
        ],
        scratch_shapes=[
            pltpu.SMEM((n,), jnp.int32),
            pltpu.VMEM((n,) + parts[0].shape[1:], BF16),
        ],
        cost_estimate=pl.CostEstimate(
            flops=hpg * window * n * keys * 8, bytes_accessed=hpg * window * n * keys * 6, transcendentals=0
        ),
        compiler_params=pltpu.CompilerParams(vmem_limit_bytes=limit),
        name="bias_order",
    )(me.reshape(1), span_owner, qsel, *parts)


def heads_kernel(pieces, direct, keys, *refs):
    own_refs, far_refs, refs = refs[:pieces], refs[pieces : 2 * pieces], refs[2 * pieces :]
    if not direct:
        query_ref, refs = refs[0], refs[1:]
    wq_ref, wk_ref, wv_ref, wg_ref, q_ref, k_ref, v_ref, gate_ref = refs
    total_rows, width = own_refs[0].shape[1:]

    def own_rows(start, stop):
        return jnp.concatenate([ref[0, start:stop] for ref in own_refs], axis=0)

    def far_rows(ref, start, stop):
        block = ref[:, 0, start:stop]
        return block.reshape(block.shape[0] * block.shape[1], width)

    at = 0
    for m in range(-1, pieces):
        block = own_rows(0, keys) if m < 0 else far_rows(far_refs[m], 0, keys)
        span = slice(at, at + block.shape[0])
        k_ref[0, :, span] = nn_dot(block, wk_ref[...]).T.astype(BF16)
        v_ref[0, span, :] = nn_dot(block, wv_ref[...]).astype(BF16)
        at += block.shape[0]
    if direct:
        at = 0
        for m in range(-1, pieces):
            block = own_rows(keys, total_rows) if m < 0 else far_rows(far_refs[m], keys, total_rows)
            q_ref[0, at : at + block.shape[0], :] = nn_dot(block, wq_ref[...]).astype(BF16)
            at += block.shape[0]
        block = jnp.concatenate([own_refs[0][0, keys:], far_rows(far_refs[0], keys, total_rows)], axis=0)
        gate_ref[0] = jax.nn.sigmoid(nn_dot(block, wg_ref[...]))
    else:
        q_ref[0] = nn_dot(query_ref[0], wq_ref[...]).astype(BF16)
        gate_ref[...] = jnp.zeros_like(gate_ref)


def projections(first, own, far, queries, wq, wk, wv, w_gate, keys, query_rows, window, tokens):
    pieces = len(far)
    others, size, rows, width = far[0].shape
    feats = wq.shape[1]
    direct = queries is None
    whole = pl.BlockSpec(memory_space=pltpu.VMEM)
    specs = [pl.BlockSpec((1, rows, width), lambda s: (first + s, 0, 0))] * pieces
    specs += [pl.BlockSpec((others, 1, rows, width), lambda s: (0, s, 0, 0))] * pieces
    args = list(own) + list(far)
    gate_rows = (others + 1) * query_rows
    if not direct:
        specs.append(pl.BlockSpec((1, window, width), lambda s: (s, 0, 0)))
        args.append(queries)
    consts = [wq, wk, wv, w_gate]
    shapes = [(window, feats), (feats, tokens), (tokens, feats), (gate_rows, width)]
    return pl.pallas_call(
        functools.partial(heads_kernel, pieces, direct, keys),
        grid=(size,),
        in_specs=specs + [whole] * len(consts),
        out_specs=[pl.BlockSpec((1,) + x, lambda s: (s, 0, 0)) for x in shapes],
        out_shape=[
            jax.ShapeDtypeStruct((size,) + x, F32 if i == 3 else BF16) for i, x in enumerate(shapes)
        ],
        cost_estimate=pl.CostEstimate(
            flops=4 * size * tokens * width * feats, bytes_accessed=size * tokens * width * 3, transcendentals=0
        ),
        compiler_params=pltpu.CompilerParams(vmem_limit_bytes=(48 if tokens > 2048 else 16) * MIB),
        name="heads",
    )(*args, *consts)


def attention_kernel(hpg, splits, q_ref, k_ref, v_ref, bias_ref, mask_ref, *out_refs):
    q = q_ref[0]
    k = k_ref[0] * mask_ref[:1].astype(BF16)
    head_size = q.shape[1] // hpg
    scale = LOG2E / math.sqrt(head_size)
    owner = lax.broadcasted_iota(jnp.int32, q.shape, 1) // head_size
    total = None
    for h in range(hpg):
        mine = owner == h
        scores = nn_dot(jnp.where(mine, q, jnp.zeros_like(q)), k)
        scores = scores * scale + bias_ref[h]
        weights = jnp.exp2(scores - jnp.max(scores, axis=-1, keepdims=True))
        norm = 1.0 / jnp.sum(weights, axis=-1, keepdims=True)
        result = nn_dot((weights * norm).astype(BF16), v_ref[0])
        total = result if total is None else jnp.where(mine, result, total)
    total = total.astype(BF16)
    if splits is None:
        out_refs[0][0] = total
        return
    own, far = splits
    pieces = len(out_refs)
    for m, out_ref in enumerate(out_refs):
        out_ref[0, :own] = total[m * own : (m + 1) * own]
        out_ref[0, own:] = total[pieces * own + m * far : pieces * own + (m + 1) * far]


def attention(q, k, v, bias, mask, hpg, splits, pieces):
    size, window, feats = q.shape
    tokens = k.shape[2]
    out_rows = [window] if splits is None else [sum(splits)] * pieces
    return pl.pallas_call(
        functools.partial(attention_kernel, hpg, splits),
        grid=(size,),
        in_specs=[pl.BlockSpec((1,) + x.shape[1:], lambda s: (s, 0, 0)) for x in (q, k, v)]
        + [pl.BlockSpec(memory_space=pltpu.VMEM)] * 2,
        out_specs=[pl.BlockSpec((1, r, feats), lambda s: (s, 0, 0)) for r in out_rows],
        out_shape=[jax.ShapeDtypeStruct((size, r, feats), BF16) for r in out_rows],
        cost_estimate=pl.CostEstimate(
            flops=2 * size * hpg * window * tokens * 512,
            bytes_accessed=size * tokens * feats * 4 + hpg * window * tokens * 4,
            transcendentals=size * hpg * window * tokens,
        ),
        compiler_params=pltpu.CompilerParams(vmem_limit_bytes=(58 if tokens > 2048 else 20) * MIB),
        name="attend",
    )(q, k, v, bias, mask)


def project_kernel(labels, sizes, lane_ref, *refs):
    count = len(labels)
    chunks = len(sizes)
    head_refs, refs = refs[: count * chunks], refs[count * chunks :]
    gate_refs, w_ref, refs = refs[:chunks], refs[chunks], refs[chunks + 1 :]
    out_refs, joined_ref = refs[:-1], refs[-1]
    lane = lane_ref[0]
    width = w_ref.shape[1]
    first = 0
    for c, size in enumerate(sizes):
        parts = head_refs[c * count : (c + 1) * count]
        _, rows, feats = parts[0].shape
        values = [ref[...].astype(F32).reshape(size * rows, feats) for ref in parts]
        for g in range(count):
            value = values[0]
            for label, other in zip(labels[1:], values[1:]):
                value = jnp.where(lane == g ^ label, other, value)
            joined_ref[: size * rows, g * feats : (g + 1) * feats] = value
        gate = gate_refs[c][...].reshape(size * rows, width)
        gated = (gate * joined_ref[: size * rows]).astype(BF16)
        result = nn_dot(gated, w_ref[...]).astype(BF16)
        result = result.reshape(size, len(out_refs), rows // len(out_refs), width)
        for k, out_ref in enumerate(out_refs):
            out_ref[first : first + size] = result[:, k]
        first += size


def projected(lane, heads, gates, w_out, labels, sg, query_rows):
    sizes = [x[0].shape[0] for x in heads]
    _, rows, _ = heads[0][0].shape
    width = w_out.shape[1]
    vmem = pl.BlockSpec(memory_space=pltpu.VMEM)
    flat = [x for chunk in heads for x in chunk]
    return pl.pallas_call(
        functools.partial(project_kernel, labels, sizes),
        in_specs=[pl.BlockSpec(memory_space=pltpu.SMEM)] + [vmem] * (len(flat) + len(gates) + 1),
        out_specs=[vmem] * sg,
        out_shape=[jax.ShapeDtypeStruct((sum(sizes), query_rows, width), BF16)] * sg,
        scratch_shapes=[pltpu.VMEM((max(sizes) * rows, width), F32)],
        cost_estimate=pl.CostEstimate(
            flops=2 * sum(sizes) * rows * width * width, bytes_accessed=2 * width * width, transcendentals=0
        ),
        compiler_params=pltpu.CompilerParams(vmem_limit_bytes=12 * MIB),
        name="project",
    )(lane.reshape(1), *flat, *gates, w_out)


def assemble_kernel(sg, firsts, group_ref, *refs):
    out_ref = refs[-1]
    group = group_ref[0]
    for i, ref in enumerate(refs[:-1]):
        first, k = firsts[i // sg], i % sg
        out_ref[group ^ k, first : first + ref.shape[0]] = ref[...]


def assembled(group, parts, firsts, shape):
    vmem = pl.BlockSpec(memory_space=pltpu.VMEM)
    return pl.pallas_call(
        functools.partial(assemble_kernel, shape[0], firsts),
        in_specs=[pl.BlockSpec(memory_space=pltpu.SMEM)] + [vmem] * len(parts),
        out_specs=vmem,
        out_shape=jax.ShapeDtypeStruct(shape, BF16),
        compiler_params=pltpu.CompilerParams(vmem_limit_bytes=8 * MIB),
        name="assemble",
    )(group.reshape(1), *parts)


def head_groups(n, samples):
    hg = 1
    while hg * hg < n or H % hg or samples % (n // hg):
        hg *= 2
    return hg


def chunk_sizes(group_samples):
    if group_samples < 4:
        return [1] * group_samples
    first = group_samples - 2
    return [first - first // 2, first // 2, 1, 1]


def local(
    query_tokens,
    key_tokens,
    pair,
    key_mask,
    span_owner,
    pair_gain,
    pair_proj,
    w_query,
    w_key,
    w_value,
    w_gate,
    w_out,
):
    n = lax.axis_size("key")
    samples, query_rows, width = query_tokens.shape
    keys = key_tokens.shape[1]
    window = pair.shape[0]
    hg = head_groups(n, samples)
    sg = n // hg
    hpg = H // hg
    feats = width // hg
    group_samples = samples // sg
    sizes = chunk_sizes(group_samples)
    firsts = [sum(sizes[:c]) for c in range(len(sizes))]
    direct = query_rows % 16 == 0
    me = lax.axis_index("key")
    group, lane = me // hg, me % hg

    def across(x, code):
        if code == 0:
            return x
        return lax.ppermute(x, "key", [(i, i ^ code) for i in range(n)])

    labels = [0]
    bit = hg // 2
    while bit:
        labels = labels + [m ^ bit for m in labels]
        bit //= 2
    codes = labels + [k * hg + m for m in labels for k in range(1, sg)]
    code_list = jnp.array(codes, jnp.int32)
    slot_of = [0] * n
    for p, code in enumerate(codes):
        slot_of[code] = p

    key_groups = key_tokens.reshape(sg, group_samples, keys, width)
    query_groups = query_tokens.reshape(sg, group_samples, query_rows, width)

    others = range(1, sg)
    packed = pack(group, key_groups, query_groups, 0, sizes[:1], others, 56 * MIB)
    own_tokens = pack(group, key_groups, query_groups, 0, [group_samples], [0], 8 * MIB)[0]
    packed = packed + pack(group, key_groups, query_groups, firsts[1], sizes[1:], others, 12 * MIB)
    got = [[across(x, k * hg) for k, x in zip(others, sent)] for sent in packed]

    def over_lanes(arrays):
        bit = hg // 2
        while bit:
            arrays = arrays + [across(x, bit) for x in arrays]
            bit //= 2
        return arrays

    own_tokens = over_lanes(list(own_tokens))

    pieces = local_bias(lane, pair, key_mask, pair_gain, pair_proj, hpg)
    pieces = [across(x, m) for m, x in enumerate(pieces)]
    parts = {0: stacked(pieces)}
    bit = sg // 2
    while bit:
        parts.update({k ^ bit: across(x, bit * hg) for k, x in parts.items()})
        bit //= 2
    if direct:
        each = query_rows // 16
        qsel = ((code_list ^ me)[:, None] * each + jnp.arange(each)).reshape(window // 16)
    else:
        qsel = jnp.arange(window // 16, dtype=jnp.int32)
    bias, mask = ordered_bias(
        [parts[k] for k in range(sg)], me, span_owner, qsel, hpg, keys, codes, window
    )

    def own(w):
        return lax.dynamic_slice_in_dim(w, lane * feats, feats, 1)

    wq, wk, wv = own(w_query), own(w_key), own(w_value)

    heads, gates = [], []
    for c, size in enumerate(sizes):
        far = [stacked(got[c])]
        far = over_lanes(far)
        queries = None
        if not direct:
            order = jnp.array(slot_of, jnp.int32)[me ^ jnp.arange(n)]
            mine = [x[None, firsts[c] : firsts[c] + size, keys:] for x in own_tokens]
            queries = jnp.concatenate(mine + [x[:, :, keys:] for x in far], axis=0)
            queries = jnp.swapaxes(jnp.take(queries, order, axis=0), 0, 1).reshape(size, window, width)
        if c:
            far, previous = lax.optimization_barrier((far, previous))
        q, k, v, gate = projections(
            firsts[c], own_tokens, far, queries, wq, wk, wv, w_gate, keys, query_rows, window, n * keys
        )
        splits = (query_rows, (sg - 1) * query_rows) if direct else None
        results = attention(q, k, v, bias, mask, hpg, splits, hg)
        previous = results[0]
        if not direct:
            blocks = jnp.take(results[0].reshape(size, n, query_rows, feats), code_list ^ me, axis=1)
            results = []
            for i in range(hg):
                start = hg + i * (sg - 1)
                part = jnp.concatenate([blocks[:, i : i + 1], blocks[:, start : start + sg - 1]], axis=1)
                results.append(part.reshape(size, sg * query_rows, feats))
            mine = own_tokens[0][None, firsts[c] : firsts[c] + size, keys:]
            tokens = jnp.concatenate([mine, far[0][:, :, keys:]], axis=0)
            tokens = jnp.swapaxes(tokens, 0, 1).reshape(size, sg * query_rows, width)
            gate = jax.nn.sigmoid(nn_dot(tokens, w_gate))
        heads.append([across(r, m) for r, m in zip(results, labels)])
        gates.append(gate)
    outs = []
    cut = (len(sizes) + 1) // 2
    for span in (slice(0, cut), slice(cut, len(sizes))):
        back = projected(lane, heads[span], gates[span], w_out, labels, sg, query_rows)
        outs.extend(across(x, k * hg) for k, x in enumerate(back))
    out = assembled(group, outs, [0, firsts[cut]], (sg, group_samples, query_rows, width))
    return out.reshape(samples, query_rows, width)


def solution(mesh):
    return jax.shard_map(
        local,
        mesh=mesh,
        in_specs=(
            P("rep", "key", None),
            P("rep", "key", None),
            P("rep", "key", None),
            P(("rep", "key")),
            P("rep"),
            P(),
            P(),
            P(),
            P(),
            P(),
            P(),
            P(),
        ),
        out_specs=P("rep", "key", None),
        check_vma=False,
    )
```

```python
import functools
import math

import jax
import jax.numpy as jnp
from jax import lax
from jax.experimental import pallas as pl
from jax.experimental.pallas import tpu as pltpu
from jax.sharding import PartitionSpec as P


H = 16
LOG2E = 1.4426950408889634
NEG = -1e9
MIB = 1024 * 1024
F32 = jnp.float32
BF16 = jnp.bfloat16


def nt_dot(a, b):
    return lax.dot_general(a, b, (((1,), (1,)), ((), ())), preferred_element_type=F32)


def nn_dot(a, b):
    return jnp.dot(a, b, preferred_element_type=F32)


def bias_kernel(hpg, lane_ref, mask_ref, pair_ref, gain_ref, proj_ref, *out_refs):
    fold, rows, keys, c = pair_ref.shape
    groups = proj_ref.shape[0]
    heads = groups * hpg
    step = pl.program_id(0)
    proj = jnp.concatenate([proj_ref[lane_ref[0] ^ m] for m in range(groups)], axis=0).astype(BF16)
    total_rows = (out_refs[0].shape[0] - 16) // hpg
    x = jnp.swapaxes(pair_ref[...], 0, 1).reshape(rows * fold * keys, c).astype(F32)
    center = x - jnp.mean(x, axis=-1, keepdims=True)
    spread = jnp.mean(center * center, axis=-1, keepdims=True)
    normed = (center * lax.rsqrt(spread + 1e-5) * gain_ref[...]).astype(BF16)
    bias = nt_dot(proj, normed)
    bias = bias.reshape(heads, rows, fold * keys).astype(BF16)
    for h in range(heads):
        start = pl.multiple_of((h % hpg) * total_rows + step * rows, 16)
        out_refs[h // hpg][pl.ds(start, rows), :] = bias[h]

    @pl.when(step == 0)
    def _():
        row = jnp.concatenate([mask_ref[...].astype(F32)] * fold, axis=1)
        row = jnp.broadcast_to(row, (16, fold * keys)).astype(BF16)
        for out_ref in out_refs:
            out_ref[hpg * total_rows :, :] = row


def local_bias(lane, pair, key_mask, pair_gain, pair_proj, hpg):
    window, keys, c = pair.shape
    groups = pair_proj.shape[1] // hpg
    fold = 128 // keys
    rows = window // fold
    tile = 16
    proj = pair_proj.T.reshape(groups, hpg, c).astype(F32)
    shape = (hpg * rows + 16, 128)
    return pl.pallas_call(
        functools.partial(bias_kernel, hpg),
        grid=(rows // tile,),
        in_specs=[
            pl.BlockSpec(memory_space=pltpu.SMEM),
            pl.BlockSpec((1, keys), lambda i: (0, 0)),
            pl.BlockSpec((fold, tile, keys, c), lambda i: (0, i, 0, 0)),
            pl.BlockSpec((1, c), lambda i: (0, 0)),
            pl.BlockSpec((groups, hpg, c), lambda i: (0, 0, 0)),
        ],
        out_specs=[pl.BlockSpec(shape, lambda i: (0, 0))] * groups,
        out_shape=[jax.ShapeDtypeStruct(shape, BF16)] * groups,
        cost_estimate=pl.CostEstimate(
            flops=2 * window * keys * c * 256, bytes_accessed=window * keys * c * 2, transcendentals=0
        ),
        compiler_params=pltpu.CompilerParams(vmem_limit_bytes=56 * MIB),
        name="bias_local",
    )(lane.reshape(1), key_mask[None], pair.reshape(fold, rows, keys, c), pair_gain[None], proj)


def pack_kernel(sizes, count, group_ref, *refs):
    step = pl.program_id(0)
    start = 0
    for i, size in enumerate(sizes):

        @pl.when((step >= start) & (step < start + size))
        def _(i=i):
            for k in range(count):
                out_ref = refs[(2 + i) * count + k]
                keys = refs[k].shape[2]
                out_ref[0, :keys] = refs[k][0, 0]
                out_ref[0, keys:] = refs[count + k][0, 0]

        start += size


def pack(group, key_groups, query_groups, first, sizes, steps, limit):
    _, _, keys, width = key_groups.shape
    rows = query_groups.shape[2]
    total = sum(sizes)
    count = len(steps)

    def spec(length, k):
        return pl.BlockSpec((1, 1, length, width), lambda s, g: (g[0] ^ k, first + s, 0, 0))

    def out_spec(i):
        start = sum(sizes[:i])
        return pl.BlockSpec(
            (1, keys + rows, width), lambda s, g: (jnp.clip(s - start, 0, sizes[i] - 1), 0, 0)
        )

    outs = pl.pallas_call(
        functools.partial(pack_kernel, sizes, count),
        grid_spec=pltpu.PrefetchScalarGridSpec(
            num_scalar_prefetch=1,
            grid=(total,),
            in_specs=[spec(keys, k) for k in steps] + [spec(rows, k) for k in steps],
            out_specs=[out_spec(i) for i in range(len(sizes)) for _ in steps],
        ),
        out_shape=[jax.ShapeDtypeStruct((size, keys + rows, width), BF16) for size in sizes for _ in steps],
        cost_estimate=pl.CostEstimate(
            flops=0, bytes_accessed=4 * count * total * (keys + rows) * width, transcendentals=0
        ),
        compiler_params=pltpu.CompilerParams(vmem_limit_bytes=limit),
        name="pack",
    )(group.reshape(1), *([key_groups] * count), *([query_groups] * count))
    return [outs[i * count : (i + 1) * count] for i in range(len(sizes))]


def stack_kernel(*refs):
    for i, ref in enumerate(refs[:-1]):
        refs[-1][i] = ref[...]


def stacked(parts):
    count, shape = len(parts), parts[0].shape
    rest = (0,) * (len(shape) - 1)
    block = (1,) + shape[1:] if len(shape) == 3 else shape
    steps = shape[0] if len(shape) == 3 else 1
    return pl.pallas_call(
        stack_kernel,
        grid=(steps,),
        in_specs=[pl.BlockSpec(block, lambda s: (s,) + rest)] * count,
        out_specs=pl.BlockSpec((count,) + block, lambda s: (0, s) + rest),
        out_shape=jax.ShapeDtypeStruct((count,) + shape, BF16),
        cost_estimate=pl.CostEstimate(
            flops=0, bytes_accessed=4 * count * math.prod(shape), transcendentals=0
        ),
        compiler_params=pltpu.CompilerParams(vmem_limit_bytes=8 * MIB),
        name="stack",
    )(*parts)


def order_kernel(hpg, keys, codes, me_ref, owner_ref, qsel_ref, *refs):
    parts, (bias_ref, mask_ref, inv_ref, x_ref) = refs[:-4], refs[-4:]
    n = len(codes)
    each = n // len(parts)
    for k, part_ref in enumerate(parts):
        x_ref[k * each : (k + 1) * each] = part_ref[...]
    fold = 128 // keys
    me = me_ref[0]
    rows = (x_ref.shape[1] - 16) // hpg
    slots = bias_ref.shape[1] // 16
    for d in range(n):
        inv_ref[owner_ref[d]] = d
    lane = lax.broadcasted_iota(jnp.int32, (16, 128), 1) // keys

    def of_tile(t):
        stored = [inv_ref[me ^ codes[t * fold + f]] ^ me for f in range(fold)]
        masks = x_ref[codes[t * fold], hpg * rows : hpg * rows + 16, :].astype(F32)
        for f in range(1, fold):
            part = x_ref[codes[t * fold + f], hpg * rows : hpg * rows + 16, :].astype(F32)
            masks = jnp.where(lane == f, part, masks)
        mask_ref[:, t * 128 : (t + 1) * 128] = masks[:8]
        return stored, masks > 0

    tiles = [of_tile(t) for t in range(n // fold)]

    def query_slot(p, carry):
        a = qsel_ref[p]
        part = a // (rows // 16)
        row = a % (rows // 16) * 16
        out = pl.multiple_of(p * 16, 16)
        for h in range(hpg):
            start = pl.multiple_of(h * rows + row, 16)
            for t, (stored, present) in enumerate(tiles):
                value = None
                for f in range(fold):
                    block = x_ref[stored[f], pl.ds(start, 16), :].astype(F32)
                    if fold == 2:
                        block = jnp.where(part == f, block, pltpu.roll(block, keys, 1))
                    value = block if value is None else jnp.where(lane == f, block, value)
                value = jnp.where(present, value * LOG2E, NEG * LOG2E)
                bias_ref[h, pl.ds(out, 16), t * 128 : (t + 1) * 128] = value
        return carry

    lax.fori_loop(0, slots, query_slot, 0)


def ordered_bias(parts, me, span_owner, qsel, hpg, keys, codes, window):
    n = len(codes)
    limit = (40 if n * keys > 2048 else 14) * MIB
    smem = pl.BlockSpec(memory_space=pltpu.SMEM)
    vmem = pl.BlockSpec(memory_space=pltpu.VMEM)
    return pl.pallas_call(
        functools.partial(order_kernel, hpg, keys, codes),
        in_specs=[smem, smem, smem] + [vmem] * len(parts),
        out_specs=[vmem, vmem],
        out_shape=[
            jax.ShapeDtypeStruct((hpg, window, n * keys), F32),
            jax.ShapeDtypeStruct((8, n * keys), F32),
        ],
        scratch_shapes=[
            pltpu.SMEM((n,), jnp.int32),
            pltpu.VMEM((n,) + parts[0].shape[1:], BF16),
        ],
        cost_estimate=pl.CostEstimate(
            flops=hpg * window * n * keys * 8, bytes_accessed=hpg * window * n * keys * 6, transcendentals=0
        ),
        compiler_params=pltpu.CompilerParams(vmem_limit_bytes=limit),
        name="bias_order",
    )(me.reshape(1), span_owner, qsel, *parts)


def heads_kernel(pieces, direct, keys, *refs):
    own_refs, far_refs, refs = refs[:pieces], refs[pieces : 2 * pieces], refs[2 * pieces :]
    if not direct:
        query_ref, refs = refs[0], refs[1:]
    wq_ref, wk_ref, wv_ref, wg_ref, q_ref, k_ref, v_ref, gate_ref = refs
    total_rows, width = own_refs[0].shape[1:]

    def own_rows(start, stop):
        return jnp.concatenate([ref[0, start:stop] for ref in own_refs], axis=0)

    def far_rows(ref, start, stop):
        block = ref[:, 0, start:stop]
        return block.reshape(block.shape[0] * block.shape[1], width)

    at = 0
    for m in range(-1, pieces):
        block = own_rows(0, keys) if m < 0 else far_rows(far_refs[m], 0, keys)
        span = slice(at, at + block.shape[0])
        k_ref[0, :, span] = nn_dot(block, wk_ref[...]).T.astype(BF16)
        v_ref[0, span, :] = nn_dot(block, wv_ref[...]).astype(BF16)
        at += block.shape[0]
    if direct:
        at = 0
        for m in range(-1, pieces):
            block = own_rows(keys, total_rows) if m < 0 else far_rows(far_refs[m], keys, total_rows)
            q_ref[0, at : at + block.shape[0], :] = nn_dot(block, wq_ref[...]).astype(BF16)
            at += block.shape[0]
        block = jnp.concatenate([own_refs[0][0, keys:], far_rows(far_refs[0], keys, total_rows)], axis=0)
        gate_ref[0] = jax.nn.sigmoid(nn_dot(block, wg_ref[...]))
    else:
        q_ref[0] = nn_dot(query_ref[0], wq_ref[...]).astype(BF16)
        gate_ref[...] = jnp.zeros_like(gate_ref)


def projections(first, own, far, queries, wq, wk, wv, w_gate, keys, query_rows, window, tokens):
    pieces = len(far)
    others, size, rows, width = far[0].shape
    feats = wq.shape[1]
    direct = queries is None
    whole = pl.BlockSpec(memory_space=pltpu.VMEM)
    specs = [pl.BlockSpec((1, rows, width), lambda s: (first + s, 0, 0))] * pieces
    specs += [pl.BlockSpec((others, 1, rows, width), lambda s: (0, s, 0, 0))] * pieces
    args = list(own) + list(far)
    gate_rows = (others + 1) * query_rows
    if not direct:
        specs.append(pl.BlockSpec((1, window, width), lambda s: (s, 0, 0)))
        args.append(queries)
    consts = [wq, wk, wv, w_gate]
    shapes = [(window, feats), (feats, tokens), (tokens, feats), (gate_rows, width)]
    return pl.pallas_call(
        functools.partial(heads_kernel, pieces, direct, keys),
        grid=(size,),
        in_specs=specs + [whole] * len(consts),
        out_specs=[pl.BlockSpec((1,) + x, lambda s: (s, 0, 0)) for x in shapes],
        out_shape=[
            jax.ShapeDtypeStruct((size,) + x, F32 if i == 3 else BF16) for i, x in enumerate(shapes)
        ],
        cost_estimate=pl.CostEstimate(
            flops=4 * size * tokens * width * feats, bytes_accessed=size * tokens * width * 3, transcendentals=0
        ),
        compiler_params=pltpu.CompilerParams(vmem_limit_bytes=(48 if tokens > 2048 else 16) * MIB),
        name="heads",
    )(*args, *consts)


def attention_kernel(hpg, splits, q_ref, k_ref, v_ref, bias_ref, mask_ref, *out_refs):
    q = q_ref[0]
    k = k_ref[0] * mask_ref[:1].astype(BF16)
    head_size = q.shape[1] // hpg
    scale = LOG2E / math.sqrt(head_size)
    owner = lax.broadcasted_iota(jnp.int32, q.shape, 1) // head_size
    total = None
    for h in range(hpg):
        mine = owner == h
        scores = nn_dot(jnp.where(mine, q, jnp.zeros_like(q)), k)
        scores = scores * scale + bias_ref[h]
        weights = jnp.exp2(scores - jnp.max(scores, axis=-1, keepdims=True))
        norm = 1.0 / jnp.sum(weights, axis=-1, keepdims=True)
        result = nn_dot((weights * norm).astype(BF16), v_ref[0])
        total = result if total is None else jnp.where(mine, result, total)
    total = total.astype(BF16)
    if splits is None:
        out_refs[0][0] = total
        return
    own, far = splits
    pieces = len(out_refs)
    for m, out_ref in enumerate(out_refs):
        out_ref[0, :own] = total[m * own : (m + 1) * own]
        out_ref[0, own:] = total[pieces * own + m * far : pieces * own + (m + 1) * far]


def attention(q, k, v, bias, mask, hpg, splits, pieces):
    size, window, feats = q.shape
    tokens = k.shape[2]
    out_rows = [window] if splits is None else [sum(splits)] * pieces
    return pl.pallas_call(
        functools.partial(attention_kernel, hpg, splits),
        grid=(size,),
        in_specs=[pl.BlockSpec((1,) + x.shape[1:], lambda s: (s, 0, 0)) for x in (q, k, v)]
        + [pl.BlockSpec(memory_space=pltpu.VMEM)] * 2,
        out_specs=[pl.BlockSpec((1, r, feats), lambda s: (s, 0, 0)) for r in out_rows],
        out_shape=[jax.ShapeDtypeStruct((size, r, feats), BF16) for r in out_rows],
        cost_estimate=pl.CostEstimate(
            flops=2 * size * hpg * window * tokens * 512,
            bytes_accessed=size * tokens * feats * 4 + hpg * window * tokens * 4,
            transcendentals=size * hpg * window * tokens,
        ),
        compiler_params=pltpu.CompilerParams(vmem_limit_bytes=(58 if tokens > 2048 else 20) * MIB),
        name="attend",
    )(q, k, v, bias, mask)


def project_kernel(labels, sizes, lane_ref, *refs):
    count = len(labels)
    chunks = len(sizes)
    head_refs, refs = refs[: count * chunks], refs[count * chunks :]
    gate_refs, w_ref, refs = refs[:chunks], refs[chunks], refs[chunks + 1 :]
    out_refs, joined_ref = refs[:-1], refs[-1]
    lane = lane_ref[0]
    width = w_ref.shape[1]
    first = 0
    for c, size in enumerate(sizes):
        parts = head_refs[c * count : (c + 1) * count]
        _, rows, feats = parts[0].shape
        values = [ref[...].astype(F32).reshape(size * rows, feats) for ref in parts]
        for g in range(count):
            value = values[0]
            for label, other in zip(labels[1:], values[1:]):
                value = jnp.where(lane == g ^ label, other, value)
            joined_ref[: size * rows, g * feats : (g + 1) * feats] = value
        gate = gate_refs[c][...].reshape(size * rows, width)
        gated = (gate * joined_ref[: size * rows]).astype(BF16)
        result = nn_dot(gated, w_ref[...]).astype(BF16)
        result = result.reshape(size, len(out_refs), rows // len(out_refs), width)
        for k, out_ref in enumerate(out_refs):
            out_ref[first : first + size] = result[:, k]
        first += size


def projected(lane, heads, gates, w_out, labels, sg, query_rows):
    sizes = [x[0].shape[0] for x in heads]
    _, rows, _ = heads[0][0].shape
    width = w_out.shape[1]
    vmem = pl.BlockSpec(memory_space=pltpu.VMEM)
    flat = [x for chunk in heads for x in chunk]
    return pl.pallas_call(
        functools.partial(project_kernel, labels, sizes),
        in_specs=[pl.BlockSpec(memory_space=pltpu.SMEM)] + [vmem] * (len(flat) + len(gates) + 1),
        out_specs=[vmem] * sg,
        out_shape=[jax.ShapeDtypeStruct((sum(sizes), query_rows, width), BF16)] * sg,
        scratch_shapes=[pltpu.VMEM((max(sizes) * rows, width), F32)],
        cost_estimate=pl.CostEstimate(
            flops=2 * sum(sizes) * rows * width * width, bytes_accessed=2 * width * width, transcendentals=0
        ),
        compiler_params=pltpu.CompilerParams(vmem_limit_bytes=12 * MIB),
        name="project",
    )(lane.reshape(1), *flat, *gates, w_out)


def assemble_kernel(sg, firsts, group_ref, *refs):
    out_ref = refs[-1]
    group = group_ref[0]
    for i, ref in enumerate(refs[:-1]):
        first, k = firsts[i // sg], i % sg
        out_ref[group ^ k, first : first + ref.shape[0]] = ref[...]


def assembled(group, parts, firsts, shape):
    vmem = pl.BlockSpec(memory_space=pltpu.VMEM)
    return pl.pallas_call(
        functools.partial(assemble_kernel, shape[0], firsts),
        in_specs=[pl.BlockSpec(memory_space=pltpu.SMEM)] + [vmem] * len(parts),
        out_specs=vmem,
        out_shape=jax.ShapeDtypeStruct(shape, BF16),
        compiler_params=pltpu.CompilerParams(vmem_limit_bytes=8 * MIB),
        name="assemble",
    )(group.reshape(1), *parts)


def head_groups(n, samples):
    hg = 1
    while hg * hg < n or H % hg or samples % (n // hg):
        hg *= 2
    return hg


def chunk_sizes(group_samples):
    last = max(group_samples // 6, 1)
    middle = max(group_samples // 3, 1)
    return [group_samples - middle - last, middle, last]


def local(
    query_tokens,
    key_tokens,
    pair,
    key_mask,
    span_owner,
    pair_gain,
    pair_proj,
    w_query,
    w_key,
    w_value,
    w_gate,
    w_out,
):
    n = lax.axis_size("key")
    samples, query_rows, width = query_tokens.shape
    keys = key_tokens.shape[1]
    window = pair.shape[0]
    hg = head_groups(n, samples)
    sg = n // hg
    hpg = H // hg
    feats = width // hg
    group_samples = samples // sg
    sizes = chunk_sizes(group_samples)
    firsts = [sum(sizes[:c]) for c in range(len(sizes))]
    direct = query_rows % 16 == 0
    me = lax.axis_index("key")
    group, lane = me // hg, me % hg

    def across(x, code):
        if code == 0:
            return x
        return lax.ppermute(x, "key", [(i, i ^ code) for i in range(n)])

    labels = [0]
    bit = hg // 2
    while bit:
        labels = labels + [m ^ bit for m in labels]
        bit //= 2
    codes = labels + [k * hg + m for m in labels for k in range(1, sg)]
    code_list = jnp.array(codes, jnp.int32)
    slot_of = [0] * n
    for p, code in enumerate(codes):
        slot_of[code] = p

    key_groups = key_tokens.reshape(sg, group_samples, keys, width)
    query_groups = query_tokens.reshape(sg, group_samples, query_rows, width)

    others = range(1, sg)
    packed = pack(group, key_groups, query_groups, 0, sizes[:1], others, 56 * MIB)
    own_tokens = pack(group, key_groups, query_groups, 0, [group_samples], [0], 8 * MIB)[0]
    packed = packed + pack(group, key_groups, query_groups, firsts[1], sizes[1:], others, 12 * MIB)
    got = [[across(x, k * hg) for k, x in zip(others, sent)] for sent in packed]

    def over_lanes(arrays):
        bit = hg // 2
        while bit:
            arrays = arrays + [across(x, bit) for x in arrays]
            bit //= 2
        return arrays

    own_tokens = over_lanes(list(own_tokens))

    pieces = local_bias(lane, pair, key_mask, pair_gain, pair_proj, hpg)
    pieces = [across(x, m) for m, x in enumerate(pieces)]
    parts = {0: stacked(pieces)}
    bit = sg // 2
    while bit:
        parts.update({k ^ bit: across(x, bit * hg) for k, x in parts.items()})
        bit //= 2
    if direct:
        each = query_rows // 16
        qsel = ((code_list ^ me)[:, None] * each + jnp.arange(each)).reshape(window // 16)
    else:
        qsel = jnp.arange(window // 16, dtype=jnp.int32)
    bias, mask = ordered_bias(
        [parts[k] for k in range(sg)], me, span_owner, qsel, hpg, keys, codes, window
    )

    def own(w):
        return lax.dynamic_slice_in_dim(w, lane * feats, feats, 1)

    wq, wk, wv = own(w_query), own(w_key), own(w_value)

    heads, gates = [], []
    for c, size in enumerate(sizes):
        far = [stacked(got[c])]
        far = over_lanes(far)
        queries = None
        if not direct:
            order = jnp.array(slot_of, jnp.int32)[me ^ jnp.arange(n)]
            mine = [x[None, firsts[c] : firsts[c] + size, keys:] for x in own_tokens]
            queries = jnp.concatenate(mine + [x[:, :, keys:] for x in far], axis=0)
            queries = jnp.swapaxes(jnp.take(queries, order, axis=0), 0, 1).reshape(size, window, width)
        if c:
            far, previous = lax.optimization_barrier((far, previous))
        q, k, v, gate = projections(
            firsts[c], own_tokens, far, queries, wq, wk, wv, w_gate, keys, query_rows, window, n * keys
        )
        splits = (query_rows, (sg - 1) * query_rows) if direct else None
        results = attention(q, k, v, bias, mask, hpg, splits, hg)
        previous = results[0]
        if not direct:
            blocks = jnp.take(results[0].reshape(size, n, query_rows, feats), code_list ^ me, axis=1)
            results = []
            for i in range(hg):
                start = hg + i * (sg - 1)
                part = jnp.concatenate([blocks[:, i : i + 1], blocks[:, start : start + sg - 1]], axis=1)
                results.append(part.reshape(size, sg * query_rows, feats))
            mine = own_tokens[0][None, firsts[c] : firsts[c] + size, keys:]
            tokens = jnp.concatenate([mine, far[0][:, :, keys:]], axis=0)
            tokens = jnp.swapaxes(tokens, 0, 1).reshape(size, sg * query_rows, width)
            gate = jax.nn.sigmoid(nn_dot(tokens, w_gate))
        heads.append([across(r, m) for r, m in zip(results, labels)])
        gates.append(gate)
    outs = []
    cut = (len(sizes) + 1) // 2
    for span in (slice(0, cut), slice(cut, len(sizes))):
        back = projected(lane, heads[span], gates[span], w_out, labels, sg, query_rows)
        outs.extend(across(x, k * hg) for k, x in enumerate(back))
    out = assembled(group, outs, [0, firsts[cut]], (sg, group_samples, query_rows, width))
    return out.reshape(samples, query_rows, width)


def solution(mesh):
    return jax.shard_map(
        local,
        mesh=mesh,
        in_specs=(
            P("rep", "key", None),
            P("rep", "key", None),
            P("rep", "key", None),
            P(("rep", "key")),
            P("rep"),
            P(),
            P(),
            P(),
            P(),
            P(),
            P(),
            P(),
        ),
        out_specs=P("rep", "key", None),
        check_vma=False,
    )
```

```python
import functools
import math

import jax
import jax.numpy as jnp
from jax import lax
from jax.experimental import pallas as pl
from jax.experimental.pallas import tpu as pltpu
from jax.sharding import PartitionSpec as P


H = 16
LOG2E = 1.4426950408889634
NEG = -1e9
MIB = 1024 * 1024
F32 = jnp.float32
BF16 = jnp.bfloat16


def nt_dot(a, b):
    return lax.dot_general(a, b, (((1,), (1,)), ((), ())), preferred_element_type=F32)


def nn_dot(a, b):
    return jnp.dot(a, b, preferred_element_type=F32)


def bias_kernel(hpg, mask_ref, pair_ref, gain_ref, proj_ref, *out_refs):
    fold, rows, keys, c = pair_ref.shape
    heads = proj_ref.shape[0]
    step = pl.program_id(0)
    total_rows = (out_refs[0].shape[0] - 16) // hpg
    x = jnp.swapaxes(pair_ref[...], 0, 1).reshape(rows * fold * keys, c).astype(F32)
    center = x - jnp.mean(x, axis=-1, keepdims=True)
    spread = jnp.mean(center * center, axis=-1, keepdims=True)
    normed = (center * lax.rsqrt(spread + 1e-5) * gain_ref[...]).astype(BF16)
    bias = nt_dot(proj_ref[...], normed)
    bias = bias.reshape(heads, rows, fold * keys).astype(BF16)
    for h in range(heads):
        start = pl.multiple_of((h % hpg) * total_rows + step * rows, 16)
        out_refs[h // hpg][pl.ds(start, rows), :] = bias[h]

    @pl.when(step == 0)
    def _():
        row = jnp.broadcast_to(mask_ref[...], (16, fold * keys)).astype(BF16)
        for out_ref in out_refs:
            out_ref[hpg * total_rows :, :] = row


def local_bias(pair, key_mask, pair_gain, proj_t, hpg):
    window, keys, c = pair.shape
    heads = proj_t.shape[0]
    fold = 128 // keys
    rows = window // fold
    tile = 16
    mask = jnp.tile(key_mask.astype(F32), fold)[None]
    shape = (hpg * rows + 16, 128)
    return pl.pallas_call(
        functools.partial(bias_kernel, hpg),
        grid=(rows // tile,),
        in_specs=[
            pl.BlockSpec((1, 128), lambda i: (0, 0)),
            pl.BlockSpec((fold, tile, keys, c), lambda i: (0, i, 0, 0)),
            pl.BlockSpec((1, c), lambda i: (0, 0)),
            pl.BlockSpec((heads, c), lambda i: (0, 0)),
        ],
        out_specs=[pl.BlockSpec(shape, lambda i: (0, 0))] * (heads // hpg),
        out_shape=[jax.ShapeDtypeStruct(shape, BF16)] * (heads // hpg),
        cost_estimate=pl.CostEstimate(
            flops=2 * window * keys * c * 256, bytes_accessed=window * keys * c * 2, transcendentals=0
        ),
        compiler_params=pltpu.CompilerParams(vmem_limit_bytes=16 * MIB),
        name="bias_local",
    )(mask, pair.reshape(fold, rows, keys, c), pair_gain[None], proj_t)


def pack_kernel(sizes, count, group_ref, *refs):
    step = pl.program_id(0)
    start = 0
    for i, size in enumerate(sizes):

        @pl.when((step >= start) & (step < start + size))
        def _(i=i):
            for k in range(count):
                out_ref = refs[(2 + i) * count + k]
                keys = refs[k].shape[2]
                out_ref[0, :keys] = refs[k][0, 0]
                out_ref[0, keys:] = refs[count + k][0, 0]

        start += size


def pack(group, key_groups, query_groups, first, sizes, steps, limit):
    _, _, keys, width = key_groups.shape
    rows = query_groups.shape[2]
    total = sum(sizes)
    count = len(steps)

    def spec(length, k):
        return pl.BlockSpec((1, 1, length, width), lambda s, g: (g[0] ^ k, first + s, 0, 0))

    def out_spec(i):
        start = sum(sizes[:i])
        return pl.BlockSpec(
            (1, keys + rows, width), lambda s, g: (jnp.clip(s - start, 0, sizes[i] - 1), 0, 0)
        )

    outs = pl.pallas_call(
        functools.partial(pack_kernel, sizes, count),
        grid_spec=pltpu.PrefetchScalarGridSpec(
            num_scalar_prefetch=1,
            grid=(total,),
            in_specs=[spec(keys, k) for k in steps] + [spec(rows, k) for k in steps],
            out_specs=[out_spec(i) for i in range(len(sizes)) for _ in steps],
        ),
        out_shape=[jax.ShapeDtypeStruct((size, keys + rows, width), BF16) for size in sizes for _ in steps],
        cost_estimate=pl.CostEstimate(
            flops=0, bytes_accessed=4 * count * total * (keys + rows) * width, transcendentals=0
        ),
        compiler_params=pltpu.CompilerParams(vmem_limit_bytes=limit),
        name="pack",
    )(group.reshape(1), *([key_groups] * count), *([query_groups] * count))
    return [outs[i * count : (i + 1) * count] for i in range(len(sizes))]


def stack_kernel(*refs):
    for i, ref in enumerate(refs[:-1]):
        refs[-1][i] = ref[...]


def stacked(parts):
    count, shape = len(parts), parts[0].shape
    rest = (0,) * (len(shape) - 1)
    block = (1,) + shape[1:] if len(shape) == 3 else shape
    steps = shape[0] if len(shape) == 3 else 1
    return pl.pallas_call(
        stack_kernel,
        grid=(steps,),
        in_specs=[pl.BlockSpec(block, lambda s: (s,) + rest)] * count,
        out_specs=pl.BlockSpec((count,) + block, lambda s: (0, s) + rest),
        out_shape=jax.ShapeDtypeStruct((count,) + shape, BF16),
        cost_estimate=pl.CostEstimate(
            flops=0, bytes_accessed=4 * count * math.prod(shape), transcendentals=0
        ),
        compiler_params=pltpu.CompilerParams(vmem_limit_bytes=8 * MIB),
        name="stack",
    )(*parts)


def order_kernel(hpg, keys, codes, me_ref, owner_ref, qsel_ref, *refs):
    parts, (bias_ref, mask_ref, inv_ref, x_ref) = refs[:-4], refs[-4:]
    n = len(codes)
    each = n // len(parts)
    for k, part_ref in enumerate(parts):
        x_ref[k * each : (k + 1) * each] = part_ref[...]
    fold = 128 // keys
    me = me_ref[0]
    rows = (x_ref.shape[1] - 16) // hpg
    slots = bias_ref.shape[1] // 16
    for d in range(n):
        inv_ref[owner_ref[d]] = d
    lane = lax.broadcasted_iota(jnp.int32, (16, 128), 1) // keys

    def of_tile(t):
        stored = [inv_ref[me ^ codes[t * fold + f]] ^ me for f in range(fold)]
        masks = x_ref[codes[t * fold], hpg * rows : hpg * rows + 16, :].astype(F32)
        for f in range(1, fold):
            part = x_ref[codes[t * fold + f], hpg * rows : hpg * rows + 16, :].astype(F32)
            masks = jnp.where(lane == f, part, masks)
        mask_ref[:, t * 128 : (t + 1) * 128] = masks[:8]
        return stored, masks > 0

    tiles = [of_tile(t) for t in range(n // fold)]

    def query_slot(p, carry):
        a = qsel_ref[p]
        part = a // (rows // 16)
        row = a % (rows // 16) * 16
        out = pl.multiple_of(p * 16, 16)
        for h in range(hpg):
            start = pl.multiple_of(h * rows + row, 16)
            for t, (stored, present) in enumerate(tiles):
                value = None
                for f in range(fold):
                    block = x_ref[stored[f], pl.ds(start, 16), :].astype(F32)
                    if fold == 2:
                        block = jnp.where(part == f, block, pltpu.roll(block, keys, 1))
                    value = block if value is None else jnp.where(lane == f, block, value)
                value = jnp.where(present, value * LOG2E, NEG * LOG2E)
                bias_ref[h, pl.ds(out, 16), t * 128 : (t + 1) * 128] = value
        return carry

    lax.fori_loop(0, slots, query_slot, 0)


def ordered_bias(parts, me, span_owner, qsel, hpg, keys, codes, window):
    n = len(codes)
    limit = (40 if n * keys > 2048 else 14) * MIB
    smem = pl.BlockSpec(memory_space=pltpu.SMEM)
    vmem = pl.BlockSpec(memory_space=pltpu.VMEM)
    return pl.pallas_call(
        functools.partial(order_kernel, hpg, keys, codes),
        in_specs=[smem, smem, smem] + [vmem] * len(parts),
        out_specs=[vmem, vmem],
        out_shape=[
            jax.ShapeDtypeStruct((hpg, window, n * keys), F32),
            jax.ShapeDtypeStruct((8, n * keys), F32),
        ],
        scratch_shapes=[
            pltpu.SMEM((n,), jnp.int32),
            pltpu.VMEM((n,) + parts[0].shape[1:], BF16),
        ],
        cost_estimate=pl.CostEstimate(
            flops=hpg * window * n * keys * 8, bytes_accessed=hpg * window * n * keys * 6, transcendentals=0
        ),
        compiler_params=pltpu.CompilerParams(vmem_limit_bytes=limit),
        name="bias_order",
    )(me.reshape(1), span_owner, qsel, *parts)


def heads_kernel(pieces, direct, keys, *refs):
    own_refs, far_refs, refs = refs[:pieces], refs[pieces : 2 * pieces], refs[2 * pieces :]
    if not direct:
        query_ref, refs = refs[0], refs[1:]
    wq_ref, wk_ref, wv_ref, wg_ref = refs[:4]
    q_ref, k_ref, v_ref, gate_ref = refs[-4:]
    total_rows, width = own_refs[0].shape[1:]

    def own_rows(start, stop):
        return jnp.concatenate([ref[0, start:stop] for ref in own_refs], axis=0)

    def far_rows(ref, start, stop):
        block = ref[:, 0, start:stop]
        return block.reshape(block.shape[0] * block.shape[1], width)

    at = 0
    for m in range(-1, pieces):
        block = own_rows(0, keys) if m < 0 else far_rows(far_refs[m], 0, keys)
        span = slice(at, at + block.shape[0])
        k_ref[0, :, span] = nn_dot(block, wk_ref[...]).T.astype(BF16)
        v_ref[0, span, :] = nn_dot(block, wv_ref[...]).astype(BF16)
        at += block.shape[0]
    if direct:
        at = 0
        for m in range(-1, pieces):
            block = own_rows(keys, total_rows) if m < 0 else far_rows(far_refs[m], keys, total_rows)
            q_ref[0, at : at + block.shape[0], :] = nn_dot(block, wq_ref[...]).astype(BF16)
            at += block.shape[0]
        block = jnp.concatenate([own_refs[0][0, keys:], far_rows(far_refs[0], keys, total_rows)], axis=0)
        gate_ref[0] = jax.nn.sigmoid(nn_dot(block, wg_ref[...]))
    else:
        q_ref[0] = nn_dot(query_ref[0], wq_ref[...]).astype(BF16)
        gate_ref[...] = jnp.zeros_like(gate_ref)


def projections(first, total, offset, filled, own, far, queries, wq, wk, wv, w_gate, keys, query_rows, window, tokens):
    pieces = len(far)
    others, size, rows, width = far[0].shape
    feats = wq.shape[1]
    direct = queries is None
    whole = pl.BlockSpec(memory_space=pltpu.VMEM)
    specs = [pl.BlockSpec((1, rows, width), lambda s: (first + s, 0, 0))] * pieces
    specs += [pl.BlockSpec((others, 1, rows, width), lambda s: (0, s, 0, 0))] * pieces
    args = list(own) + list(far)
    gate_rows = (others + 1) * query_rows
    if not direct:
        specs.append(pl.BlockSpec((1, window, width), lambda s: (s, 0, 0)))
        args.append(queries)
    consts = [wq, wk, wv, w_gate]
    shapes = [(window, feats), (feats, tokens), (tokens, feats), (gate_rows, width)]
    before = len(args) + len(consts)
    return pl.pallas_call(
        functools.partial(heads_kernel, pieces, direct, keys),
        grid=(size,),
        in_specs=specs + [whole] * len(consts) + [pl.BlockSpec(memory_space=pl.ANY)] * len(filled),
        out_specs=[pl.BlockSpec((1,) + x, lambda s: (offset + s, 0, 0)) for x in shapes],
        out_shape=[
            jax.ShapeDtypeStruct((total,) + x, F32 if i == 3 else BF16) for i, x in enumerate(shapes)
        ],
        input_output_aliases={before + i: i for i in range(len(filled))},
        cost_estimate=pl.CostEstimate(
            flops=4 * size * tokens * width * feats, bytes_accessed=size * tokens * width * 3, transcendentals=0
        ),
        compiler_params=pltpu.CompilerParams(vmem_limit_bytes=(48 if tokens > 2048 else 16) * MIB),
        name="heads",
    )(*args, *consts, *filled)


def attention_kernel(hpg, splits, q_ref, k_ref, v_ref, bias_ref, mask_ref, *out_refs):
    q = q_ref[0]
    k = k_ref[0] * mask_ref[:1].astype(BF16)
    head_size = q.shape[1] // hpg
    scale = LOG2E / math.sqrt(head_size)
    owner = lax.broadcasted_iota(jnp.int32, q.shape, 1) // head_size
    total = None
    for h in range(hpg):
        mine = owner == h
        scores = nn_dot(jnp.where(mine, q, jnp.zeros_like(q)), k)
        scores = scores * scale + bias_ref[h]
        weights = jnp.exp2(scores - jnp.max(scores, axis=-1, keepdims=True))
        norm = 1.0 / jnp.sum(weights, axis=-1, keepdims=True)
        result = nn_dot((weights * norm).astype(BF16), v_ref[0])
        total = result if total is None else jnp.where(mine, result, total)
    total = total.astype(BF16)
    if splits is None:
        out_refs[0][0] = total
        return
    own, far = splits
    pieces = len(out_refs)
    for m, out_ref in enumerate(out_refs):
        out_ref[0, :own] = total[m * own : (m + 1) * own]
        out_ref[0, own:] = total[pieces * own + m * far : pieces * own + (m + 1) * far]


def attention(q, k, v, bias, mask, hpg, splits, pieces):
    size, window, feats = q.shape
    tokens = k.shape[2]
    out_rows = [window] if splits is None else [sum(splits)] * pieces
    return pl.pallas_call(
        functools.partial(attention_kernel, hpg, splits),
        grid=(size,),
        in_specs=[pl.BlockSpec((1,) + x.shape[1:], lambda s: (s, 0, 0)) for x in (q, k, v)]
        + [pl.BlockSpec(memory_space=pltpu.VMEM)] * 2,
        out_specs=[pl.BlockSpec((1, r, feats), lambda s: (s, 0, 0)) for r in out_rows],
        out_shape=[jax.ShapeDtypeStruct((size, r, feats), BF16) for r in out_rows],
        cost_estimate=pl.CostEstimate(
            flops=2 * size * hpg * window * tokens * 512,
            bytes_accessed=size * tokens * feats * 4 + hpg * window * tokens * 4,
            transcendentals=size * hpg * window * tokens,
        ),
        compiler_params=pltpu.CompilerParams(vmem_limit_bytes=(58 if tokens > 2048 else 20) * MIB),
        name="attend",
    )(q, k, v, bias, mask)


def project_kernel(labels, sizes, lane_ref, *refs):
    count = len(labels)
    chunks = len(sizes)
    head_refs, refs = refs[: count * chunks], refs[count * chunks :]
    gate_refs, w_ref, refs = refs[:chunks], refs[chunks], refs[chunks + 1 :]
    out_refs, joined_ref = refs[:-1], refs[-1]
    lane = lane_ref[0]
    width = w_ref.shape[1]
    first = 0
    for c, size in enumerate(sizes):
        parts = head_refs[c * count : (c + 1) * count]
        _, rows, feats = parts[0].shape
        values = [ref[...].astype(F32).reshape(size * rows, feats) for ref in parts]
        for g in range(count):
            value = values[0]
            for label, other in zip(labels[1:], values[1:]):
                value = jnp.where(lane == g ^ label, other, value)
            joined_ref[: size * rows, g * feats : (g + 1) * feats] = value
        gate = gate_refs[c][...].reshape(size * rows, width)
        gated = (gate * joined_ref[: size * rows]).astype(BF16)
        result = nn_dot(gated, w_ref[...]).astype(BF16)
        result = result.reshape(size, len(out_refs), rows // len(out_refs), width)
        for k, out_ref in enumerate(out_refs):
            out_ref[first : first + size] = result[:, k]
        first += size


def projected(lane, heads, gates, w_out, labels, sg, query_rows):
    sizes = [x[0].shape[0] for x in heads]
    _, rows, _ = heads[0][0].shape
    width = w_out.shape[1]
    vmem = pl.BlockSpec(memory_space=pltpu.VMEM)
    flat = [x for chunk in heads for x in chunk]
    return pl.pallas_call(
        functools.partial(project_kernel, labels, sizes),
        in_specs=[pl.BlockSpec(memory_space=pltpu.SMEM)] + [vmem] * (len(flat) + len(gates) + 1),
        out_specs=[vmem] * sg,
        out_shape=[jax.ShapeDtypeStruct((sum(sizes), query_rows, width), BF16)] * sg,
        scratch_shapes=[pltpu.VMEM((max(sizes) * rows, width), F32)],
        cost_estimate=pl.CostEstimate(
            flops=2 * sum(sizes) * rows * width * width, bytes_accessed=2 * width * width, transcendentals=0
        ),
        compiler_params=pltpu.CompilerParams(vmem_limit_bytes=12 * MIB),
        name="project",
    )(lane.reshape(1), *flat, *gates, w_out)


def assemble_kernel(sg, firsts, group_ref, *refs):
    out_ref = refs[-1]
    group = group_ref[0]
    for i, ref in enumerate(refs[:-1]):
        first, k = firsts[i // sg], i % sg
        out_ref[group ^ k, first : first + ref.shape[0]] = ref[...]


def assembled(group, parts, firsts, shape):
    vmem = pl.BlockSpec(memory_space=pltpu.VMEM)
    return pl.pallas_call(
        functools.partial(assemble_kernel, shape[0], firsts),
        in_specs=[pl.BlockSpec(memory_space=pltpu.SMEM)] + [vmem] * len(parts),
        out_specs=vmem,
        out_shape=jax.ShapeDtypeStruct(shape, BF16),
        compiler_params=pltpu.CompilerParams(vmem_limit_bytes=8 * MIB),
        name="assemble",
    )(group.reshape(1), *parts)


def head_groups(n, samples):
    hg = 1
    while hg * hg < n or H % hg or samples % (n // hg):
        hg *= 2
    return hg


def chunk_sizes(group_samples):
    size = max(group_samples // 3, 1)
    return [group_samples - 2 * size, size, size]


def local(
    query_tokens,
    key_tokens,
    pair,
    key_mask,
    span_owner,
    pair_gain,
    pair_proj,
    w_query,
    w_key,
    w_value,
    w_gate,
    w_out,
):
    n = lax.axis_size("key")
    samples, query_rows, width = query_tokens.shape
    keys = key_tokens.shape[1]
    window = pair.shape[0]
    hg = head_groups(n, samples)
    sg = n // hg
    hpg = H // hg
    feats = width // hg
    group_samples = samples // sg
    sizes = chunk_sizes(group_samples)
    firsts = [sum(sizes[:c]) for c in range(len(sizes))]
    direct = query_rows % 16 == 0
    me = lax.axis_index("key")
    group, lane = me // hg, me % hg

    def across(x, code):
        if code == 0:
            return x
        return lax.ppermute(x, "key", [(i, i ^ code) for i in range(n)])

    labels = [0]
    bit = hg // 2
    while bit:
        labels = labels + [m ^ bit for m in labels]
        bit //= 2
    codes = labels + [k * hg + m for m in labels for k in range(1, sg)]
    code_list = jnp.array(codes, jnp.int32)
    slot_of = [0] * n
    for p, code in enumerate(codes):
        slot_of[code] = p

    key_groups = key_tokens.reshape(sg, group_samples, keys, width)
    query_groups = query_tokens.reshape(sg, group_samples, query_rows, width)

    others = range(1, sg)
    packed = pack(group, key_groups, query_groups, 0, sizes[:1], others, 56 * MIB)
    own_tokens = pack(group, key_groups, query_groups, 0, [group_samples], [0], 8 * MIB)[0]
    packed = packed + pack(group, key_groups, query_groups, firsts[1], sizes[1:], others, 12 * MIB)
    got = [[across(x, k * hg) for k, x in zip(others, sent)] for sent in packed]

    def over_lanes(arrays):
        bit = hg // 2
        while bit:
            arrays = arrays + [across(x, bit) for x in arrays]
            bit //= 2
        return arrays

    own_tokens = over_lanes(list(own_tokens))

    relative = jnp.arange(hg) ^ lane
    proj_t = jnp.take(pair_proj.T.reshape(hg, hpg, -1), relative, axis=0).reshape(H, -1)
    pieces = local_bias(pair, key_mask, pair_gain, proj_t, hpg)
    pieces = [across(x, m) for m, x in enumerate(pieces)]
    parts = {0: stacked(pieces)}
    bit = sg // 2
    while bit:
        parts.update({k ^ bit: across(x, bit * hg) for k, x in parts.items()})
        bit //= 2
    if direct:
        each = query_rows // 16
        qsel = ((code_list ^ me)[:, None] * each + jnp.arange(each)).reshape(window // 16)
    else:
        qsel = jnp.arange(window // 16, dtype=jnp.int32)
    bias, mask = ordered_bias(
        [parts[k] for k in range(sg)], me, span_owner, qsel, hpg, keys, codes, window
    )

    def own(w):
        return lax.dynamic_slice_in_dim(w, lane * feats, feats, 1)

    wq, wk, wv = own(w_query), own(w_key), own(w_value)

    heads, gates = [], []
    groups = [[0, 1], [2]]
    for g, members in enumerate(groups):
        total = sum(sizes[c] for c in members)
        filled = ()
        rows = []
        for c in members:
            size = sizes[c]
            far = [stacked(got[c])]
            far = over_lanes(far)
            queries = None
            if not direct:
                slots = jnp.array(slot_of, jnp.int32)[me ^ jnp.arange(n)]
                mine = [x[None, firsts[c] : firsts[c] + size, keys:] for x in own_tokens]
                queries = jnp.concatenate(mine + [x[:, :, keys:] for x in far], axis=0)
                queries = jnp.swapaxes(jnp.take(queries, slots, axis=0), 0, 1).reshape(size, window, width)
                tokens = jnp.concatenate([mine[0], far[0][:, :, keys:]], axis=0)
                rows.append(jnp.swapaxes(tokens, 0, 1).reshape(size, sg * query_rows, width))
            if g:
                far, _ = lax.optimization_barrier((far, heads[-1][0]))
            offset = firsts[c] - firsts[members[0]]
            filled = projections(
                firsts[c], total, offset, filled, own_tokens, far, queries,
                wq, wk, wv, w_gate, keys, query_rows, window, n * keys,
            )
        q, k, v, gate = filled
        splits = (query_rows, (sg - 1) * query_rows) if direct else None
        results = attention(q, k, v, bias, mask, hpg, splits, hg)
        if not direct:
            blocks = jnp.take(results[0].reshape(total, n, query_rows, feats), code_list ^ me, axis=1)
            results = []
            for i in range(hg):
                start = hg + i * (sg - 1)
                part = jnp.concatenate([blocks[:, i : i + 1], blocks[:, start : start + sg - 1]], axis=1)
                results.append(part.reshape(total, sg * query_rows, feats))
            gate = jax.nn.sigmoid(nn_dot(jnp.concatenate(rows, axis=0), w_gate))
        heads.append([across(r, m) for r, m in zip(results, labels)])
        gates.append(gate)
    outs = []
    for g in range(len(groups)):
        back = projected(lane, heads[g : g + 1], gates[g : g + 1], w_out, labels, sg, query_rows)
        outs.extend(across(x, k * hg) for k, x in enumerate(back))
    out = assembled(group, outs, [0, firsts[2]], (sg, group_samples, query_rows, width))
    return out.reshape(samples, query_rows, width)


def solution(mesh):
    return jax.shard_map(
        local,
        mesh=mesh,
        in_specs=(
            P("rep", "key", None),
            P("rep", "key", None),
            P("rep", "key", None),
            P(("rep", "key")),
            P("rep"),
            P(),
            P(),
            P(),
            P(),
            P(),
            P(),
            P(),
        ),
        out_specs=P("rep", "key", None),
        check_vma=False,
    )
```

```python
import functools
import math

import jax
import jax.numpy as jnp
from jax import lax
from jax.experimental import pallas as pl
from jax.experimental.pallas import tpu as pltpu
from jax.sharding import PartitionSpec as P


H = 16
LOG2E = 1.4426950408889634
NEG = -1e9
MIB = 1024 * 1024
F32 = jnp.float32
BF16 = jnp.bfloat16


def nt_dot(a, b):
    return lax.dot_general(a, b, (((1,), (1,)), ((), ())), preferred_element_type=F32)


def nn_dot(a, b):
    return jnp.dot(a, b, preferred_element_type=F32)


def bias_kernel(hpg, mask_ref, pair_ref, gain_ref, proj_ref, *out_refs):
    fold, rows, keys, c = pair_ref.shape
    heads = proj_ref.shape[0]
    step = pl.program_id(0)
    total_rows = (out_refs[0].shape[0] - 16) // hpg
    x = jnp.swapaxes(pair_ref[...], 0, 1).reshape(rows * fold * keys, c).astype(F32)
    center = x - jnp.mean(x, axis=-1, keepdims=True)
    spread = jnp.mean(center * center, axis=-1, keepdims=True)
    normed = (center * lax.rsqrt(spread + 1e-5) * gain_ref[...]).astype(BF16)
    bias = nt_dot(proj_ref[...], normed)
    bias = bias.reshape(heads, rows, fold * keys).astype(BF16)
    for h in range(heads):
        start = pl.multiple_of((h % hpg) * total_rows + step * rows, 16)
        out_refs[h // hpg][pl.ds(start, rows), :] = bias[h]

    @pl.when(step == 0)
    def _():
        row = jnp.broadcast_to(mask_ref[...], (16, fold * keys)).astype(BF16)
        for out_ref in out_refs:
            out_ref[hpg * total_rows :, :] = row


def local_bias(pair, key_mask, pair_gain, proj_t, hpg):
    window, keys, c = pair.shape
    heads = proj_t.shape[0]
    fold = 128 // keys
    rows = window // fold
    tile = 16
    mask = jnp.tile(key_mask.astype(F32), fold)[None]
    shape = (hpg * rows + 16, 128)
    return pl.pallas_call(
        functools.partial(bias_kernel, hpg),
        grid=(rows // tile,),
        in_specs=[
            pl.BlockSpec((1, 128), lambda i: (0, 0)),
            pl.BlockSpec((fold, tile, keys, c), lambda i: (0, i, 0, 0)),
            pl.BlockSpec((1, c), lambda i: (0, 0)),
            pl.BlockSpec((heads, c), lambda i: (0, 0)),
        ],
        out_specs=[pl.BlockSpec(shape, lambda i: (0, 0))] * (heads // hpg),
        out_shape=[jax.ShapeDtypeStruct(shape, BF16)] * (heads // hpg),
        cost_estimate=pl.CostEstimate(
            flops=2 * window * keys * c * 256, bytes_accessed=window * keys * c * 2, transcendentals=0
        ),
        compiler_params=pltpu.CompilerParams(vmem_limit_bytes=16 * MIB),
        name="bias_local",
    )(mask, pair.reshape(fold, rows, keys, c), pair_gain[None], proj_t)


def pack_kernel(sizes, count, group_ref, *refs):
    step = pl.program_id(0)
    start = 0
    for i, size in enumerate(sizes):

        @pl.when((step >= start) & (step < start + size))
        def _(i=i):
            for k in range(count):
                out_ref = refs[(2 + i) * count + k]
                keys = refs[k].shape[2]
                out_ref[0, :keys] = refs[k][0, 0]
                out_ref[0, keys:] = refs[count + k][0, 0]

        start += size


def pack(group, key_groups, query_groups, first, sizes, steps, limit):
    _, _, keys, width = key_groups.shape
    rows = query_groups.shape[2]
    total = sum(sizes)
    count = len(steps)

    def spec(length, k):
        return pl.BlockSpec((1, 1, length, width), lambda s, g: (g[0] ^ k, first + s, 0, 0))

    def out_spec(i):
        start = sum(sizes[:i])
        return pl.BlockSpec(
            (1, keys + rows, width), lambda s, g: (jnp.clip(s - start, 0, sizes[i] - 1), 0, 0)
        )

    outs = pl.pallas_call(
        functools.partial(pack_kernel, sizes, count),
        grid_spec=pltpu.PrefetchScalarGridSpec(
            num_scalar_prefetch=1,
            grid=(total,),
            in_specs=[spec(keys, k) for k in steps] + [spec(rows, k) for k in steps],
            out_specs=[out_spec(i) for i in range(len(sizes)) for _ in steps],
        ),
        out_shape=[jax.ShapeDtypeStruct((size, keys + rows, width), BF16) for size in sizes for _ in steps],
        cost_estimate=pl.CostEstimate(
            flops=0, bytes_accessed=4 * count * total * (keys + rows) * width, transcendentals=0
        ),
        compiler_params=pltpu.CompilerParams(vmem_limit_bytes=limit),
        name="pack",
    )(group.reshape(1), *([key_groups] * count), *([query_groups] * count))
    return [outs[i * count : (i + 1) * count] for i in range(len(sizes))]


def stack_kernel(*refs):
    for i, ref in enumerate(refs[:-1]):
        refs[-1][i] = ref[...]


def stacked(parts):
    count, shape = len(parts), parts[0].shape
    rest = (0,) * (len(shape) - 1)
    block = (1,) + shape[1:] if len(shape) == 3 else shape
    steps = shape[0] if len(shape) == 3 else 1
    return pl.pallas_call(
        stack_kernel,
        grid=(steps,),
        in_specs=[pl.BlockSpec(block, lambda s: (s,) + rest)] * count,
        out_specs=pl.BlockSpec((count,) + block, lambda s: (0, s) + rest),
        out_shape=jax.ShapeDtypeStruct((count,) + shape, BF16),
        cost_estimate=pl.CostEstimate(
            flops=0, bytes_accessed=4 * count * math.prod(shape), transcendentals=0
        ),
        compiler_params=pltpu.CompilerParams(vmem_limit_bytes=8 * MIB),
        name="stack",
    )(*parts)


def order_kernel(hpg, keys, codes, me_ref, owner_ref, qsel_ref, *refs):
    parts, (bias_ref, mask_ref, inv_ref, x_ref) = refs[:-4], refs[-4:]
    n = len(codes)
    each = n // len(parts)
    for k, part_ref in enumerate(parts):
        x_ref[k * each : (k + 1) * each] = part_ref[...]
    fold = 128 // keys
    me = me_ref[0]
    rows = (x_ref.shape[1] - 16) // hpg
    slots = bias_ref.shape[1] // 16
    for d in range(n):
        inv_ref[owner_ref[d]] = d
    lane = lax.broadcasted_iota(jnp.int32, (16, 128), 1) // keys

    def of_tile(t):
        stored = [inv_ref[me ^ codes[t * fold + f]] ^ me for f in range(fold)]
        masks = x_ref[codes[t * fold], hpg * rows : hpg * rows + 16, :].astype(F32)
        for f in range(1, fold):
            part = x_ref[codes[t * fold + f], hpg * rows : hpg * rows + 16, :].astype(F32)
            masks = jnp.where(lane == f, part, masks)
        mask_ref[:, t * 128 : (t + 1) * 128] = masks[:8]
        return stored, masks > 0

    tiles = [of_tile(t) for t in range(n // fold)]

    def query_slot(p, carry):
        a = qsel_ref[p]
        part = a // (rows // 16)
        row = a % (rows // 16) * 16
        out = pl.multiple_of(p * 16, 16)
        for h in range(hpg):
            start = pl.multiple_of(h * rows + row, 16)
            for t, (stored, present) in enumerate(tiles):
                value = None
                for f in range(fold):
                    block = x_ref[stored[f], pl.ds(start, 16), :].astype(F32)
                    if fold == 2:
                        block = jnp.where(part == f, block, pltpu.roll(block, keys, 1))
                    value = block if value is None else jnp.where(lane == f, block, value)
                value = jnp.where(present, value * LOG2E, NEG * LOG2E)
                bias_ref[h, pl.ds(out, 16), t * 128 : (t + 1) * 128] = value
        return carry

    lax.fori_loop(0, slots, query_slot, 0)


def ordered_bias(parts, me, span_owner, qsel, hpg, keys, codes, window):
    n = len(codes)
    limit = (40 if n * keys > 2048 else 14) * MIB
    smem = pl.BlockSpec(memory_space=pltpu.SMEM)
    vmem = pl.BlockSpec(memory_space=pltpu.VMEM)
    return pl.pallas_call(
        functools.partial(order_kernel, hpg, keys, codes),
        in_specs=[smem, smem, smem] + [vmem] * len(parts),
        out_specs=[vmem, vmem],
        out_shape=[
            jax.ShapeDtypeStruct((hpg, window, n * keys), F32),
            jax.ShapeDtypeStruct((8, n * keys), F32),
        ],
        scratch_shapes=[
            pltpu.SMEM((n,), jnp.int32),
            pltpu.VMEM((n,) + parts[0].shape[1:], BF16),
        ],
        cost_estimate=pl.CostEstimate(
            flops=hpg * window * n * keys * 8, bytes_accessed=hpg * window * n * keys * 6, transcendentals=0
        ),
        compiler_params=pltpu.CompilerParams(vmem_limit_bytes=limit),
        name="bias_order",
    )(me.reshape(1), span_owner, qsel, *parts)


def heads_kernel(pieces, direct, keys, *refs):
    own_refs, far_refs, refs = refs[:pieces], refs[pieces : 2 * pieces], refs[2 * pieces :]
    if not direct:
        query_ref, refs = refs[0], refs[1:]
    wq_ref, wk_ref, wv_ref, wg_ref = refs[:4]
    q_ref, k_ref, v_ref, gate_ref = refs[-4:]
    total_rows, width = own_refs[0].shape[1:]

    def own_rows(start, stop):
        return jnp.concatenate([ref[0, start:stop] for ref in own_refs], axis=0)

    def far_rows(ref, start, stop):
        block = ref[:, 0, start:stop]
        return block.reshape(block.shape[0] * block.shape[1], width)

    at = 0
    for m in range(-1, pieces):
        block = own_rows(0, keys) if m < 0 else far_rows(far_refs[m], 0, keys)
        span = slice(at, at + block.shape[0])
        k_ref[0, :, span] = nn_dot(block, wk_ref[...]).T.astype(BF16)
        v_ref[0, span, :] = nn_dot(block, wv_ref[...]).astype(BF16)
        at += block.shape[0]
    if direct:
        at = 0
        for m in range(-1, pieces):
            block = own_rows(keys, total_rows) if m < 0 else far_rows(far_refs[m], keys, total_rows)
            q_ref[0, at : at + block.shape[0], :] = nn_dot(block, wq_ref[...]).astype(BF16)
            at += block.shape[0]
        block = jnp.concatenate([own_refs[0][0, keys:], far_rows(far_refs[0], keys, total_rows)], axis=0)
        gate_ref[0] = jax.nn.sigmoid(nn_dot(block, wg_ref[...]))
    else:
        q_ref[0] = nn_dot(query_ref[0], wq_ref[...]).astype(BF16)
        gate_ref[...] = jnp.zeros_like(gate_ref)


def projections(first, total, offset, filled, own, far, queries, wq, wk, wv, w_gate, keys, query_rows, window, tokens):
    pieces = len(far)
    others, size, rows, width = far[0].shape
    feats = wq.shape[1]
    direct = queries is None
    whole = pl.BlockSpec(memory_space=pltpu.VMEM)
    specs = [pl.BlockSpec((1, rows, width), lambda s: (first + s, 0, 0))] * pieces
    specs += [pl.BlockSpec((others, 1, rows, width), lambda s: (0, s, 0, 0))] * pieces
    args = list(own) + list(far)
    gate_rows = (others + 1) * query_rows
    if not direct:
        specs.append(pl.BlockSpec((1, window, width), lambda s: (s, 0, 0)))
        args.append(queries)
    consts = [wq, wk, wv, w_gate]
    shapes = [(window, feats), (feats, tokens), (tokens, feats), (gate_rows, width)]
    before = len(args) + len(consts)
    return pl.pallas_call(
        functools.partial(heads_kernel, pieces, direct, keys),
        grid=(size,),
        in_specs=specs + [whole] * len(consts) + [pl.BlockSpec(memory_space=pl.ANY)] * len(filled),
        out_specs=[pl.BlockSpec((1,) + x, lambda s: (offset + s, 0, 0)) for x in shapes],
        out_shape=[
            jax.ShapeDtypeStruct((total,) + x, F32 if i == 3 else BF16) for i, x in enumerate(shapes)
        ],
        input_output_aliases={before + i: i for i in range(len(filled))},
        cost_estimate=pl.CostEstimate(
            flops=4 * size * tokens * width * feats, bytes_accessed=size * tokens * width * 3, transcendentals=0
        ),
        compiler_params=pltpu.CompilerParams(vmem_limit_bytes=(48 if tokens > 2048 else 16) * MIB),
        name="heads",
    )(*args, *consts, *filled)


def attention_kernel(hpg, splits, q_ref, k_ref, v_ref, bias_ref, mask_ref, *out_refs):
    q = q_ref[0]
    k = k_ref[0] * mask_ref[:1].astype(BF16)
    head_size = q.shape[1] // hpg
    scale = LOG2E / math.sqrt(head_size)
    tile = min(128, q.shape[0])
    parts = []
    for r in range(0, q.shape[0], tile):
        rows = q[r : r + tile]
        owner = lax.broadcasted_iota(jnp.int32, rows.shape, 1) // head_size
        part = None
        for h in range(hpg):
            mine = owner == h
            scores = nn_dot(jnp.where(mine, rows, jnp.zeros_like(rows)), k)
            scores = scores * scale + bias_ref[h, r : r + tile]
            weights = jnp.exp2(scores - jnp.max(scores, axis=-1, keepdims=True))
            norm = 1.0 / jnp.sum(weights, axis=-1, keepdims=True)
            result = nn_dot(weights.astype(BF16), v_ref[0]) * norm
            part = result if part is None else jnp.where(mine, result, part)
        parts.append(part)
    total = jnp.concatenate(parts, axis=0)
    total = total.astype(BF16)
    if splits is None:
        out_refs[0][0] = total
        return
    own, far = splits
    pieces = len(out_refs)
    for m, out_ref in enumerate(out_refs):
        out_ref[0, :own] = total[m * own : (m + 1) * own]
        out_ref[0, own:] = total[pieces * own + m * far : pieces * own + (m + 1) * far]


def attention(q, k, v, bias, mask, hpg, splits, pieces):
    size, window, feats = q.shape
    tokens = k.shape[2]
    out_rows = [window] if splits is None else [sum(splits)] * pieces
    return pl.pallas_call(
        functools.partial(attention_kernel, hpg, splits),
        grid=(size,),
        in_specs=[pl.BlockSpec((1,) + x.shape[1:], lambda s: (s, 0, 0)) for x in (q, k, v)]
        + [pl.BlockSpec(memory_space=pltpu.VMEM)] * 2,
        out_specs=[pl.BlockSpec((1, r, feats), lambda s: (s, 0, 0)) for r in out_rows],
        out_shape=[jax.ShapeDtypeStruct((size, r, feats), BF16) for r in out_rows],
        cost_estimate=pl.CostEstimate(
            flops=2 * size * hpg * window * tokens * 512,
            bytes_accessed=size * tokens * feats * 4 + hpg * window * tokens * 4,
            transcendentals=size * hpg * window * tokens,
        ),
        compiler_params=pltpu.CompilerParams(vmem_limit_bytes=(58 if tokens > 2048 else 20) * MIB),
        name="attend",
    )(q, k, v, bias, mask)


def project_kernel(labels, sizes, lane_ref, *refs):
    count = len(labels)
    chunks = len(sizes)
    head_refs, refs = refs[: count * chunks], refs[count * chunks :]
    gate_refs, w_ref, refs = refs[:chunks], refs[chunks], refs[chunks + 1 :]
    out_refs, joined_ref = refs[:-1], refs[-1]
    lane = lane_ref[0]
    width = w_ref.shape[1]
    first = 0
    for c, size in enumerate(sizes):
        parts = head_refs[c * count : (c + 1) * count]
        _, rows, feats = parts[0].shape
        values = [ref[...].astype(F32).reshape(size * rows, feats) for ref in parts]
        for g in range(count):
            value = values[0]
            for label, other in zip(labels[1:], values[1:]):
                value = jnp.where(lane == g ^ label, other, value)
            joined_ref[: size * rows, g * feats : (g + 1) * feats] = value
        gate = gate_refs[c][...].reshape(size * rows, width)
        gated = (gate * joined_ref[: size * rows]).astype(BF16)
        result = nn_dot(gated, w_ref[...]).astype(BF16)
        result = result.reshape(size, len(out_refs), rows // len(out_refs), width)
        for k, out_ref in enumerate(out_refs):
            out_ref[first : first + size] = result[:, k]
        first += size


def projected(lane, heads, gates, w_out, labels, sg, query_rows):
    sizes = [x[0].shape[0] for x in heads]
    _, rows, _ = heads[0][0].shape
    width = w_out.shape[1]
    vmem = pl.BlockSpec(memory_space=pltpu.VMEM)
    flat = [x for chunk in heads for x in chunk]
    return pl.pallas_call(
        functools.partial(project_kernel, labels, sizes),
        in_specs=[pl.BlockSpec(memory_space=pltpu.SMEM)] + [vmem] * (len(flat) + len(gates) + 1),
        out_specs=[vmem] * sg,
        out_shape=[jax.ShapeDtypeStruct((sum(sizes), query_rows, width), BF16)] * sg,
        scratch_shapes=[pltpu.VMEM((max(sizes) * rows, width), F32)],
        cost_estimate=pl.CostEstimate(
            flops=2 * sum(sizes) * rows * width * width, bytes_accessed=2 * width * width, transcendentals=0
        ),
        compiler_params=pltpu.CompilerParams(vmem_limit_bytes=12 * MIB),
        name="project",
    )(lane.reshape(1), *flat, *gates, w_out)


def assemble_kernel(sg, firsts, group_ref, *refs):
    out_ref = refs[-1]
    group = group_ref[0]
    for i, ref in enumerate(refs[:-1]):
        first, k = firsts[i // sg], i % sg
        out_ref[group ^ k, first : first + ref.shape[0]] = ref[...]


def assembled(group, parts, firsts, shape):
    vmem = pl.BlockSpec(memory_space=pltpu.VMEM)
    return pl.pallas_call(
        functools.partial(assemble_kernel, shape[0], firsts),
        in_specs=[pl.BlockSpec(memory_space=pltpu.SMEM)] + [vmem] * len(parts),
        out_specs=vmem,
        out_shape=jax.ShapeDtypeStruct(shape, BF16),
        compiler_params=pltpu.CompilerParams(vmem_limit_bytes=8 * MIB),
        name="assemble",
    )(group.reshape(1), *parts)


def head_groups(n, samples):
    hg = 1
    while hg * hg < n or H % hg or samples % (n // hg):
        hg *= 2
    return hg


def chunk_sizes(group_samples):
    size = max(group_samples // 3, 1)
    return [group_samples - 2 * size, size, size]


def local(
    query_tokens,
    key_tokens,
    pair,
    key_mask,
    span_owner,
    pair_gain,
    pair_proj,
    w_query,
    w_key,
    w_value,
    w_gate,
    w_out,
):
    n = lax.axis_size("key")
    samples, query_rows, width = query_tokens.shape
    keys = key_tokens.shape[1]
    window = pair.shape[0]
    hg = head_groups(n, samples)
    sg = n // hg
    hpg = H // hg
    feats = width // hg
    group_samples = samples // sg
    sizes = chunk_sizes(group_samples)
    firsts = [sum(sizes[:c]) for c in range(len(sizes))]
    direct = query_rows % 16 == 0
    me = lax.axis_index("key")
    group, lane = me // hg, me % hg

    def across(x, code):
        if code == 0:
            return x
        return lax.ppermute(x, "key", [(i, i ^ code) for i in range(n)])

    labels = [0]
    bit = hg // 2
    while bit:
        labels = labels + [m ^ bit for m in labels]
        bit //= 2
    codes = labels + [k * hg + m for m in labels for k in range(1, sg)]
    code_list = jnp.array(codes, jnp.int32)
    slot_of = [0] * n
    for p, code in enumerate(codes):
        slot_of[code] = p

    key_groups = key_tokens.reshape(sg, group_samples, keys, width)
    query_groups = query_tokens.reshape(sg, group_samples, query_rows, width)

    others = range(1, sg)
    packed = pack(group, key_groups, query_groups, 0, sizes[:1], others, 56 * MIB)
    own_tokens = pack(group, key_groups, query_groups, 0, [group_samples], [0], 8 * MIB)[0]
    packed = packed + pack(group, key_groups, query_groups, firsts[1], sizes[1:], others, 12 * MIB)
    got = [[across(x, k * hg) for k, x in zip(others, sent)] for sent in packed]

    def over_lanes(arrays):
        bit = hg // 2
        while bit:
            arrays = arrays + [across(x, bit) for x in arrays]
            bit //= 2
        return arrays

    own_tokens = over_lanes(list(own_tokens))

    relative = jnp.arange(hg) ^ lane
    proj_t = jnp.take(pair_proj.T.reshape(hg, hpg, -1), relative, axis=0).reshape(H, -1)
    pieces = local_bias(pair, key_mask, pair_gain, proj_t, hpg)
    pieces = [across(x, m) for m, x in enumerate(pieces)]
    parts = {0: stacked(pieces)}
    bit = sg // 2
    while bit:
        parts.update({k ^ bit: across(x, bit * hg) for k, x in parts.items()})
        bit //= 2
    if direct:
        each = query_rows // 16
        qsel = ((code_list ^ me)[:, None] * each + jnp.arange(each)).reshape(window // 16)
    else:
        qsel = jnp.arange(window // 16, dtype=jnp.int32)
    bias, mask = ordered_bias(
        [parts[k] for k in range(sg)], me, span_owner, qsel, hpg, keys, codes, window
    )

    def own(w):
        return lax.dynamic_slice_in_dim(w, lane * feats, feats, 1)

    wq, wk, wv = own(w_query), own(w_key), own(w_value)

    heads, gates = [], []
    groups = [[0, 1], [2]]
    for g, members in enumerate(groups):
        total = sum(sizes[c] for c in members)
        filled = ()
        rows = []
        for c in members:
            size = sizes[c]
            far = [stacked(got[c])]
            far = over_lanes(far)
            queries = None
            if not direct:
                slots = jnp.array(slot_of, jnp.int32)[me ^ jnp.arange(n)]
                mine = [x[None, firsts[c] : firsts[c] + size, keys:] for x in own_tokens]
                queries = jnp.concatenate(mine + [x[:, :, keys:] for x in far], axis=0)
                queries = jnp.swapaxes(jnp.take(queries, slots, axis=0), 0, 1).reshape(size, window, width)
                tokens = jnp.concatenate([mine[0], far[0][:, :, keys:]], axis=0)
                rows.append(jnp.swapaxes(tokens, 0, 1).reshape(size, sg * query_rows, width))
            if g:
                far, _ = lax.optimization_barrier((far, heads[-1][0]))
            offset = firsts[c] - firsts[members[0]]
            filled = projections(
                firsts[c], total, offset, filled, own_tokens, far, queries,
                wq, wk, wv, w_gate, keys, query_rows, window, n * keys,
            )
        q, k, v, gate = filled
        splits = (query_rows, (sg - 1) * query_rows) if direct else None
        results = attention(q, k, v, bias, mask, hpg, splits, hg)
        if not direct:
            blocks = jnp.take(results[0].reshape(total, n, query_rows, feats), code_list ^ me, axis=1)
            results = []
            for i in range(hg):
                start = hg + i * (sg - 1)
                part = jnp.concatenate([blocks[:, i : i + 1], blocks[:, start : start + sg - 1]], axis=1)
                results.append(part.reshape(total, sg * query_rows, feats))
            gate = jax.nn.sigmoid(nn_dot(jnp.concatenate(rows, axis=0), w_gate))
        heads.append([across(r, m) for r, m in zip(results, labels)])
        gates.append(gate)
    outs = []
    for g in range(len(groups)):
        back = projected(lane, heads[g : g + 1], gates[g : g + 1], w_out, labels, sg, query_rows)
        outs.extend(across(x, k * hg) for k, x in enumerate(back))
    out = assembled(group, outs, [0, firsts[2]], (sg, group_samples, query_rows, width))
    return out.reshape(samples, query_rows, width)


def solution(mesh):
    return jax.shard_map(
        local,
        mesh=mesh,
        in_specs=(
            P("rep", "key", None),
            P("rep", "key", None),
            P("rep", "key", None),
            P(("rep", "key")),
            P("rep"),
            P(),
            P(),
            P(),
            P(),
            P(),
            P(),
            P(),
        ),
        out_specs=P("rep", "key", None),
        check_vma=False,
    )
```
